32 devices in a mesh: seq: 8 (over z, x), head: 4 (over y, core).
Axes of the slice: x: 2, y: 2, z: 4, core: 2. Of those that a mesh axis runs over, the one named last changes fastest.
Arguments:
- hidden_in: bfloat16 [8192, 768], P('seq'), may hold values from -6 to 6
- q_weight: bfloat16 [768, 768], P(None, 'head'), may hold values from -0.3125 to 0.3125
- q_bias: float32 [768], P('head'), may hold values from -3 to 3
- k_weight: bfloat16 [768, 768], P(None, 'head'), may hold values from -0.21875 to 0.21875
- v_weight: bfloat16 [768, 768], P(None, 'head'), may hold values from -0.21875 to 0.21875
- v_bias: float32 [768], P('head'), may hold values from -3 to 3
- o_weight: bfloat16 [768, 768], P('head'), may hold values from -0.875 to 0.875
- o_bias: float32 [768], replicated, may hold values from -3 to 3
- norm1_gain: float32 [768], replicated, may hold values from 0.5 to 1.5
- norm1_shift: float32 [768], replicated, may hold values from -3 to 3
- up_weight: bfloat16 [768, 3072], P(None, 'head'), may hold values from -0.21875 to 0.21875
- up_bias: float32 [3072], P('head'), may hold values from -3 to 3
- down_weight: bfloat16 [3072, 768], P('head'), may hold values from -0.109375 to 0.109375
- down_bias: float32 [768], replicated, may hold values from -3 to 3
- norm2_gain: float32 [768], replicated, may hold values from 0.5 to 1.5
- norm2_shift: float32 [768], replicated, may hold values from -3 to 3
- doc_mask: int32 [8192], replicated, may hold values from 0 to 1, as said below
- doc_blocks: int32 [2], replicated, may hold values from 8 to 64, as said below
- rand_blocks: int32 [128, 3], P('seq'), may hold values from 2 to 63, as said below
- out_grad: float32 [8192, 768], P(('seq', 'head')), may hold values from -6 to 6
Outputs:
- layer_out: float32 [8192, 768], P(('seq', 'head'))
- in_grad: float32 [8192, 768], P(('seq', 'head'))
- q_weight_grad: float32 [768, 768], P(None, 'head')
- q_bias_grad: float32 [768], P('head')
- k_weight_grad: float32 [768, 768], P(None, 'head')
- v_weight_grad: float32 [768, 768], P(None, 'head')
- v_bias_grad: float32 [768], P('head')
- o_weight_grad: float32 [768, 768], P('head')
- o_bias_grad: float32 [768], replicated
- norm1_gain_grad: float32 [768], replicated
- norm1_shift_grad: float32 [768], replicated
- up_weight_grad: float32 [768, 3072], P(None, 'head')
- up_bias_grad: float32 [3072], P('head')
- down_weight_grad: float32 [3072, 768], P('head')
- down_bias_grad: float32 [768], replicated
- norm2_gain_grad: float32 [768], replicated
- norm2_shift_grad: float32 [768], replicated
The draws below stay inside these ranges and needn't reach their ends.
Inputs may be any that keep to these rules, and one draw needn't show every extreme that they name: `doc_blocks`: some slot has 64 blocks and some slot 8. `doc_mask`: in each slot the ones are exactly its first positions; their number exceeds 64 times (the slot's doc_blocks - 1) and is at most 64 times its doc_blocks. `rand_blocks`: A row holds three different block indices of its block's slot, each below that slot's doc_blocks and more than one away from the row's own block index within the slot.
All inputs are finite; a program needn't handle non-finite values.
Results may differ from the reference program's by a relative error of at most 0.019.
Values may be sent and summed in bfloat16 or wider, within the bound.
A program may use at most 256 MiB of HBM per device.

```python
import jax
import jax.numpy as jnp
from jax import lax

D = 768
HEADS = 12
HD = 64
FF = 3072
BLOCK = 64
SLOT_LEN = 4096
DOC_MIN_BLOCKS = 8
TOKENS = 8192
SLOTS = 2
SLOT_BLOCKS = 64
BLOCKS = 128


def layout_draw(key):
    base = jax.random.fold_in(key, 90211)
    keys_list = jax.random.split(base, 5)
    counts = jax.random.randint(keys_list[0], (SLOTS,), DOC_MIN_BLOCKS, SLOT_BLOCKS + 1)
    full_slot = jax.random.randint(keys_list[1], (), 0, SLOTS)
    short_slot = (full_slot + 1 + jax.random.randint(keys_list[2], (), 0, SLOTS - 1)) % SLOTS
    slot_ids = jnp.arange(SLOTS)
    counts = jnp.where(slot_ids == full_slot, SLOT_BLOCKS, jnp.where(slot_ids == short_slot, DOC_MIN_BLOCKS, counts)).astype(jnp.int32)
    tails = jax.random.randint(keys_list[3], (SLOTS,), 1, BLOCK + 1)
    lengths = (counts - 1) * BLOCK + tails
    return (counts, lengths, full_slot, short_slot, keys_list[4])


def draw_doc_blocks(key, part):
    counts, lengths, full_slot, short_slot, rand_key = layout_draw(key)
    return counts.astype(jnp.int32)


def draw_doc_mask(key, part):
    counts, lengths, full_slot, short_slot, rand_key = layout_draw(key)
    positions = jnp.arange(SLOT_LEN)
    return (positions[None, :] < lengths[:, None]).astype(jnp.int32).reshape(TOKENS)


def draw_rand_blocks(key, part):
    counts, lengths, full_slot, short_slot, rand_key = layout_draw(key)
    candidates = jnp.arange(SLOT_BLOCKS, dtype=jnp.int32)[None, None, :]
    row_blocks = jnp.arange(SLOT_BLOCKS, dtype=jnp.int32)[None, :, None]
    slot_ids = jnp.arange(SLOTS, dtype=jnp.int32)[:, None, None]
    scores = jax.random.randint(rand_key, (SLOTS, SLOT_BLOCKS, SLOT_BLOCKS), 0, 65536) * SLOT_BLOCKS + candidates
    allowed = (candidates >= 2) & (candidates < counts[:, None, None]) & (jnp.abs(candidates - row_blocks) > 1)
    forced_high = (slot_ids == full_slot) & (row_blocks == 2) & (candidates == SLOT_BLOCKS - 1)
    forced_low = (slot_ids == short_slot) & (row_blocks == SLOT_BLOCKS - 1) & (candidates == 2)
    scores = jnp.where(allowed, scores + jnp.where(forced_high | forced_low, 1 << 24, 0), -1)
    picked = lax.top_k(scores, 3)[1]
    return picked.astype(jnp.int32).reshape(BLOCKS, 3)


def block_scale(key, extent, pieces, smallest, high):
    gain, own = 1.0, jax.random.fold_in(key, 6)
    for axis_at, shards_of in pieces:
        heights = jnp.exp(jax.random.uniform(jax.random.fold_in(own, axis_at), (shards_of,), jnp.float32, smallest / len(pieces), high / len(pieces)))
        gain = gain * jnp.repeat(heights, extent[axis_at] // shards_of).reshape([-1 if axis == axis_at else 1 for axis in range(len(extent))])
    return gain


def scatter_about(rng, shape, scale, most, shards=(), kind=jnp.bfloat16):
    level = block_scale(rng, shape, shards, -0.22, 0.18) if shards else 1.0
    result = jax.random.normal(rng, shape, jnp.float32) * scale * level
    return jnp.minimum(jnp.maximum(result, -most), most).astype(kind)


def setup_inputs(seed: int = 0) -> dict:
    splits = jax.random.split(jax.random.key(seed), 21)
    return {
        "hidden_in": scatter_about(splits[0], (TOKENS, D), 1.0, 6.0, ((0, 8),)),
        "q_weight": scatter_about(splits[1], (D, D), (D // 2) ** -0.5, 0.3125, ((1, 4),)),
        "q_bias": scatter_about(splits[2], (D,), 0.5, 3.0, ((0, 4),), jnp.float32),
        "k_weight": scatter_about(splits[3], (D, D), D ** -0.5, 0.21875, ((1, 4),)),
        "v_weight": scatter_about(splits[4], (D, D), D ** -0.5, 0.21875, ((1, 4),)),
        "v_bias": scatter_about(splits[5], (D,), 0.5, 3.0, ((0, 4),), jnp.float32),
        "o_weight": scatter_about(splits[6], (D, D), (D // 16) ** -0.5, 0.875, ((0, 4),)),
        "o_bias": scatter_about(splits[7], (D,), 0.5, 3.0, (), jnp.float32),
        "norm1_gain": jnp.clip(1.0 + 0.1 * jax.random.normal(splits[8], (D,), jnp.float32), 0.5, 1.5),
        "norm1_shift": scatter_about(splits[9], (D,), 0.5, 3.0, (), jnp.float32),
        "up_weight": scatter_about(splits[10], (D, FF), D ** -0.5, 0.21875, ((1, 4),)),
        "up_bias": scatter_about(splits[11], (FF,), 0.5, 3.0, ((0, 4),), jnp.float32),
        "down_weight": scatter_about(splits[12], (FF, D), FF ** -0.5, 0.109375, ((0, 4),)),
        "down_bias": scatter_about(splits[13], (D,), 0.5, 3.0, (), jnp.float32),
        "norm2_gain": jnp.clip(1.0 + 0.1 * jax.random.normal(splits[14], (D,), jnp.float32), 0.5, 1.5),
        "norm2_shift": scatter_about(splits[15], (D,), 0.5, 3.0, (), jnp.float32),
        "doc_mask": draw_doc_mask(jax.random.fold_in(splits[20], 71), 0),
        "doc_blocks": draw_doc_blocks(jax.random.fold_in(splits[20], 71), 0),
        "rand_blocks": draw_rand_blocks(jax.random.fold_in(splits[20], 71), 0),
        "out_grad": scatter_about(splits[19], (TOKENS, D), 1.0, 6.0, ((0, 32),), jnp.float32),
    }


NEG = -1e+30
EPS = 1e-12

@jax.custom_vjp
def low(v):
    return lax.optimization_barrier(v.astype(jnp.bfloat16)).astype(jnp.float32)

@jax.custom_vjp
def low_back(v):
    return v

def low_keep(v):
    return (low(v), None)

def low_pass(kept, grad):
    return (grad,)

def back_keep(v):
    return (v, None)

def back_low(kept, grad):
    return (low(grad),)
low.defvjp(low_keep, low_pass)
low_back.defvjp(back_keep, back_low)

def layer_norm(values_in, gain_vec, shift_vec):
    row_mean = lax.optimization_barrier(jnp.mean(values_in, axis=-1, keepdims=True))
    centred = values_in - row_mean
    variance = lax.optimization_barrier(jnp.mean(centred * centred, axis=-1, keepdims=True))
    return centred * lax.rsqrt(variance + EPS) * gain_vec + shift_vec

def attend_slot(query, keys, values, valid, rand_rows):
    highest = lax.Precision.HIGHEST
    scale = HD ** (-0.5)
    block_index = jnp.arange(SLOT_BLOCKS, dtype=jnp.int32)
    near = block_index[:, None] + jnp.arange(-1, 2, dtype=jnp.int32)[None, :]
    near_valid = (near >= 2) & (near < SLOT_BLOCKS)
    near_clip = jnp.clip(near, 0, SLOT_BLOCKS - 1)
    global_ids = jnp.zeros((SLOT_BLOCKS, 2), jnp.int32) + jnp.arange(2, dtype=jnp.int32)[None, :]
    block_ids = jnp.concatenate([near_clip, rand_rows, global_ids], axis=1)
    block_valid = jnp.concatenate([near_valid, jnp.ones((SLOT_BLOCKS, 5), dtype=bool)], axis=1)
    token_valid = valid.reshape(SLOT_BLOCKS, BLOCK)[block_ids] & block_valid[:, :, None]
    token_valid = token_valid.reshape(SLOT_BLOCKS, 8 * BLOCK)
    key_blocks = keys.reshape(SLOT_BLOCKS, BLOCK, HEADS, HD)[block_ids].reshape(SLOT_BLOCKS, 8 * BLOCK, HEADS, HD)
    value_blocks = values.reshape(SLOT_BLOCKS, BLOCK, HEADS, HD)[block_ids].reshape(SLOT_BLOCKS, 8 * BLOCK, HEADS, HD)
    query_blocks = query.reshape(SLOT_BLOCKS, BLOCK, HEADS, HD)
    raw = low_back(jnp.einsum('nqhd,nkhd->nhqk', query_blocks, key_blocks, precision=highest) * scale)
    probs = low(jax.nn.softmax(jnp.where(token_valid[:, None, None, :], raw, NEG), axis=-1))
    sparse_ctx = jnp.einsum('nhqk,nkhd->nqhd', probs, value_blocks, precision=highest).reshape(SLOT_LEN, D)
    head_rows = 2 * BLOCK
    head_query = query[:head_rows].reshape(head_rows, HEADS, HD)
    global_raw = low_back(jnp.einsum('qhd,khd->hqk', head_query, keys.reshape(SLOT_LEN, HEADS, HD), precision=highest) * scale)
    global_probs = low(jax.nn.softmax(jnp.where(valid[None, None, :], global_raw, NEG), axis=-1))
    global_ctx = jnp.einsum('hqk,khd->qhd', global_probs, values.reshape(SLOT_LEN, HEADS, HD), precision=highest).reshape(head_rows, D)
    return jnp.concatenate([global_ctx, sparse_ctx[head_rows:]], axis=0)

def slot_layer(params, slot_tokens, slot_mask, slot_count, rand_rows):
    q_weight, q_bias, k_weight, v_weight, v_bias, o_weight, o_bias, norm1_gain, norm1_shift, up_weight, up_bias, down_weight, down_bias, norm2_gain, norm2_shift = params
    highest = lax.Precision.HIGHEST
    query = low(low_back(jnp.dot(slot_tokens, q_weight, precision=highest) + q_bias))
    keys = low(low_back(jnp.dot(slot_tokens, k_weight, precision=highest)))
    values = low(low_back(jnp.dot(slot_tokens, v_weight, precision=highest) + v_bias))
    positions = jnp.arange(SLOT_LEN, dtype=jnp.int32)
    valid = (slot_mask == 1) & (positions // BLOCK < slot_count)
    context = low(low_back(attend_slot(query, keys, values, valid, rand_rows)))
    attn_out = low_back(jnp.dot(context, o_weight, precision=highest))
    normed_one = layer_norm(slot_tokens + attn_out + o_bias, norm1_gain, norm1_shift)
    pre_act = low_back(jnp.dot(low(normed_one), up_weight, precision=highest) + up_bias)
    ffn_out = low_back(jnp.dot(low(jax.nn.gelu(pre_act, approximate=True)), down_weight, precision=highest))
    return layer_norm(normed_one + ffn_out + down_bias, norm2_gain, norm2_shift)

def reference(hidden_in, q_weight, q_bias, k_weight, v_weight, v_bias, o_weight, o_bias, norm1_gain, norm1_shift, up_weight, up_bias, down_weight, down_bias, norm2_gain, norm2_shift, doc_mask, doc_blocks, rand_blocks, out_grad):
    params = tuple((weight.astype(jnp.float32) for weight in (q_weight, q_bias, k_weight, v_weight, v_bias, o_weight, o_bias, norm1_gain, norm1_shift, up_weight, up_bias, down_weight, down_bias, norm2_gain, norm2_shift)))
    tokens = hidden_in.astype(jnp.float32).reshape(SLOTS, SLOT_LEN, D)
    masks = doc_mask.reshape(SLOTS, SLOT_LEN)
    rands = rand_blocks.reshape(SLOTS, SLOT_BLOCKS, 3)

    def whole(weights, inputs):

        def one_slot(element):
            return slot_layer(weights, element[0], element[1], element[2], element[3])
        return lax.map(jax.checkpoint(one_slot), (inputs, masks, doc_blocks, rands))
    outputs, pull = jax.vjp(whole, params, tokens)
    weight_grads, token_grads = pull(out_grad.reshape(SLOTS, SLOT_LEN, D))
    return (outputs.reshape(TOKENS, D), token_grads.reshape(TOKENS, D), weight_grads[0], weight_grads[1], weight_grads[2], weight_grads[3], weight_grads[4], weight_grads[5], weight_grads[6], weight_grads[7], weight_grads[8], weight_grads[9], weight_grads[10], weight_grads[11], weight_grads[12], weight_grads[13], weight_grads[14])
```

```python
import jax
import jax.numpy as jnp
from jax import lax
from jax.experimental import pallas as pl
from jax.experimental.pallas import tpu as pltpu
from jax.sharding import PartitionSpec as P

HD = 64
BLOCK = 64
SLOT_LEN = 4096
NEG = -1e30
EPS = 1e-12
WIN = 8


def dot_nt(left, right):
    return lax.dot_general(left, right, (((1,), (1,)), ((), ())), preferred_element_type=jnp.float32)


def dot_tn(left, right):
    return lax.dot_general(left, right, (((0,), (0,)), ((), ())), preferred_element_type=jnp.float32)


def dot_nn(left, right):
    return jnp.dot(left, right, preferred_element_type=jnp.float32)


def head_pick(rows, first):
    lane = lax.broadcasted_iota(jnp.int32, (1, rows.shape[1]), 1) // HD
    return [jnp.where(lane == first + head, rows, jnp.zeros_like(rows)) for head in range(3)]


def spread_heads(rows, first):
    return jnp.concatenate(head_pick(rows, first), axis=0)


def fold_heads(stacked, first):
    size = stacked.shape[0] // 3
    lane = lax.broadcasted_iota(jnp.int32, (1, stacked.shape[1]), 1) // HD
    total = None
    for head in range(3):
        part = jnp.where(lane == first + head, stacked[head * size : (head + 1) * size], 0.0)
        total = part if total is None else total + part
    return total


def window_ids(scal_ref, rand_ref, step, local_blocks):
    place, count = scal_ref[0], scal_ref[1]
    mine = place * local_blocks + step
    last = SLOT_LEN // BLOCK - 1
    ids, limits = [], []
    for shift in (-1, 0, 1):
        near = mine + shift
        good = (near >= 2) & (near <= last)
        at = jnp.clip(near, 0, last)
        ids.append(at)
        limits.append(jnp.where(good, jnp.clip(count - at * BLOCK, 0, BLOCK), 0))
    for slot in range(3):
        at = rand_ref[step * 3 + slot]
        ids.append(at)
        limits.append(jnp.clip(count - at * BLOCK, 0, BLOCK))
    for at in (0, 1):
        ids.append(jnp.int32(at))
        limits.append(jnp.clip(count - at * BLOCK, 0, BLOCK))
    return ids, limits


def take_blocks(ref, ids, low):
    parts = [ref[pl.ds(pl.multiple_of(at * BLOCK, BLOCK), BLOCK), low : low + 256] for at in ids]
    return jnp.concatenate(parts, axis=0)


def attend_fwd_kernel(scal_ref, rand_ref, q_ref, kv_ref, ctx_ref, p_ref, pg_ref, wide_ref):
    local_blocks = q_ref.shape[0] // BLOCK
    place, count = scal_ref[0], scal_ref[1]
    half = lax.broadcasted_iota(jnp.int32, (1, 128), 1)

    def one_block(step):
        ids, limits = window_ids(scal_ref, rand_ref, step, local_blocks)
        rows = pl.ds(pl.multiple_of(step * BLOCK, BLOCK), BLOCK)
        q_all = spread_heads(q_ref[rows, :], 0)
        raw = dot_nt(q_all, take_blocks(kv_ref, ids, 0))
        cut = jnp.concatenate(
            [jnp.where(half < BLOCK, limits[2 * t], limits[2 * t + 1]) for t in range(WIN // 2)], axis=1
        )
        inside = lax.broadcasted_iota(jnp.int32, (1, WIN * BLOCK), 1) % BLOCK
        raw = jnp.where(inside < cut, raw, NEG)
        expo = jnp.exp(raw - jnp.max(raw, axis=1, keepdims=True))
        probs = (expo * (1.0 / jnp.sum(expo, axis=1, keepdims=True))).astype(jnp.bfloat16)
        p_ref[step] = probs
        out = dot_nn(probs, take_blocks(kv_ref, ids, 128))
        ctx_ref[rows, :] = fold_heads(out, 1).astype(jnp.bfloat16)

    @pl.when(place == 0)
    def _():
        q_all = spread_heads(q_ref[0 : 2 * BLOCK, :], 0)
        chunk = WIN * BLOCK
        rows_all = q_all.shape[0]

        def scan_scores(part, top):
            at = pl.multiple_of(part * chunk, chunk)
            raw = dot_nt(q_all, kv_ref[pl.ds(at, chunk), 0:256])
            where_at = at + lax.broadcasted_iota(jnp.int32, (1, chunk), 1)
            raw = jnp.where(where_at < count, raw, NEG)
            wide_ref[part] = raw
            return jnp.maximum(top, jnp.max(raw, axis=1, keepdims=True))

        parts = SLOT_LEN // chunk
        top = lax.fori_loop(0, parts, scan_scores, jnp.full((rows_all, 1), NEG, jnp.float32))

        def scan_sum(part, total):
            expo = jnp.exp(wide_ref[part] - top)
            wide_ref[part] = expo
            return total + jnp.sum(expo, axis=1, keepdims=True)

        total = lax.fori_loop(0, parts, scan_sum, jnp.zeros((rows_all, 1), jnp.float32))
        inv = 1.0 / total

        def scan_out(part, out):
            probs = (wide_ref[part] * inv).astype(jnp.bfloat16)
            pg_ref[part] = probs
            at = pl.multiple_of(part * chunk, chunk)
            return out + dot_nn(probs, kv_ref[pl.ds(at, chunk), 128:384])

        out = lax.fori_loop(0, parts, scan_out, jnp.zeros((rows_all, 256), jnp.float32))
        ctx_ref[0 : 2 * BLOCK, :] = fold_heads(out, 1).astype(jnp.bfloat16)

    def pair(at, carry):
        one_block(2 * at)
        one_block(2 * at + 1)
        return carry

    lax.fori_loop(jnp.where(place == 0, 1, 0), local_blocks // 2, pair, 0)


def attend_forward(scal, rand, q_rows, kv_slot):
    tokens = q_rows.shape[0]
    blocks = tokens // BLOCK
    vmem = pl.BlockSpec(memory_space=pltpu.VMEM)
    smem = pl.BlockSpec(memory_space=pltpu.SMEM)
    return pl.pallas_call(
        attend_fwd_kernel,
        name="attend_forward",
        out_shape=(
            jax.ShapeDtypeStruct((tokens, 256), jnp.bfloat16),
            jax.ShapeDtypeStruct((blocks, 3 * BLOCK, WIN * BLOCK), jnp.bfloat16),
            jax.ShapeDtypeStruct((SLOT_LEN // (WIN * BLOCK), 6 * BLOCK, WIN * BLOCK), jnp.bfloat16),
        ),
        in_specs=[smem, smem, vmem, vmem],
        out_specs=(vmem, vmem, vmem),
        scratch_shapes=[pltpu.VMEM((SLOT_LEN // (WIN * BLOCK), 6 * BLOCK, WIN * BLOCK), jnp.float32)],
        compiler_params=pltpu.CompilerParams(vmem_limit_bytes=40 << 20),
    )(scal, rand, q_rows, kv_slot)


def attend_bwd_kernel(scal_ref, rand_ref, q_ref, kv_ref, p_ref, pg_ref, do_ref, dq_ref, dkv_ref, acc_ref):
    local_blocks = q_ref.shape[0] // BLOCK
    place = scal_ref[0]
    scale = HD ** (-0.5)
    acc_ref[...] = jnp.zeros_like(acc_ref)

    def add_rows(at, size, d_key, d_value):
        where_at = pl.ds(pl.multiple_of(at, BLOCK), size)
        acc_ref[where_at, 0:128] += d_key[:, 0:128]
        acc_ref[where_at, 128:256] += d_key[:, 128:256] + d_value[:, 0:128]
        acc_ref[where_at, 256:384] += d_value[:, 128:256]

    def one_block(step):
        ids, _ = window_ids(scal_ref, rand_ref, step, local_blocks)
        rows = pl.ds(pl.multiple_of(step * BLOCK, BLOCK), BLOCK)
        q_all = spread_heads(q_ref[rows, :], 0)
        do_all = spread_heads(do_ref[rows, :], 1)
        probs = p_ref[step]
        d_prob = dot_nt(do_all, take_blocks(kv_ref, ids, 128))
        wide = probs.astype(jnp.float32)
        mean = jnp.sum(d_prob * wide, axis=1, keepdims=True)
        d_score = (wide * (d_prob - mean)).astype(jnp.bfloat16)
        dq = dot_nn(d_score, take_blocks(kv_ref, ids, 0))
        dq_ref[rows, :] = (fold_heads(dq, 0) * scale).astype(jnp.bfloat16)
        d_key = dot_tn(d_score, q_all)
        d_value = dot_tn(probs, do_all)
        for slot in range(WIN):
            cut = slice(slot * BLOCK, (slot + 1) * BLOCK)
            add_rows(ids[slot] * BLOCK, BLOCK, d_key[cut], d_value[cut])

    @pl.when(place == 0)
    def _():
        chunk = WIN * BLOCK
        parts = SLOT_LEN // chunk
        q_all = spread_heads(q_ref[0 : 2 * BLOCK, :], 0)
        do_all = spread_heads(do_ref[0 : 2 * BLOCK, :], 1)

        def scan_mean(part, mean):
            at = pl.multiple_of(part * chunk, chunk)
            d_prob = dot_nt(do_all, kv_ref[pl.ds(at, chunk), 128:384])
            return mean + jnp.sum(d_prob * pg_ref[part].astype(jnp.float32), axis=1, keepdims=True)

        mean = lax.fori_loop(0, parts, scan_mean, jnp.zeros((q_all.shape[0], 1), jnp.float32))

        def scan_grad(part, dq):
            at = pl.multiple_of(part * chunk, chunk)
            probs = pg_ref[part]
            d_prob = dot_nt(do_all, kv_ref[pl.ds(at, chunk), 128:384])
            d_score = (probs.astype(jnp.float32) * (d_prob - mean)).astype(jnp.bfloat16)
            add_rows(at, chunk, dot_tn(d_score, q_all), dot_tn(probs, do_all))
            return dq + dot_nn(d_score, kv_ref[pl.ds(at, chunk), 0:256])

        dq = lax.fori_loop(0, parts, scan_grad, jnp.zeros((q_all.shape[0], 256), jnp.float32))
        dq_ref[0 : 2 * BLOCK, :] = (fold_heads(dq, 0) * scale).astype(jnp.bfloat16)

    def pair(at, carry):
        one_block(2 * at)
        one_block(2 * at + 1)
        return carry

    lax.fori_loop(jnp.where(place == 0, 1, 0), local_blocks // 2, pair, 0)
    dkv_ref[...] = acc_ref[...].astype(jnp.bfloat16)


def attend_backward(scal, rand, q_rows, kv_slot, probs, wide_probs, d_ctx):
    tokens = q_rows.shape[0]
    vmem = pl.BlockSpec(memory_space=pltpu.VMEM)
    smem = pl.BlockSpec(memory_space=pltpu.SMEM)
    return pl.pallas_call(
        attend_bwd_kernel,
        name="attend_backward",
        out_shape=(
            jax.ShapeDtypeStruct((tokens, 256), jnp.bfloat16),
            jax.ShapeDtypeStruct((SLOT_LEN, 384), jnp.bfloat16),
        ),
        in_specs=[smem, smem] + [vmem] * 5,
        out_specs=(vmem, vmem),
        scratch_shapes=[pltpu.VMEM((SLOT_LEN, 384), jnp.float32)],
        compiler_params=pltpu.CompilerParams(vmem_limit_bytes=40 << 20),
    )(scal, rand, q_rows, kv_slot, probs, wide_probs, d_ctx)


def norm_forward(values_in, gain_vec, shift_vec):
    row_mean = jnp.mean(values_in, axis=1, keepdims=True)
    centred = values_in - row_mean
    inv_std = lax.rsqrt(jnp.mean(centred * centred, axis=1, keepdims=True) + EPS)
    normed = centred * inv_std
    return (normed * gain_vec + shift_vec, normed, inv_std)


def norm_backward(gradient, normed, inv_std, gain_vec):
    scaled = gradient * gain_vec
    inner_term = (
        scaled
        - jnp.mean(scaled, axis=1, keepdims=True)
        - normed * jnp.mean(scaled * normed, axis=1, keepdims=True)
    )
    return (inner_term * inv_std, jnp.sum(gradient * normed, axis=0), jnp.sum(gradient, axis=0))


def partner_2(value, axis, apart):
    mask = 2**apart
    pairs = [(source, source ^ mask) for source in range(lax.axis_size(axis))]
    return lax.ppermute(value, axis, pairs)


def gelu_grad(pre_act, act_grad):
    _, gelu_pull = jax.vjp(lambda inner_val: jax.nn.gelu(inner_val, approximate=True), pre_act)
    return gelu_pull(act_grad)[0].astype(jnp.bfloat16)


def per_device(
    hidden_in, q_weight, q_bias, k_weight, v_weight, v_bias, o_weight, o_bias, norm1_gain, norm1_shift,
    up_weight, up_bias, down_weight, down_bias, norm2_gain, norm2_shift, doc_mask, doc_blocks, rand_blocks,
    out_grad,
):
    low = jnp.bfloat16
    tok_dev = hidden_in.shape[0]
    local_width = q_weight.shape[1]
    share_rows = out_grad.shape[0]
    slot_span = SLOT_LEN // tok_dev
    group_bits = slot_span.bit_length() - 1
    seq_index = lax.axis_index("seq")
    head_index = lax.axis_index("head")
    slot_place = seq_index % slot_span
    slot_index = seq_index // slot_span
    scale = HD ** (-0.5)
    query = ((dot_nn(hidden_in, q_weight) + q_bias).astype(low) * jnp.asarray(scale, low))
    query = jnp.pad(query, ((0, 0), (0, 256 - local_width)))
    kv_weight = jnp.concatenate([k_weight, v_weight], axis=1)
    kv_bias = jnp.concatenate([jnp.zeros_like(v_bias), v_bias])
    slot_pair = (dot_nn(hidden_in, kv_weight) + kv_bias).astype(low)
    for bit_index in range(group_bits):
        partner = partner_2(slot_pair, "seq", bit_index)
        upper_half = seq_index // 2**bit_index % 2 == 1
        slot_pair = jnp.where(
            upper_half,
            jnp.concatenate([partner, slot_pair], axis=0),
            jnp.concatenate([slot_pair, partner], axis=0),
        )
    slot_mask = lax.dynamic_slice_in_dim(doc_mask, slot_index * SLOT_LEN, SLOT_LEN, 0)
    count = jnp.minimum(jnp.sum(slot_mask), doc_blocks[slot_index] * BLOCK)
    scal = jnp.stack([slot_place, count]).astype(jnp.int32)
    rand = rand_blocks.reshape(-1)
    context, probs, wide_probs = attend_forward(scal, rand, query, slot_pair)
    o_pad = jnp.concatenate([jnp.zeros((256 - local_width, o_weight.shape[1]), low), o_weight], axis=0)
    attn_share = lax.psum_scatter(
        dot_nn(context, o_pad).astype(low), "head", scatter_dimension=0, tiled=True
    ).astype(jnp.float32)
    token_share = lax.dynamic_slice_in_dim(hidden_in, head_index * share_rows, share_rows, 0)
    first_sum = token_share.astype(jnp.float32) + attn_share + o_bias
    normed_one, unit_one, inv_one = norm_forward(first_sum, norm1_gain, norm1_shift)
    normed_low = lax.all_gather(normed_one.astype(low), "head", axis=0, tiled=True)
    pre_act = dot_nn(normed_low, up_weight) + up_bias
    act_low = jax.nn.gelu(pre_act, approximate=True).astype(low)
    ffn_share = lax.psum_scatter(
        dot_nn(act_low, down_weight).astype(low), "head", scatter_dimension=0, tiled=True
    ).astype(jnp.float32)
    second_sum = normed_one + ffn_share + down_bias
    layer_out, unit_two, inv_two = norm_forward(second_sum, norm2_gain, norm2_shift)
    second_grad, gain_two_grad, shift_two_grad = norm_backward(out_grad, unit_two, inv_two, norm2_gain)
    down_bias_grad = jnp.sum(second_grad, axis=0)
    second_low = lax.all_gather(second_grad.astype(low), "head", axis=0, tiled=True)
    pre_grad = gelu_grad(pre_act, dot_nt(second_low, down_weight))
    branch_grad = lax.psum_scatter(
        dot_nt(pre_grad, up_weight).astype(low), "head", scatter_dimension=0, tiled=True
    ).astype(jnp.float32)
    down_grad = dot_tn(act_low, second_low)
    up_grad = dot_tn(normed_low, pre_grad)
    up_bias_grad = jnp.sum(pre_grad.astype(jnp.float32), axis=0)
    first_grad, gain_one_grad, shift_one_grad = norm_backward(
        second_grad + branch_grad, unit_one, inv_one, norm1_gain
    )
    o_bias_grad = jnp.sum(first_grad, axis=0)
    first_full = lax.all_gather(first_grad.astype(low), "head", axis=0, tiled=True)
    o_grad = dot_tn(context, first_full)[256 - local_width :]
    d_ctx = dot_nt(first_full, o_pad).astype(low)
    query_low, slot_grad = attend_backward(scal, rand, query, slot_pair, probs, wide_probs, d_ctx)
    query_low = query_low[:, :local_width]
    own_grad = slot_grad.astype(jnp.float32)
    for bit_index in reversed(range(group_bits)):
        half_len = own_grad.shape[0] // 2
        upper_half = seq_index // 2**bit_index % 2 == 1
        lower_part = own_grad[:half_len]
        upper_part = own_grad[half_len:]
        kept_half = jnp.where(upper_half, upper_part, lower_part)
        given_half = jnp.where(upper_half, lower_part, upper_part)
        own_grad = kept_half + partner_2(given_half.astype(low), "seq", bit_index).astype(jnp.float32)
    kv_low = own_grad.astype(low)
    q_grad = dot_tn(hidden_in, query_low)
    q_bias_grad = jnp.sum(query_low.astype(jnp.float32), axis=0)
    kv_grad = dot_tn(hidden_in, kv_low)
    v_bias_grad = jnp.sum(kv_low[:, local_width:].astype(jnp.float32), axis=0)
    in_grad = first_grad + lax.psum_scatter(
        (dot_nt(query_low, q_weight) + dot_nt(kv_low, kv_weight)).astype(low),
        "head", scatter_dimension=0, tiled=True,
    ).astype(jnp.float32)
    summed = lax.psum(
        tuple(part.astype(low) for part in (q_grad, kv_grad, o_grad, up_grad, down_grad)), "seq"
    )
    summed = [part.astype(jnp.float32) for part in summed]
    bias_sums = lax.psum((q_bias_grad, v_bias_grad, up_bias_grad), "seq")
    norm_sums = lax.psum(
        (o_bias_grad, gain_one_grad, shift_one_grad, down_bias_grad, gain_two_grad, shift_two_grad),
        ("seq", "head"),
    )
    return (
        layer_out, in_grad, summed[0], bias_sums[0], summed[1][:, :local_width], summed[1][:, local_width:],
        bias_sums[1], summed[2], norm_sums[0], norm_sums[1], norm_sums[2], summed[3], bias_sums[2], summed[4],
        norm_sums[3], norm_sums[4], norm_sums[5],
    )


def solution(mesh):
    columns, vector, rows, whole = P(None, "head"), P("head"), P("head", None), P()
    tokens, shares = P("seq", None), P(("seq", "head"), None)
    in_specs = (
        tokens, columns, vector, columns, columns, vector, rows, whole, whole, whole, columns, vector, rows,
        whole, whole, whole, whole, whole, tokens, shares,
    )
    out_specs = (
        shares, shares, columns, vector, columns, columns, vector, rows, whole, whole, whole, columns, vector,
        rows, whole, whole, whole,
    )
    return jax.shard_map(per_device, mesh=mesh, in_specs=in_specs, out_specs=out_specs, check_vma=False)
```

```python
import jax
import jax.numpy as jnp
from jax import lax
from jax.experimental import pallas as pl
from jax.experimental.pallas import tpu as pltpu
from jax.sharding import PartitionSpec as P

HD = 64
BLOCK = 64
SLOT_LEN = 4096
NEG = -1e30
EPS = 1e-12
WIN = 8


def dot_nt(left, right):
    return lax.dot_general(left, right, (((1,), (1,)), ((), ())), preferred_element_type=jnp.float32)


def dot_tn(left, right):
    return lax.dot_general(left, right, (((0,), (0,)), ((), ())), preferred_element_type=jnp.float32)


def dot_nn(left, right):
    return jnp.dot(left, right, preferred_element_type=jnp.float32)


def head_pick(rows, first):
    lane = lax.broadcasted_iota(jnp.int32, (1, rows.shape[1]), 1) // HD
    return [jnp.where(lane == first + head, rows, jnp.zeros_like(rows)) for head in range(3)]


def spread_heads(rows, first):
    return jnp.concatenate(head_pick(rows, first), axis=0)


def fold_heads(stacked, first):
    size = stacked.shape[0] // 3
    lane = lax.broadcasted_iota(jnp.int32, (1, stacked.shape[1]), 1) // HD
    total = None
    for head in range(3):
        part = jnp.where(lane == first + head, stacked[head * size : (head + 1) * size], 0.0)
        total = part if total is None else total + part
    return total


def window_ids(scal_ref, rand_ref, step, local_blocks):
    place, count = scal_ref[0], scal_ref[1]
    mine = place * local_blocks + step
    last = SLOT_LEN // BLOCK - 1
    ids, limits = [], []
    for shift in (-1, 0, 1):
        near = mine + shift
        good = (near >= 2) & (near <= last)
        at = jnp.clip(near, 0, last)
        ids.append(at)
        limits.append(jnp.where(good, jnp.clip(count - at * BLOCK, 0, BLOCK), 0))
    for slot in range(3):
        at = rand_ref[step * 3 + slot]
        ids.append(at)
        limits.append(jnp.clip(count - at * BLOCK, 0, BLOCK))
    for at in (0, 1):
        ids.append(jnp.int32(at))
        limits.append(jnp.clip(count - at * BLOCK, 0, BLOCK))
    return ids, limits


def take_blocks(ref, ids, low):
    parts = [ref[pl.ds(pl.multiple_of(at * BLOCK, BLOCK), BLOCK), low : low + 256] for at in ids]
    return jnp.concatenate(parts, axis=0)


def attend_fwd_kernel(scal_ref, rand_ref, q_ref, kv_ref, ctx_ref, p_ref, pg_ref, wide_ref):
    local_blocks = q_ref.shape[0] // BLOCK
    place, count = scal_ref[0], scal_ref[1]
    half = lax.broadcasted_iota(jnp.int32, (1, 128), 1)

    def one_block(step):
        ids, limits = window_ids(scal_ref, rand_ref, step, local_blocks)
        rows = pl.ds(pl.multiple_of(step * BLOCK, BLOCK), BLOCK)
        q_all = spread_heads(q_ref[rows, :], 0)
        raw = dot_nt(q_all, take_blocks(kv_ref, ids, 0))
        cut = jnp.concatenate(
            [jnp.where(half < BLOCK, limits[2 * t], limits[2 * t + 1]) for t in range(WIN // 2)], axis=1
        )
        inside = lax.broadcasted_iota(jnp.int32, (1, WIN * BLOCK), 1) % BLOCK
        raw = jnp.where(inside < cut, raw, NEG)
        expo = jnp.exp(raw - jnp.max(raw, axis=1, keepdims=True))
        probs = (expo * (1.0 / jnp.sum(expo, axis=1, keepdims=True))).astype(jnp.bfloat16)
        p_ref[step] = probs
        out = dot_nn(probs, take_blocks(kv_ref, ids, 128))
        ctx_ref[rows, :] = fold_heads(out, 1).astype(jnp.bfloat16)

    @pl.when(place == 0)
    def _():
        q_all = spread_heads(q_ref[0 : 2 * BLOCK, :], 0)
        chunk = WIN * BLOCK
        rows_all = q_all.shape[0]

        def scan_scores(part, top):
            at = pl.multiple_of(part * chunk, chunk)
            raw = dot_nt(q_all, kv_ref[pl.ds(at, chunk), 0:256])
            where_at = at + lax.broadcasted_iota(jnp.int32, (1, chunk), 1)
            raw = jnp.where(where_at < count, raw, NEG)
            wide_ref[part] = raw
            return jnp.maximum(top, jnp.max(raw, axis=1, keepdims=True))

        parts = SLOT_LEN // chunk
        top = lax.fori_loop(0, parts, scan_scores, jnp.full((rows_all, 1), NEG, jnp.float32))

        def scan_sum(part, total):
            expo = jnp.exp(wide_ref[part] - top)
            wide_ref[part] = expo
            return total + jnp.sum(expo, axis=1, keepdims=True)

        total = lax.fori_loop(0, parts, scan_sum, jnp.zeros((rows_all, 1), jnp.float32))
        inv = 1.0 / total

        def scan_out(part, out):
            probs = (wide_ref[part] * inv).astype(jnp.bfloat16)
            pg_ref[part] = probs
            at = pl.multiple_of(part * chunk, chunk)
            return out + dot_nn(probs, kv_ref[pl.ds(at, chunk), 128:384])

        out = lax.fori_loop(0, parts, scan_out, jnp.zeros((rows_all, 256), jnp.float32))
        ctx_ref[0 : 2 * BLOCK, :] = fold_heads(out, 1).astype(jnp.bfloat16)

    def pair(at, carry):
        one_block(2 * at)
        one_block(2 * at + 1)
        return carry

    lax.fori_loop(jnp.where(place == 0, 1, 0), local_blocks // 2, pair, 0)


def attend_forward(scal, rand, q_rows, kv_slot):
    tokens = q_rows.shape[0]
    blocks = tokens // BLOCK
    vmem = pl.BlockSpec(memory_space=pltpu.VMEM)
    smem = pl.BlockSpec(memory_space=pltpu.SMEM)
    return pl.pallas_call(
        attend_fwd_kernel,
        name="attend_forward",
        out_shape=(
            jax.ShapeDtypeStruct((tokens, 256), jnp.bfloat16),
            jax.ShapeDtypeStruct((blocks, 3 * BLOCK, WIN * BLOCK), jnp.bfloat16),
            jax.ShapeDtypeStruct((SLOT_LEN // (WIN * BLOCK), 6 * BLOCK, WIN * BLOCK), jnp.bfloat16),
        ),
        in_specs=[smem, smem, vmem, vmem],
        out_specs=(vmem, vmem, vmem),
        scratch_shapes=[pltpu.VMEM((SLOT_LEN // (WIN * BLOCK), 6 * BLOCK, WIN * BLOCK), jnp.float32)],
        compiler_params=pltpu.CompilerParams(vmem_limit_bytes=40 << 20),
    )(scal, rand, q_rows, kv_slot)


def attend_bwd_kernel(scal_ref, rand_ref, q_ref, kv_ref, p_ref, pg_ref, do_ref, dq_ref, dkv_ref, acc_ref):
    local_blocks = q_ref.shape[0] // BLOCK
    place = scal_ref[0]
    scale = HD ** (-0.5)
    acc_ref[...] = jnp.zeros_like(acc_ref)

    def add_rows(at, size, d_key, d_value):
        where_at = pl.ds(pl.multiple_of(at, BLOCK), size)
        acc_ref[where_at, 0:128] += d_key[:, 0:128]
        acc_ref[where_at, 128:256] += d_key[:, 128:256] + d_value[:, 0:128]
        acc_ref[where_at, 256:384] += d_value[:, 128:256]

    def one_block(step):
        ids, _ = window_ids(scal_ref, rand_ref, step, local_blocks)
        rows = pl.ds(pl.multiple_of(step * BLOCK, BLOCK), BLOCK)
        q_all = spread_heads(q_ref[rows, :], 0)
        do_all = spread_heads(do_ref[rows, :], 1)
        probs = p_ref[step]
        d_prob = dot_nt(do_all, take_blocks(kv_ref, ids, 128))
        wide = probs.astype(jnp.float32)
        mean = jnp.sum(d_prob * wide, axis=1, keepdims=True)
        d_score = (wide * (d_prob - mean)).astype(jnp.bfloat16)
        dq = dot_nn(d_score, take_blocks(kv_ref, ids, 0))
        dq_ref[rows, :] = (fold_heads(dq, 0) * scale).astype(jnp.bfloat16)
        d_key = dot_tn(d_score, q_all)
        d_value = dot_tn(probs, do_all)
        for slot in range(WIN):
            cut = slice(slot * BLOCK, (slot + 1) * BLOCK)
            add_rows(ids[slot] * BLOCK, BLOCK, d_key[cut], d_value[cut])

    @pl.when(place == 0)
    def _():
        chunk = WIN * BLOCK
        parts = SLOT_LEN // chunk
        q_all = spread_heads(q_ref[0 : 2 * BLOCK, :], 0)
        do_all = spread_heads(do_ref[0 : 2 * BLOCK, :], 1)

        def scan_mean(part, mean):
            at = pl.multiple_of(part * chunk, chunk)
            d_prob = dot_nt(do_all, kv_ref[pl.ds(at, chunk), 128:384])
            return mean + jnp.sum(d_prob * pg_ref[part].astype(jnp.float32), axis=1, keepdims=True)

        mean = lax.fori_loop(0, parts, scan_mean, jnp.zeros((q_all.shape[0], 1), jnp.float32))

        def scan_grad(part, dq):
            at = pl.multiple_of(part * chunk, chunk)
            probs = pg_ref[part]
            d_prob = dot_nt(do_all, kv_ref[pl.ds(at, chunk), 128:384])
            d_score = (probs.astype(jnp.float32) * (d_prob - mean)).astype(jnp.bfloat16)
            add_rows(at, chunk, dot_tn(d_score, q_all), dot_tn(probs, do_all))
            return dq + dot_nn(d_score, kv_ref[pl.ds(at, chunk), 0:256])

        dq = lax.fori_loop(0, parts, scan_grad, jnp.zeros((q_all.shape[0], 256), jnp.float32))
        dq_ref[0 : 2 * BLOCK, :] = (fold_heads(dq, 0) * scale).astype(jnp.bfloat16)

    def pair(at, carry):
        one_block(2 * at)
        one_block(2 * at + 1)
        return carry

    lax.fori_loop(jnp.where(place == 0, 1, 0), local_blocks // 2, pair, 0)
    dkv_ref[...] = acc_ref[...].astype(jnp.bfloat16)


def attend_backward(scal, rand, q_rows, kv_slot, probs, wide_probs, d_ctx):
    tokens = q_rows.shape[0]
    vmem = pl.BlockSpec(memory_space=pltpu.VMEM)
    smem = pl.BlockSpec(memory_space=pltpu.SMEM)
    return pl.pallas_call(
        attend_bwd_kernel,
        name="attend_backward",
        out_shape=(
            jax.ShapeDtypeStruct((tokens, 256), jnp.bfloat16),
            jax.ShapeDtypeStruct((SLOT_LEN, 384), jnp.bfloat16),
        ),
        in_specs=[smem, smem] + [vmem] * 5,
        out_specs=(vmem, vmem),
        scratch_shapes=[pltpu.VMEM((SLOT_LEN, 384), jnp.float32)],
        compiler_params=pltpu.CompilerParams(vmem_limit_bytes=40 << 20),
    )(scal, rand, q_rows, kv_slot, probs, wide_probs, d_ctx)


MESH = pl.DeviceIdType.MESH
VM = pl.BlockSpec(memory_space=pltpu.VMEM)
LOW = jnp.bfloat16


def flip(index, bit):
    step = 1 << bit
    return index + step - 2 * step * ((index // step) % 2)


def remote(src, dst, send, recv, slot, where):
    return pltpu.make_async_remote_copy(
        src_ref=src, dst_ref=dst, send_sem=send.at[slot], recv_sem=recv.at[slot],
        device_id=where, device_id_type=MESH,
    )


def greet(partners):
    barrier = pltpu.get_barrier_semaphore()
    for where in partners:
        pl.semaphore_signal(barrier, inc=1, device_id=where, device_id_type=MESH)
    pl.semaphore_wait(barrier, len(partners))


def project_kernel(hid, qw, kw, vw, qb, vb, ow, q_out, kv_out, o_out, send, recv):
    tokens = hid.shape[0]
    half = tokens // 2
    seq, head = lax.axis_index("seq"), lax.axis_index("head")
    spans = SLOT_LEN // tokens
    place = seq % spans
    by_x, by_z = {"seq": flip(seq, 0)}, {"seq": flip(seq, 1)}
    core, far = {"head": flip(head, 0)}, {"head": flip(head, 1)}
    greet((by_x, by_z, core, far))

    mine, theirs = o_out.at[head], o_out.at[flip(head, 1)]
    o_core = remote(ow, mine, send, recv, 6, core)
    o_far = remote(ow, mine, send, recv, 7, far)
    o_relay = remote(theirs, theirs, send, recv, 8, core)
    o_far.start()
    o_core.start()
    o_out[head] = ow[...]

    def rows_of(owner, part):
        at = pl.multiple_of(owner * tokens + part * half, half)
        return kv_out.at[pl.ds(at, half)]

    def fill(part):
        rows = hid[part * half : (part + 1) * half, :]
        keys = dot_nn(rows, kw[...])
        values = dot_nn(rows, vw[...]) + vb[...]
        at = pl.multiple_of(place * tokens + part * half, half)
        kv_out[pl.ds(at, half), :] = jnp.concatenate([keys.astype(LOW), values.astype(LOW)], axis=1)

    own_a, own_b = rows_of(place, 0), rows_of(place, 1)
    fwd_a, fwd_b = rows_of(flip(place, 0), 0), rows_of(flip(place, 1), 1)
    copies = [
        remote(own_a, own_a, send, recv, 0, by_x),
        remote(own_b, own_b, send, recv, 1, by_z),
        remote(own_b, own_b, send, recv, 2, by_x),
        remote(own_a, own_a, send, recv, 3, by_z),
        remote(fwd_a, fwd_a, send, recv, 4, by_z),
        remote(fwd_b, fwd_b, send, recv, 5, by_x),
    ]
    fill(0)
    copies[0].start()
    fill(1)
    for at in (1, 2, 3):
        copies[at].start()
    for part in range(2):
        rows = hid[part * half : (part + 1) * half, :]
        query = (dot_nn(rows, qw[...]) + qb[...]).astype(LOW) * jnp.asarray(HD ** (-0.5), LOW)
        query = jnp.concatenate([query, jnp.zeros((half, 256 - query.shape[1]), LOW)], axis=1)
        q_out[part * half : (part + 1) * half, :] = query
    copies[0].wait_recv()
    copies[4].start()
    copies[1].wait_recv()
    copies[5].start()
    o_far.wait_recv()
    o_relay.start()
    for at in (2, 3, 4, 5):
        copies[at].wait_recv()
    o_core.wait_recv()
    o_relay.wait_recv()
    for copy in copies + [o_core, o_far, o_relay]:
        copy.wait_send()


def project(hid, qw, kw, vw, qb, vb, ow):
    tokens, width = hid.shape
    heads = lax.axis_size("head")
    return pl.pallas_call(
        project_kernel,
        name="project_gather",
        out_shape=(
            jax.ShapeDtypeStruct((tokens, 256), LOW),
            jax.ShapeDtypeStruct((SLOT_LEN, 2 * kw.shape[1]), LOW),
            jax.ShapeDtypeStruct((heads, ow.shape[0], width), LOW),
        ),
        in_specs=[VM] * 7,
        out_specs=(VM,) * 3,
        scratch_shapes=[pltpu.SemaphoreType.DMA((9,)), pltpu.SemaphoreType.DMA((9,))],
        compiler_params=pltpu.CompilerParams(
            collective_id=0, has_side_effects=True, vmem_limit_bytes=32 << 20
        ),
    )(hid, qw, kw, vw, qb.reshape(1, -1), vb.reshape(1, -1), ow)


def norm_fwd(values, gain, shift):
    centred = values - jnp.mean(values, axis=1, keepdims=True)
    inv = lax.rsqrt(jnp.mean(centred * centred, axis=1, keepdims=True) + EPS)
    unit = centred * inv
    return unit * gain + shift, unit, inv


def norm_bwd(grad, unit, inv, gain):
    scaled = grad * gain
    inner = (
        scaled
        - jnp.mean(scaled, axis=1, keepdims=True)
        - unit * jnp.mean(scaled * unit, axis=1, keepdims=True)
    )
    return inner * inv


def column_sum(values):
    return jnp.sum(values, axis=0, keepdims=True)


CHUNKS = 2
ROOT = 0.7978845608028654
CUBE = 0.044715


def middle_kernel(
    ctx, o_full, hid, o_bias, gain1, shift1, up_w, up_b, down_w, down_b, gain2, shift2, out_grad,
    layer_out, first_out, d_ctx, up_grad, down_grad, o_grad, vec,
    ctx_all, normed, unit1, inv1, second, x_all, s_all, f_all, slope, act, pre_all,
    keep, to_core, from_core, to_far, from_far, send, recv,
):
    share = out_grad.shape[0]
    rows = share // CHUNKS
    width = hid.shape[1]
    seq, head = lax.axis_index("seq"), lax.axis_index("head")
    core, far, both = flip(head, 0), flip(head, 1), flip(flip(head, 0), 1)
    order = (head, core, far, both)
    greet(tuple({"head": at} for at in order[1:]))
    counter = [0]

    def copy_to(src, dst, where):
        slot = counter[0]
        counter[0] += 1
        made.append(remote(src, dst, send, recv, slot, {"head": where}))
        return made[-1]

    made = []

    def own_rows(part):
        return slice(part * rows, (part + 1) * rows)

    def block_rows(owner, part):
        return pl.ds(pl.multiple_of(owner * share + part * rows, rows), rows)

    ctx_copies = []
    for part in range(CHUNKS):
        for at in (3, 2, 1):
            ctx_copies.append(
                copy_to(ctx.at[block_rows(order[at], part)], ctx_all.at[head, own_rows(part)], order[at])
            )
            ctx_copies[-1].start()
    for part in range(CHUNKS):
        ctx_all[head, own_rows(part)] = ctx[block_rows(head, part), :]

    class Gather:
        def __init__(self, buffer):
            self.buffer = buffer
            self.to_core, self.to_far, self.relay = [None] * CHUNKS, [None] * CHUNKS, [None] * CHUNKS

        def start(self, part):
            own = self.buffer.at[part, 0]
            self.to_far[part] = copy_to(own, self.buffer.at[part, 2], far)
            self.to_far[part].start()
            self.to_core[part] = copy_to(own, self.buffer.at[part, 1], core)
            self.to_core[part].start()

        def pass_on(self, part):
            self.to_far[part].wait_recv()
            self.relay[part] = copy_to(self.buffer.at[part, 2], self.buffer.at[part, 3], core)
            self.relay[part].start()

        def pair(self, part, at):
            return self.buffer[part, 2 * at : 2 * at + 2].reshape(2 * rows, width)

    class Scatter:
        def __init__(self, at):
            self.at = at
            self.near, self.through, self.away = [None] * CHUNKS, [None] * CHUNKS, [None] * CHUNKS

        def put_near(self, part, partial):
            keep[part, 0] = partial[:rows]
            to_core[self.at, part, 0] = partial[rows:].astype(LOW)
            self.near[part] = copy_to(to_core.at[self.at, part, 0], from_core.at[self.at, part, 0], core)
            self.near[part].start()

        def put_far(self, part, partial):
            to_core[self.at, part, 1] = partial[rows:].astype(LOW)
            self.through[part] = copy_to(to_core.at[self.at, part, 1], from_core.at[self.at, part, 1], core)
            self.through[part].start()
            keep[part, 1] = partial[:rows]

        def pass_on(self, part):
            self.through[part].wait_recv()
            total = keep[part, 1] + from_core[self.at, part, 1].astype(jnp.float32)
            to_far[self.at, part] = total.astype(LOW)
            self.away[part] = copy_to(to_far.at[self.at, part], from_far.at[self.at, part], far)
            self.away[part].start()

        def result(self, part):
            self.near[part].wait_recv()
            self.away[part].wait_recv()
            return (
                keep[part, 0]
                + from_core[self.at, part, 0].astype(jnp.float32)
                + from_far[self.at, part].astype(jnp.float32)
            )

    def exchange(gather, scatter, make):
        for part in range(CHUNKS):
            gather.to_core[part].wait_recv()
            scatter.put_near(part, make(part, 0))
        gather.pass_on(0)
        for part in range(CHUNKS):
            gather.relay[part].wait_recv()
            scatter.put_far(part, make(part, 1))
            if part + 1 < CHUNKS:
                gather.pass_on(part + 1)
            scatter.pass_on(part)

    x_gather, s_gather, f_gather = Gather(x_all), Gather(s_all), Gather(f_all)
    ffn_scatter, branch_scatter = Scatter(0), Scatter(1)

    for part in range(CHUNKS):
        for at in range(3):
            ctx_copies[part * 3 + at].wait_recv()
        attn = None
        for at in range(4):
            rows_at = ctx_all[at, own_rows(part)]
            weight = o_full[at]
            weight = jnp.concatenate([jnp.zeros((256 - weight.shape[0], width), LOW), weight], axis=0)
            term = dot_nn(rows_at, weight)
            attn = term if attn is None else attn + term
        token = hid[block_rows(head, part), :].astype(jnp.float32)
        normed_f, unit_f, inv_f = norm_fwd(token + attn + o_bias[...], gain1[...], shift1[...])
        normed[own_rows(part)] = normed_f
        unit1[own_rows(part)] = unit_f
        inv1[own_rows(part)] = inv_f
        x_all[part, 0] = normed_f.astype(LOW)
        x_gather.start(part)

    def ffn_forward(part, at):
        pre = dot_nn(x_gather.pair(part, at), up_w[...]) + up_b[...]
        square = pre * pre
        tanh = jnp.tanh(ROOT * (pre + CUBE * square * pre))
        slope[part, at] = 0.5 * (1.0 + tanh) + (0.5 * ROOT) * pre * (1.0 - tanh * tanh) * (
            1.0 + (3.0 * CUBE) * square
        )
        acted = (0.5 * pre * (1.0 + tanh)).astype(LOW)
        act[part, at] = acted
        return dot_nn(acted, down_w[...])

    exchange(x_gather, ffn_scatter, ffn_forward)

    gain2_sum, shift2_sum, down_sum = 0.0, 0.0, 0.0
    for part in range(CHUNKS):
        total = normed[own_rows(part)] + ffn_scatter.result(part) + down_b[...]
        out, unit_f, inv_f = norm_fwd(total, gain2[...], shift2[...])
        layer_out[own_rows(part)] = out
        grad = out_grad[own_rows(part)]
        second_f = norm_bwd(grad, unit_f, inv_f, gain2[...])
        second[own_rows(part)] = second_f
        s_all[part, 0] = second_f.astype(LOW)
        s_gather.start(part)
        gain2_sum += column_sum(grad * unit_f)
        shift2_sum += column_sum(grad)
        down_sum += column_sum(second_f)

    bias_sum = [0.0]

    def ffn_backward(part, at):
        pulled = dot_nt(s_gather.pair(part, at), down_w[...])
        pre_grad = (pulled * slope[part, at]).astype(LOW)
        pre_all[part, at] = pre_grad
        bias_sum[0] += column_sum(pre_grad.astype(jnp.float32))
        return dot_nt(pre_grad, up_w[...])

    exchange(s_gather, branch_scatter, ffn_backward)

    tokens = 4 * share
    step = 256

    def weight_rows(at, carry):
        cut = pl.ds(pl.multiple_of(at * step, step), step)
        down_grad[cut, :] = dot_tn(
            act[:, :, :, cut].reshape(tokens, step), s_all[...].reshape(tokens, width)
        ).astype(LOW)
        up_grad[cut, :] = dot_tn(
            x_all[:, :, :, cut].reshape(tokens, step), pre_all[...].reshape(tokens, up_w.shape[1])
        ).astype(LOW)
        return carry

    gain1_sum, shift1_sum, o_sum = 0.0, 0.0, 0.0
    for part in range(CHUNKS):
        grad = second[own_rows(part)] + branch_scatter.result(part)
        unit_f = unit1[own_rows(part)]
        first_f = norm_bwd(grad, unit_f, inv1[own_rows(part)], gain1[...])
        first_out[own_rows(part)] = first_f
        f_all[part, 0] = first_f.astype(LOW)
        f_gather.start(part)
        gain1_sum += column_sum(grad * unit_f)
        shift1_sum += column_sum(grad)
        o_sum += column_sum(first_f)
    lax.fori_loop(0, width // step, weight_rows, 0)

    weight = o_full[head]
    weight = jnp.concatenate([jnp.zeros((256 - weight.shape[0], width), LOW), weight], axis=0)
    o_total = None

    def back(part, at):
        rows_f = f_gather.pair(part, at)
        grad = dot_nt(rows_f, weight).astype(LOW)
        term = None
        first_ctx = ctx[block_rows(order[2 * at], part), :]
        second_ctx = ctx[block_rows(order[2 * at + 1], part), :]
        d_ctx[block_rows(order[2 * at], part), :] = grad[:rows]
        d_ctx[block_rows(order[2 * at + 1], part), :] = grad[rows:]
        return dot_tn(rows_f, jnp.concatenate([first_ctx, second_ctx], axis=0))

    o_total = 0.0
    for part in range(CHUNKS):
        f_gather.to_core[part].wait_recv()
        o_total += back(part, 0)
    for part in range(CHUNKS):
        f_gather.pass_on(part)
    for part in range(CHUNKS):
        f_gather.relay[part].wait_recv()
        o_total += back(part, 1)
    o_grad[...] = o_total
    zero = jnp.zeros((1, width), jnp.float32)
    vec[...] = jnp.concatenate(
        [o_sum, gain1_sum, shift1_sum, down_sum, gain2_sum, shift2_sum, bias_sum[0], zero], axis=0
    )
    for copy in made:
        copy.wait_send()


def middle(ctx, o_full, hid, o_bias, gain1, shift1, up_w, up_b, down_w, down_b, gain2, shift2, out_grad):
    tokens, width = hid.shape
    share = out_grad.shape[0]
    rows = share // CHUNKS
    hidden = up_w.shape[1]
    f32 = jnp.float32
    line = lambda value: value.reshape(1, -1)
    gathered = pltpu.VMEM((CHUNKS, 4, rows, width), LOW)
    copies = CHUNKS * (3 + 3 * 3 + 2 * 3)
    return pl.pallas_call(
        middle_kernel,
        name="middle",
        out_shape=(
            jax.ShapeDtypeStruct((share, width), f32),
            jax.ShapeDtypeStruct((share, width), f32),
            jax.ShapeDtypeStruct((tokens, 256), LOW),
            jax.ShapeDtypeStruct((width, hidden), LOW),
            jax.ShapeDtypeStruct((hidden, width), LOW),
            jax.ShapeDtypeStruct((width, 256), f32),
            jax.ShapeDtypeStruct((8, width), f32),
        ),
        in_specs=[VM] * 13,
        out_specs=(VM,) * 7,
        scratch_shapes=[
            pltpu.VMEM((4, share, 256), LOW),
            pltpu.VMEM((share, width), f32),
            pltpu.VMEM((share, width), f32),
            pltpu.VMEM((share, 1), f32),
            pltpu.VMEM((share, width), f32),
            gathered,
            gathered,
            gathered,
            pltpu.VMEM((CHUNKS, 2, 2 * rows, hidden), f32),
            pltpu.VMEM((CHUNKS, 2, 2 * rows, hidden), LOW),
            pltpu.VMEM((CHUNKS, 2, 2 * rows, hidden), LOW),
            pltpu.VMEM((CHUNKS, 2, rows, width), f32),
            pltpu.VMEM((2, CHUNKS, 2, rows, width), LOW),
            pltpu.VMEM((2, CHUNKS, 2, rows, width), LOW),
            pltpu.VMEM((2, CHUNKS, rows, width), LOW),
            pltpu.VMEM((2, CHUNKS, rows, width), LOW),
            pltpu.SemaphoreType.DMA((copies,)),
            pltpu.SemaphoreType.DMA((copies,)),
        ],
        compiler_params=pltpu.CompilerParams(
            collective_id=1, has_side_effects=True, vmem_limit_bytes=48 << 20
        ),
    )(
        ctx, o_full, hid, line(o_bias), line(gain1), line(shift1), up_w, line(up_b), down_w, line(down_b),
        line(gain2), line(shift2), out_grad,
    )


def tail_kernel(
    hid, dq, dkv, qw, kw, vw, first, up_grad, down_grad, o_grad, vec,
    in_grad, big_out, small_out, vec_out,
    pair_in, pair_out, partial, small, big_ring, small_ring, near_out, near_in, far_out, far_in,
    vec_now, vec_send, vec_recv, send, recv, ring_send, ring_recv,
):
    n = lax.axis_size("seq")
    tokens, width = hid.shape
    half, share = tokens // 2, first.shape[0]
    depth = big_ring.shape[2]
    spans = SLOT_LEN // tokens
    seq, head = lax.axis_index("seq"), lax.axis_index("head")
    place = seq % spans
    f32 = jnp.float32
    side, along = seq % 2, seq // 2
    spot = along + side * (n - 1 - 2 * along)

    def member(pos):
        turn = pos // (n // 2)
        return 2 * (pos + turn * (n - 1 - 2 * pos)) + turn

    ways = ({"seq": member((spot + 1) % n)}, {"seq": member((spot + n - 1) % n)})
    signs = (-1, 1)
    by_x, by_z = {"seq": flip(seq, 0)}, {"seq": flip(seq, 1)}
    core, far = flip(head, 0), flip(head, 1)
    both = flip(core, 1)
    seq_bits = n.bit_length() - 1
    vec_peers = [{"seq": flip(seq, bit)} for bit in range(seq_bits)] + [{"head": core}, {"head": far}]
    greet((by_x, by_z, *ways, *vec_peers))

    def rows_of(owner, part):
        return pl.ds(pl.multiple_of(owner * tokens + part * half, half), half)

    x_at, z_at = flip(place, 0), flip(place, 1)
    d_at = flip(x_at, 1)
    copies = [
        remote(dkv.at[rows_of(d_at, 0)], pair_in.at[0], send, recv, 0, by_z),
        remote(dkv.at[rows_of(d_at, 1)], pair_in.at[1], send, recv, 1, by_x),
        remote(dkv.at[rows_of(x_at, 1)], pair_in.at[2], send, recv, 2, by_x),
        remote(dkv.at[rows_of(z_at, 0)], pair_in.at[3], send, recv, 3, by_z),
        remote(pair_out.at[0], pair_in.at[4], send, recv, 4, by_x),
        remote(pair_out.at[1], pair_in.at[5], send, recv, 5, by_z),
    ]
    for at in range(4):
        copies[at].start()

    gap = jnp.zeros((width, 256 - qw.shape[1]), LOW)
    partial[...] = dot_nt(dq[...], jnp.concatenate([qw[...], gap], axis=1))
    copies[0].wait_recv()
    pair_out[0] = (dkv[rows_of(x_at, 0), :].astype(f32) + pair_in[0].astype(f32)).astype(LOW)
    copies[4].start()
    copies[1].wait_recv()
    pair_out[1] = (dkv[rows_of(z_at, 1), :].astype(f32) + pair_in[1].astype(f32)).astype(LOW)
    copies[5].start()

    rings = ((big_ring, big_out, (up_grad, down_grad)), (small_ring, small_out, (small.at[0], small.at[1])))

    def chunk(pos):
        return pl.ds(pl.multiple_of(((pos + 2 * n) % n) * depth, 16), depth)

    def reduce_copy(kind, way, step):
        ring = rings[kind][0]
        return pltpu.make_async_remote_copy(
            src_ref=ring.at[way, step], dst_ref=ring.at[way, step + 1],
            send_sem=ring_send.at[0, kind, way, step], recv_sem=ring_recv.at[0, kind, way, step],
            device_id=ways[way], device_id_type=MESH,
        )

    def spread_copy(kind, way, step):
        rows = rings[kind][1].at[way, chunk(spot + signs[way] * (step - 1))]
        return pltpu.make_async_remote_copy(
            src_ref=rows, dst_ref=rows,
            send_sem=ring_send.at[1, kind, way, step], recv_sem=ring_recv.at[1, kind, way, step],
            device_id=ways[way], device_id_type=MESH,
        )

    def open_ring(kind):
        ring, _, source = rings[kind]
        for way in range(2):
            ring[way, 0] = source[way][chunk(spot), :]
            reduce_copy(kind, way, 0).start()

    def add_ring(kind, way, step):
        ring, _, source = rings[kind]
        reduce_copy(kind, way, step).wait_recv()
        mine = source[way][chunk(spot + signs[way] * (step + 1)), :]
        ring[way, step + 1] = (ring[way, step + 1].astype(f32) + mine.astype(f32)).astype(LOW)

    open_ring(0)
    q_part = dot_tn(hid[...], dq[...])
    small[1, 0:width, 0:128] = q_part[:, 0:128].astype(LOW)
    small[1, 0:width, 128:256] = (q_part[:, 128:256] + o_grad[:, 0:128]).astype(LOW)
    small[1, 0:width, 256:384] = o_grad[:, 128:256].astype(LOW)
    if n * depth > width:
        small[:, width:, :] = jnp.zeros((2, n * depth - width, small.shape[2]), LOW)
    for at in range(2, 6):
        copies[at].wait_recv()
    own = []
    for part in range(2):
        mine = dkv[rows_of(place, part), :].astype(f32)
        first_in, second_in = (3, 4) if part == 0 else (2, 5)
        own.append((mine + pair_in[first_in].astype(f32) + pair_in[second_in].astype(f32)).astype(LOW))
    own = jnp.concatenate(own, axis=0)
    small[0, 0:width, :] = dot_tn(hid[...], own).astype(LOW)
    open_ring(1)
    partial[...] += dot_nt(own[:, 0:256], jnp.concatenate([kw[...], gap], axis=1)) + dot_nt(
        own[:, 128:384], jnp.concatenate([gap, vw[...]], axis=1)
    )

    def share_rows(owner):
        return partial[pl.ds(pl.multiple_of(owner * share, share), share), :]

    near_out[0] = share_rows(both).astype(LOW)
    near_out[1] = share_rows(core).astype(LOW)
    near = [remote(near_out.at[at], near_in.at[at], send, recv, 6 + at, {"head": core}) for at in range(2)]
    near[0].start()
    near[1].start()
    sums = jnp.concatenate(
        [
            jnp.concatenate(
                [column_sum(dq[...].astype(f32)), jnp.zeros((1, width - dq.shape[1]), f32)], axis=1
            ),
            jnp.concatenate(
                [column_sum(own.astype(f32)), jnp.zeros((1, width - own.shape[1]), f32)], axis=1
            ),
            jnp.zeros((6, width), f32),
        ],
        axis=0,
    )
    vec_now[0:8] = vec[...]
    vec_now[8:16] = sums
    far_copy = remote(far_out, far_in, send, recv, 8, {"head": far})

    def vec_copy(at):
        return remote(vec_send.at[at], vec_recv.at[at], send, recv, 9 + at, vec_peers[at])

    def ring_step(step):
        for kind in range(2):
            for way in range(2):
                add_ring(kind, way, step)
                reduce_copy(kind, way, step + 1).start()

    steps = seq_bits + 2
    for at in range(steps):
        vec_send[at] = vec_now[...]
        vec_copy(at).start()
        if at < n - 2:
            ring_step(at)
        if at == 0:
            near[0].wait_recv()
            far_out[...] = (share_rows(far) + near_in[0].astype(f32)).astype(LOW)
            far_copy.start()
        vec_copy(at).wait_recv()
        if at == seq_bits - 1:
            total = vec_now[...] + vec_recv[at]
            vec_now[...] = total
            vec_out[8:16] = total[8:16]
            vec_out[16:24] = total[0:8]
        else:
            vec_now[...] += vec_recv[at]
    vec_out[0:8] = vec_now[0:8]

    def ring_body(step, carry):
        ring_step(step)
        return carry

    lax.fori_loop(min(steps, n - 2), n - 2, ring_body, 0)
    for kind in range(2):
        ring, out, _ = rings[kind]
        for way in range(2):
            add_ring(kind, way, n - 2)
            out[way, chunk(spot - signs[way])] = ring[way, n - 1]
            spread_copy(kind, way, 0).start()
    near[1].wait_recv()
    far_copy.wait_recv()
    in_grad[...] = first[...] + share_rows(head) + near_in[1].astype(f32) + far_in[...].astype(f32)

    def spread_body(step, carry):
        for kind in range(2):
            for way in range(2):
                spread_copy(kind, way, step).wait_recv()
                spread_copy(kind, way, step + 1).start()
        return carry

    lax.fori_loop(0, n - 2, spread_body, 0)
    for kind in range(2):
        for way in range(2):
            spread_copy(kind, way, n - 2).wait_recv()

    def close_body(step, carry):
        for kind in range(2):
            for way in range(2):
                reduce_copy(kind, way, step).wait_send()
                spread_copy(kind, way, step).wait_send()
        return carry

    lax.fori_loop(0, n - 1, close_body, 0)
    for copy in copies + near + [far_copy] + [vec_copy(at) for at in range(steps)]:
        copy.wait_send()


def tail(hid, dq, dkv, qw, kw, vw, first, up_grad, down_grad, o_grad, vec):
    n = lax.axis_size("seq")
    tokens, width = hid.shape
    share = first.shape[0]
    pair = dkv.shape[1]
    depth = 16 * (-(-width // (16 * n)))
    rows = n * depth
    f32 = jnp.float32
    if rows > width:
        up_grad = jnp.pad(up_grad, ((0, rows - width), (0, 0)))
        down_grad = jnp.pad(down_grad, ((0, rows - width), (0, 0)))
    steps = n.bit_length() + 1
    return pl.pallas_call(
        tail_kernel,
        name="tail",
        out_shape=(
            jax.ShapeDtypeStruct((share, width), f32),
            jax.ShapeDtypeStruct((2, rows, up_grad.shape[1]), LOW),
            jax.ShapeDtypeStruct((2, rows, pair), LOW),
            jax.ShapeDtypeStruct((24, width), f32),
        ),
        in_specs=[VM] * 11,
        out_specs=(VM,) * 4,
        scratch_shapes=[
            pltpu.VMEM((6, tokens // 2, pair), LOW),
            pltpu.VMEM((2, tokens // 2, pair), LOW),
            pltpu.VMEM((tokens, width), f32),
            pltpu.VMEM((2, rows, pair), LOW),
            pltpu.VMEM((2, n, depth, up_grad.shape[1]), LOW),
            pltpu.VMEM((2, n, depth, pair), LOW),
            pltpu.VMEM((2, share, width), LOW),
            pltpu.VMEM((2, share, width), LOW),
            pltpu.VMEM((share, width), LOW),
            pltpu.VMEM((share, width), LOW),
            pltpu.VMEM((16, width), f32),
            pltpu.VMEM((steps, 16, width), f32),
            pltpu.VMEM((steps, 16, width), f32),
            pltpu.SemaphoreType.DMA((9 + steps,)),
            pltpu.SemaphoreType.DMA((9 + steps,)),
            pltpu.SemaphoreType.DMA((2, 2, 2, n - 1)),
            pltpu.SemaphoreType.DMA((2, 2, 2, n - 1)),
        ],
        compiler_params=pltpu.CompilerParams(
            collective_id=2, has_side_effects=True, vmem_limit_bytes=48 << 20
        ),
    )(hid, dq, dkv, qw, kw, vw, first, up_grad, down_grad, o_grad, vec)


def per_device(
    hidden_in, q_weight, q_bias, k_weight, v_weight, v_bias, o_weight, o_bias, norm1_gain, norm1_shift,
    up_weight, up_bias, down_weight, down_bias, norm2_gain, norm2_shift, doc_mask, doc_blocks, rand_blocks,
    out_grad,
):
    f32 = jnp.float32
    tokens, width = hidden_in.shape
    local = q_weight.shape[1]
    slot_span = SLOT_LEN // tokens
    seq_index = lax.axis_index("seq")
    slot_index = seq_index // slot_span
    slot_mask = lax.dynamic_slice_in_dim(doc_mask, slot_index * SLOT_LEN, SLOT_LEN, 0)
    count = jnp.minimum(jnp.sum(slot_mask), doc_blocks[slot_index] * BLOCK)
    scal = jnp.stack([seq_index % slot_span, count]).astype(jnp.int32)
    rand = rand_blocks.reshape(-1)
    query, slot_pair, o_full = project(hidden_in, q_weight, k_weight, v_weight, q_bias, v_bias, o_weight)
    context, probs, wide_probs = attend_forward(scal, rand, query, slot_pair)
    layer_out, first, d_ctx, up_part, down_part, o_part, vec = middle(
        context, o_full, hidden_in, o_bias, norm1_gain, norm1_shift, up_weight, up_bias, down_weight,
        down_bias, norm2_gain, norm2_shift, out_grad,
    )
    dq, dkv = attend_backward(scal, rand, query, slot_pair, probs, wide_probs, d_ctx)
    in_grad, big, small, vecs = tail(
        hidden_in, dq, dkv, q_weight, k_weight, v_weight, first, up_part, down_part, o_part, vec
    )
    small = small[:, :width].astype(f32)
    return (
        layer_out, in_grad, small[1, :, :local], vecs[8, :local], small[0, :, :local], small[0, :, local:],
        vecs[9, local : 2 * local], small[1, :, local:].T, vecs[0], vecs[1], vecs[2],
        big[0, :width].astype(f32), vecs[22], big[1, :width].astype(f32), vecs[3], vecs[4], vecs[5],
    )


def solution(mesh):
    columns, vector, rows, whole = P(None, "head"), P("head"), P("head", None), P()
    tokens, shares = P("seq", None), P(("seq", "head"), None)
    in_specs = (
        tokens, columns, vector, columns, columns, vector, rows, whole, whole, whole, columns, vector, rows,
        whole, whole, whole, whole, whole, tokens, shares,
    )
    out_specs = (
        shares, shares, columns, vector, columns, columns, vector, rows, whole, whole, whole, columns, vector,
        rows, whole, whole, whole,
    )
    return jax.shard_map(per_device, mesh=mesh, in_specs=in_specs, out_specs=out_specs, check_vma=False)
```

```python
import jax
import jax.numpy as jnp
from jax import lax
from jax.experimental import pallas as pl
from jax.experimental.pallas import tpu as pltpu
from jax.sharding import PartitionSpec as P

HD = 64
BLOCK = 64
SLOT_LEN = 4096
NEG = -1e30
EPS = 1e-12
WIN = 8


def dot_nt(left, right):
    return lax.dot_general(left, right, (((1,), (1,)), ((), ())), preferred_element_type=jnp.float32)


def dot_tn(left, right):
    return lax.dot_general(left, right, (((0,), (0,)), ((), ())), preferred_element_type=jnp.float32)


def dot_nn(left, right):
    return jnp.dot(left, right, preferred_element_type=jnp.float32)


def head_pick(rows, first):
    lane = lax.broadcasted_iota(jnp.int32, (1, rows.shape[1]), 1) // HD
    return [jnp.where(lane == first + head, rows, jnp.zeros_like(rows)) for head in range(3)]


def spread_heads(rows, first):
    return jnp.concatenate(head_pick(rows, first), axis=0)


def fold_heads(stacked, first):
    size = stacked.shape[0] // 3
    lane = lax.broadcasted_iota(jnp.int32, (1, stacked.shape[1]), 1) // HD
    total = None
    for head in range(3):
        part = jnp.where(lane == first + head, stacked[head * size : (head + 1) * size], 0.0)
        total = part if total is None else total + part
    return total


def slot_spot(tokens):
    spans = SLOT_LEN // tokens
    seq = lax.axis_index("seq")
    return seq % spans, seq // spans


def window_ids(place, count, rand_ref, step, local_blocks):
    mine = place * local_blocks + step
    last = SLOT_LEN // BLOCK - 1
    ids, limits = [], []
    for shift in (-1, 0, 1):
        near = mine + shift
        good = (near >= 2) & (near <= last)
        at = jnp.clip(near, 0, last)
        ids.append(at)
        limits.append(jnp.where(good, jnp.clip(count - at * BLOCK, 0, BLOCK), 0))
    for slot in range(3):
        at = rand_ref[slot, step]
        ids.append(at)
        limits.append(jnp.clip(count - at * BLOCK, 0, BLOCK))
    for at in (0, 1):
        ids.append(jnp.int32(at))
        limits.append(jnp.clip(count - at * BLOCK, 0, BLOCK))
    return ids, limits


def take_blocks(ref, ids, low):
    parts = [ref[pl.ds(pl.multiple_of(at * BLOCK, BLOCK), BLOCK), low : low + 256] for at in ids]
    return jnp.concatenate(parts, axis=0)


def attend_fwd_kernel(blocks_ref, rand_ref, mask_ref, q_ref, kv_ref, ctx_ref, p_ref, pg_ref, wide_ref):
    local_blocks = q_ref.shape[0] // BLOCK
    place, slot = slot_spot(q_ref.shape[0])
    lines = SLOT_LEN // mask_ref.shape[1]
    marked = jnp.sum(mask_ref[pl.ds(pl.multiple_of(slot * lines, lines), lines), :])
    count = jnp.minimum(marked, blocks_ref[slot] * BLOCK)
    half = lax.broadcasted_iota(jnp.int32, (1, 128), 1)

    def one_block(step):
        ids, limits = window_ids(place, count, rand_ref, step, local_blocks)
        rows = pl.ds(pl.multiple_of(step * BLOCK, BLOCK), BLOCK)
        q_all = spread_heads(q_ref[rows, :], 0)
        raw = dot_nt(q_all, take_blocks(kv_ref, ids, 0))
        cut = jnp.concatenate(
            [jnp.where(half < BLOCK, limits[2 * t], limits[2 * t + 1]) for t in range(WIN // 2)], axis=1
        )
        inside = lax.broadcasted_iota(jnp.int32, (1, WIN * BLOCK), 1) % BLOCK
        raw = jnp.where(inside < cut, raw, NEG)
        expo = jnp.exp(raw - jnp.max(raw, axis=1, keepdims=True))
        probs = (expo * (1.0 / jnp.sum(expo, axis=1, keepdims=True))).astype(jnp.bfloat16)
        p_ref[step] = probs
        out = dot_nn(probs, take_blocks(kv_ref, ids, 128))
        ctx_ref[rows, :] = fold_heads(out, 1).astype(jnp.bfloat16)

    @pl.when(place == 0)
    def _():
        q_all = spread_heads(q_ref[0 : 2 * BLOCK, :], 0)
        chunk = WIN * BLOCK
        rows_all = q_all.shape[0]

        def scan_scores(part, top):
            at = pl.multiple_of(part * chunk, chunk)
            raw = dot_nt(q_all, kv_ref[pl.ds(at, chunk), 0:256])
            where_at = at + lax.broadcasted_iota(jnp.int32, (1, chunk), 1)
            raw = jnp.where(where_at < count, raw, NEG)
            wide_ref[part] = raw
            return jnp.maximum(top, jnp.max(raw, axis=1, keepdims=True))

        parts = SLOT_LEN // chunk
        top = lax.fori_loop(0, parts, scan_scores, jnp.full((rows_all, 1), NEG, jnp.float32))

        def scan_sum(part, total):
            expo = jnp.exp(wide_ref[part] - top)
            wide_ref[part] = expo
            return total + jnp.sum(expo, axis=1, keepdims=True)

        total = lax.fori_loop(0, parts, scan_sum, jnp.zeros((rows_all, 1), jnp.float32))
        inv = 1.0 / total

        def scan_out(part, out):
            probs = (wide_ref[part] * inv).astype(jnp.bfloat16)
            pg_ref[part] = probs
            at = pl.multiple_of(part * chunk, chunk)
            return out + dot_nn(probs, kv_ref[pl.ds(at, chunk), 128:384])

        out = lax.fori_loop(0, parts, scan_out, jnp.zeros((rows_all, 256), jnp.float32))
        ctx_ref[0 : 2 * BLOCK, :] = fold_heads(out, 1).astype(jnp.bfloat16)

    def pair(at, carry):
        one_block(2 * at)
        one_block(2 * at + 1)
        return carry

    lax.fori_loop(jnp.where(place == 0, 1, 0), local_blocks // 2, pair, 0)


def attend_forward(doc_blocks, rand, doc_mask, q_rows, kv_slot):
    tokens = q_rows.shape[0]
    blocks = tokens // BLOCK
    vmem = pl.BlockSpec(memory_space=pltpu.VMEM)
    smem = pl.BlockSpec(memory_space=pltpu.SMEM)
    return pl.pallas_call(
        attend_fwd_kernel,
        name="attend_forward",
        out_shape=(
            jax.ShapeDtypeStruct((tokens, 256), jnp.bfloat16),
            jax.ShapeDtypeStruct((blocks, 3 * BLOCK, WIN * BLOCK), jnp.bfloat16),
            jax.ShapeDtypeStruct((SLOT_LEN // (WIN * BLOCK), 6 * BLOCK, WIN * BLOCK), jnp.bfloat16),
        ),
        in_specs=[smem, smem, vmem, vmem, vmem],
        out_specs=(vmem, vmem, vmem),
        scratch_shapes=[pltpu.VMEM((SLOT_LEN // (WIN * BLOCK), 6 * BLOCK, WIN * BLOCK), jnp.float32)],
        compiler_params=pltpu.CompilerParams(vmem_limit_bytes=16 << 20),
    )(doc_blocks, rand, doc_mask, q_rows, kv_slot)


def attend_bwd_kernel(rand_ref, q_ref, kv_ref, p_ref, pg_ref, do_ref, dq_ref, dkv_ref, acc_ref):
    local_blocks = q_ref.shape[0] // BLOCK
    place, _ = slot_spot(q_ref.shape[0])
    scale = HD ** (-0.5)
    acc_ref[...] = jnp.zeros_like(acc_ref)

    def add_rows(at, size, d_key, d_value):
        where_at = pl.ds(pl.multiple_of(at, BLOCK), size)
        acc_ref[where_at, 0:128] += d_key[:, 0:128]
        acc_ref[where_at, 128:256] += d_key[:, 128:256] + d_value[:, 0:128]
        acc_ref[where_at, 256:384] += d_value[:, 128:256]

    def one_block(step):
        ids, _ = window_ids(place, 0, rand_ref, step, local_blocks)
        rows = pl.ds(pl.multiple_of(step * BLOCK, BLOCK), BLOCK)
        q_all = spread_heads(q_ref[rows, :], 0)
        do_all = spread_heads(do_ref[rows, :], 1)
        probs = p_ref[step]
        d_prob = dot_nt(do_all, take_blocks(kv_ref, ids, 128))
        wide = probs.astype(jnp.float32)
        mean = jnp.sum(d_prob * wide, axis=1, keepdims=True)
        d_score = (wide * (d_prob - mean)).astype(jnp.bfloat16)
        dq = dot_nn(d_score, take_blocks(kv_ref, ids, 0))
        dq_ref[rows, :] = (fold_heads(dq, 0) * scale).astype(jnp.bfloat16)
        d_key = dot_tn(d_score, q_all)
        d_value = dot_tn(probs, do_all)
        for slot in range(WIN):
            cut = slice(slot * BLOCK, (slot + 1) * BLOCK)
            add_rows(ids[slot] * BLOCK, BLOCK, d_key[cut], d_value[cut])

    @pl.when(place == 0)
    def _():
        chunk = WIN * BLOCK
        parts = SLOT_LEN // chunk
        q_all = spread_heads(q_ref[0 : 2 * BLOCK, :], 0)
        do_all = spread_heads(do_ref[0 : 2 * BLOCK, :], 1)

        def scan_mean(part, mean):
            at = pl.multiple_of(part * chunk, chunk)
            d_prob = dot_nt(do_all, kv_ref[pl.ds(at, chunk), 128:384])
            return mean + jnp.sum(d_prob * pg_ref[part].astype(jnp.float32), axis=1, keepdims=True)

        mean = lax.fori_loop(0, parts, scan_mean, jnp.zeros((q_all.shape[0], 1), jnp.float32))

        def scan_grad(part, dq):
            at = pl.multiple_of(part * chunk, chunk)
            probs = pg_ref[part]
            d_prob = dot_nt(do_all, kv_ref[pl.ds(at, chunk), 128:384])
            d_score = (probs.astype(jnp.float32) * (d_prob - mean)).astype(jnp.bfloat16)
            add_rows(at, chunk, dot_tn(d_score, q_all), dot_tn(probs, do_all))
            return dq + dot_nn(d_score, kv_ref[pl.ds(at, chunk), 0:256])

        dq = lax.fori_loop(0, parts, scan_grad, jnp.zeros((q_all.shape[0], 256), jnp.float32))
        dq_ref[0 : 2 * BLOCK, :] = (fold_heads(dq, 0) * scale).astype(jnp.bfloat16)

    def pair(at, carry):
        one_block(2 * at)
        one_block(2 * at + 1)
        return carry

    lax.fori_loop(jnp.where(place == 0, 1, 0), local_blocks // 2, pair, 0)
    dkv_ref[...] = acc_ref[...].astype(jnp.bfloat16)


def attend_backward(rand, q_rows, kv_slot, probs, wide_probs, d_ctx):
    tokens = q_rows.shape[0]
    vmem = pl.BlockSpec(memory_space=pltpu.VMEM)
    smem = pl.BlockSpec(memory_space=pltpu.SMEM)
    return pl.pallas_call(
        attend_bwd_kernel,
        name="attend_backward",
        out_shape=(
            jax.ShapeDtypeStruct((tokens, 256), jnp.bfloat16),
            jax.ShapeDtypeStruct((SLOT_LEN, 384), jnp.bfloat16),
        ),
        in_specs=[smem] + [vmem] * 5,
        out_specs=(vmem, vmem),
        scratch_shapes=[pltpu.VMEM((SLOT_LEN, 384), jnp.float32)],
        compiler_params=pltpu.CompilerParams(vmem_limit_bytes=16 << 20),
    )(rand, q_rows, kv_slot, probs, wide_probs, d_ctx)


MESH = pl.DeviceIdType.MESH
VM = pl.BlockSpec(memory_space=pltpu.VMEM)
LOW = jnp.bfloat16


def flip(index, bit):
    step = 1 << bit
    return index + step - 2 * step * ((index // step) % 2)


def remote(src, dst, send, recv, slot, where):
    return pltpu.make_async_remote_copy(
        src_ref=src, dst_ref=dst, send_sem=send.at[slot], recv_sem=recv.at[slot],
        device_id=where, device_id_type=MESH,
    )


def greet(partners):
    barrier = pltpu.get_barrier_semaphore()
    for where in partners:
        pl.semaphore_signal(barrier, inc=1, device_id=where, device_id_type=MESH)
    pl.semaphore_wait(barrier, len(partners))


def project_kernel(hid, qw, kw, vw, qb, vb, ow, q_out, kv_out, o_out, send, recv):
    tokens = hid.shape[0]
    half = tokens // 2
    seq, head = lax.axis_index("seq"), lax.axis_index("head")
    spans = SLOT_LEN // tokens
    place = seq % spans
    by_x, by_z = {"seq": flip(seq, 0)}, {"seq": flip(seq, 1)}
    core, far = {"head": flip(head, 0)}, {"head": flip(head, 1)}
    greet((by_x, by_z, core, far))

    mine, theirs = o_out.at[head], o_out.at[flip(head, 1)]
    o_core = remote(ow, mine, send, recv, 6, core)
    o_far = remote(ow, mine, send, recv, 7, far)
    o_relay = remote(theirs, theirs, send, recv, 8, core)
    o_far.start()
    o_core.start()
    o_out[head] = ow[...]

    def rows_of(owner, part):
        at = pl.multiple_of(owner * tokens + part * half, half)
        return kv_out.at[pl.ds(at, half)]

    def fill(part):
        rows = hid[part * half : (part + 1) * half, :]
        keys = dot_nt(rows, kw[...])
        values = dot_nt(rows, vw[...]) + vb[...][None, :]
        at = pl.multiple_of(place * tokens + part * half, half)
        kv_out[pl.ds(at, half), :] = jnp.concatenate([keys.astype(LOW), values.astype(LOW)], axis=1)

    own_a, own_b = rows_of(place, 0), rows_of(place, 1)
    fwd_a, fwd_b = rows_of(flip(place, 0), 0), rows_of(flip(place, 1), 1)
    copies = [
        remote(own_a, own_a, send, recv, 0, by_x),
        remote(own_b, own_b, send, recv, 1, by_z),
        remote(own_b, own_b, send, recv, 2, by_x),
        remote(own_a, own_a, send, recv, 3, by_z),
        remote(fwd_a, fwd_a, send, recv, 4, by_z),
        remote(fwd_b, fwd_b, send, recv, 5, by_x),
    ]
    fill(0)
    copies[0].start()
    fill(1)
    for at in (1, 2, 3):
        copies[at].start()
    for part in range(2):
        rows = hid[part * half : (part + 1) * half, :]
        query = (dot_nt(rows, qw[...]) + qb[...][None, :]).astype(LOW) * jnp.asarray(HD ** (-0.5), LOW)
        query = jnp.concatenate([query, jnp.zeros((half, 256 - query.shape[1]), LOW)], axis=1)
        q_out[part * half : (part + 1) * half, :] = query
    copies[0].wait_recv()
    copies[4].start()
    copies[1].wait_recv()
    copies[5].start()
    o_far.wait_recv()
    o_relay.start()
    for at in (2, 3, 4, 5):
        copies[at].wait_recv()
    o_core.wait_recv()
    o_relay.wait_recv()
    for copy in copies + [o_core, o_far, o_relay]:
        copy.wait_send()


def project(hid, qw, kw, vw, qb, vb, ow):
    tokens, width = hid.shape
    heads = lax.axis_size("head")
    return pl.pallas_call(
        project_kernel,
        name="project_gather",
        out_shape=(
            jax.ShapeDtypeStruct((tokens, 256), LOW),
            jax.ShapeDtypeStruct((SLOT_LEN, 2 * kw.shape[0]), LOW),
            jax.ShapeDtypeStruct((heads, ow.shape[0], width), LOW),
        ),
        in_specs=[VM] * 7,
        out_specs=(VM,) * 3,
        scratch_shapes=[pltpu.SemaphoreType.DMA((9,)), pltpu.SemaphoreType.DMA((9,))],
        compiler_params=pltpu.CompilerParams(
            collective_id=0, has_side_effects=True, vmem_limit_bytes=12 << 20
        ),
    )(hid, qw, kw, vw, qb, vb, ow)


def norm_fwd(values, gain, shift):
    centred = values - jnp.mean(values, axis=1, keepdims=True)
    inv = lax.rsqrt(jnp.mean(centred * centred, axis=1, keepdims=True) + EPS)
    unit = centred * inv
    return unit * gain + shift, unit, inv


def norm_bwd(grad, unit, inv, gain):
    scaled = grad * gain
    inner = (
        scaled
        - jnp.mean(scaled, axis=1, keepdims=True)
        - unit * jnp.mean(scaled * unit, axis=1, keepdims=True)
    )
    return inner * inv


def column_sum(values):
    return jnp.sum(values, axis=0, keepdims=True)


CHUNKS = 2
ROOT = 0.7978845608028654
CUBE = 0.044715


def middle_kernel(
    ctx, o_full, hid, o_bias, gain1, shift1, up_w, up_b, down_w, down_b, gain2, shift2, out_grad,
    layer_out, first_out, d_ctx, up_grad, down_grad, o_grad, vec,
    ctx_all, normed, unit1, inv1, second, x_all, s_all, f_all, slope, act, pre_all,
    keep, to_core, from_core, to_far, from_far, send, recv,
):
    share = out_grad.shape[0]
    rows = share // CHUNKS
    width = hid.shape[1]
    head = lax.axis_index("head")
    o_bias, gain1, shift1, up_b, down_b, gain2, shift2 = (
        ref[...][None, :] for ref in (o_bias, gain1, shift1, up_b, down_b, gain2, shift2)
    )
    core, far, both = flip(head, 0), flip(head, 1), flip(flip(head, 0), 1)
    order = (head, core, far, both)
    greet(tuple({"head": at} for at in order[1:]))
    counter = [0]

    def copy_to(src, dst, where):
        slot = counter[0]
        counter[0] += 1
        made.append(remote(src, dst, send, recv, slot, {"head": where}))
        return made[-1]

    made = []

    def own_rows(part):
        return slice(part * rows, (part + 1) * rows)

    def block_rows(owner, part):
        return pl.ds(pl.multiple_of(owner * share + part * rows, rows), rows)

    ctx_copies = []
    for part in range(CHUNKS):
        for at in (3, 2, 1):
            ctx_copies.append(
                copy_to(ctx.at[block_rows(order[at], part)], ctx_all.at[head, own_rows(part)], order[at])
            )
            ctx_copies[-1].start()
    for part in range(CHUNKS):
        ctx_all[head, own_rows(part)] = ctx[block_rows(head, part), :]

    class Gather:
        def __init__(self, buffer):
            self.buffer = buffer
            self.to_core, self.to_far, self.relay = [None] * CHUNKS, [None] * CHUNKS, [None] * CHUNKS

        def start(self, part):
            own = self.buffer.at[part, 0]
            self.to_far[part] = copy_to(own, self.buffer.at[part, 2], far)
            self.to_far[part].start()
            self.to_core[part] = copy_to(own, self.buffer.at[part, 1], core)
            self.to_core[part].start()

        def pass_on(self, part):
            self.to_far[part].wait_recv()
            self.relay[part] = copy_to(self.buffer.at[part, 2], self.buffer.at[part, 3], core)
            self.relay[part].start()

        def pair(self, part, at):
            return self.buffer[part, 2 * at : 2 * at + 2].reshape(2 * rows, width)

    class Scatter:
        def __init__(self, at):
            self.at = at
            self.near, self.through, self.away = [None] * CHUNKS, [None] * CHUNKS, [None] * CHUNKS

        def put_near(self, part, partial):
            keep[part, 0] = partial[:rows]
            to_core[self.at, part, 0] = partial[rows:].astype(LOW)
            self.near[part] = copy_to(to_core.at[self.at, part, 0], from_core.at[self.at, part, 0], core)
            self.near[part].start()

        def put_far(self, part, partial):
            to_core[self.at, part, 1] = partial[rows:].astype(LOW)
            self.through[part] = copy_to(to_core.at[self.at, part, 1], from_core.at[self.at, part, 1], core)
            self.through[part].start()
            keep[part, 1] = partial[:rows]

        def pass_on(self, part):
            self.through[part].wait_recv()
            total = keep[part, 1] + from_core[self.at, part, 1].astype(jnp.float32)
            to_far[self.at, part] = total.astype(LOW)
            self.away[part] = copy_to(to_far.at[self.at, part], from_far.at[self.at, part], far)
            self.away[part].start()

        def result(self, part):
            self.near[part].wait_recv()
            self.away[part].wait_recv()
            return (
                keep[part, 0]
                + from_core[self.at, part, 0].astype(jnp.float32)
                + from_far[self.at, part].astype(jnp.float32)
            )

    def exchange(gather, scatter, make):
        for part in range(CHUNKS):
            gather.to_core[part].wait_recv()
            scatter.put_near(part, make(part, 0))
        gather.pass_on(0)
        for part in range(CHUNKS):
            gather.relay[part].wait_recv()
            scatter.put_far(part, make(part, 1))
            if part + 1 < CHUNKS:
                gather.pass_on(part + 1)
            scatter.pass_on(part)

    x_gather, s_gather, f_gather = Gather(x_all), Gather(s_all), Gather(f_all)
    ffn_scatter, branch_scatter = Scatter(0), Scatter(1)

    for part in range(CHUNKS):
        for at in range(3):
            ctx_copies[part * 3 + at].wait_recv()
        attn = None
        for at in range(4):
            rows_at = ctx_all[at, own_rows(part)]
            weight = o_full[at]
            weight = jnp.concatenate([jnp.zeros((256 - weight.shape[0], width), LOW), weight], axis=0)
            term = dot_nn(rows_at, weight)
            attn = term if attn is None else attn + term
        token = hid[block_rows(head, part), :].astype(jnp.float32)
        normed_f, unit_f, inv_f = norm_fwd(token + attn + o_bias, gain1, shift1)
        normed[own_rows(part)] = normed_f
        unit1[own_rows(part)] = unit_f
        inv1[own_rows(part)] = inv_f
        x_all[part, 0] = normed_f.astype(LOW)
        x_gather.start(part)

    def ffn_forward(part, at):
        pre = dot_nn(x_gather.pair(part, at), up_w[...]) + up_b
        square = pre * pre
        tanh = jnp.tanh(ROOT * (pre + CUBE * square * pre))
        slope[part, at] = 0.5 * (1.0 + tanh) + (0.5 * ROOT) * pre * (1.0 - tanh * tanh) * (
            1.0 + (3.0 * CUBE) * square
        )
        acted = (0.5 * pre * (1.0 + tanh)).astype(LOW)
        act[part, at] = acted
        return dot_nn(acted, down_w[...])

    exchange(x_gather, ffn_scatter, ffn_forward)

    gain2_sum, shift2_sum, down_sum = 0.0, 0.0, 0.0
    for part in range(CHUNKS):
        total = normed[own_rows(part)] + ffn_scatter.result(part) + down_b
        out, unit_f, inv_f = norm_fwd(total, gain2, shift2)
        layer_out[own_rows(part)] = out
        grad = out_grad[own_rows(part)]
        second_f = norm_bwd(grad, unit_f, inv_f, gain2)
        second[own_rows(part)] = second_f
        s_all[part, 0] = second_f.astype(LOW)
        s_gather.start(part)
        gain2_sum += column_sum(grad * unit_f)
        shift2_sum += column_sum(grad)
        down_sum += column_sum(second_f)

    bias_sum = [0.0]

    def ffn_backward(part, at):
        pulled = dot_nt(s_gather.pair(part, at), down_w[...])
        pre_grad = (pulled * slope[part, at]).astype(LOW)
        pre_all[part, at] = pre_grad
        bias_sum[0] += column_sum(pre_grad.astype(jnp.float32))
        return dot_nt(pre_grad, up_w[...])

    exchange(s_gather, branch_scatter, ffn_backward)

    tokens = 4 * share
    step = 256

    def weight_rows(at, carry):
        cut = pl.ds(pl.multiple_of(at * step, step), step)
        down_grad[cut, :] = dot_tn(
            act[:, :, :, cut].reshape(tokens, step), s_all[...].reshape(tokens, width)
        ).astype(LOW)
        up_grad[cut, :] = dot_tn(
            x_all[:, :, :, cut].reshape(tokens, step), pre_all[...].reshape(tokens, up_w.shape[1])
        ).astype(LOW)
        return carry

    gain1_sum, shift1_sum, o_sum = 0.0, 0.0, 0.0
    for part in range(CHUNKS):
        grad = second[own_rows(part)] + branch_scatter.result(part)
        unit_f = unit1[own_rows(part)]
        first_f = norm_bwd(grad, unit_f, inv1[own_rows(part)], gain1)
        first_out[own_rows(part)] = first_f
        f_all[part, 0] = first_f.astype(LOW)
        f_gather.start(part)
        gain1_sum += column_sum(grad * unit_f)
        shift1_sum += column_sum(grad)
        o_sum += column_sum(first_f)
    lax.fori_loop(0, width // step, weight_rows, 0)

    weight = o_full[head]
    weight = jnp.concatenate([jnp.zeros((256 - weight.shape[0], width), LOW), weight], axis=0)
    o_total = None

    def back(part, at):
        rows_f = f_gather.pair(part, at)
        grad = dot_nt(rows_f, weight).astype(LOW)
        term = None
        first_ctx = ctx[block_rows(order[2 * at], part), :]
        second_ctx = ctx[block_rows(order[2 * at + 1], part), :]
        d_ctx[block_rows(order[2 * at], part), :] = grad[:rows]
        d_ctx[block_rows(order[2 * at + 1], part), :] = grad[rows:]
        return dot_tn(jnp.concatenate([first_ctx, second_ctx], axis=0), rows_f)

    o_total = 0.0
    for part in range(CHUNKS):
        f_gather.to_core[part].wait_recv()
        o_total += back(part, 0)
    for part in range(CHUNKS):
        f_gather.pass_on(part)
    for part in range(CHUNKS):
        f_gather.relay[part].wait_recv()
        o_total += back(part, 1)
    o_grad[...] = o_total[256 - o_grad.shape[0] :].astype(LOW)
    zero = jnp.zeros((1, width), jnp.float32)
    vec[...] = jnp.concatenate(
        [o_sum, gain1_sum, shift1_sum, down_sum, gain2_sum, shift2_sum, bias_sum[0], zero], axis=0
    )
    for copy in made:
        copy.wait_send()


def middle(ctx, o_full, hid, o_bias, gain1, shift1, up_w, up_b, down_w, down_b, gain2, shift2, out_grad):
    tokens, width = hid.shape
    share = out_grad.shape[0]
    rows = share // CHUNKS
    hidden, local = up_w.shape[1], o_full.shape[1]
    f32 = jnp.float32
    gathered = pltpu.VMEM((CHUNKS, 4, rows, width), LOW)
    copies = CHUNKS * (3 + 3 * 3 + 2 * 3)
    return pl.pallas_call(
        middle_kernel,
        name="middle",
        out_shape=(
            jax.ShapeDtypeStruct((share, width), f32),
            jax.ShapeDtypeStruct((share, width), f32),
            jax.ShapeDtypeStruct((tokens, 256), LOW),
            jax.ShapeDtypeStruct((width, hidden), LOW),
            jax.ShapeDtypeStruct((hidden, width), LOW),
            jax.ShapeDtypeStruct((local, width), LOW),
            jax.ShapeDtypeStruct((8, width), f32),
        ),
        in_specs=[VM] * 13,
        out_specs=(VM,) * 7,
        scratch_shapes=[
            pltpu.VMEM((4, share, 256), LOW),
            pltpu.VMEM((share, width), f32),
            pltpu.VMEM((share, width), f32),
            pltpu.VMEM((share, 1), f32),
            pltpu.VMEM((share, width), f32),
            gathered,
            gathered,
            gathered,
            pltpu.VMEM((CHUNKS, 2, 2 * rows, hidden), f32),
            pltpu.VMEM((CHUNKS, 2, 2 * rows, hidden), LOW),
            pltpu.VMEM((CHUNKS, 2, 2 * rows, hidden), LOW),
            pltpu.VMEM((CHUNKS, 2, rows, width), f32),
            pltpu.VMEM((2, CHUNKS, 2, rows, width), LOW),
            pltpu.VMEM((2, CHUNKS, 2, rows, width), LOW),
            pltpu.VMEM((2, CHUNKS, rows, width), LOW),
            pltpu.VMEM((2, CHUNKS, rows, width), LOW),
            pltpu.SemaphoreType.DMA((copies,)),
            pltpu.SemaphoreType.DMA((copies,)),
        ],
        compiler_params=pltpu.CompilerParams(
            collective_id=1, has_side_effects=True, vmem_limit_bytes=30 << 20
        ),
    )(
        ctx, o_full, hid, o_bias, gain1, shift1, up_w, up_b, down_w, down_b, gain2, shift2, out_grad
    )


def tail_kernel(
    hid, dq, dkv, qw, kw, vw, first, up_grad, down_grad, o_grad, vec,
    in_grad, big_out, small_out, vec_out,
    pair_in, pair_out, partial, small, big_ring, small_ring, near_out, near_in, far_out, far_in,
    vec_now, vec_send, vec_recv, send, recv, ring_send, ring_recv,
):
    n = lax.axis_size("seq")
    tokens, width = hid.shape
    half, share = tokens // 2, first.shape[0]
    depths = (big_ring.shape[2], small_ring.shape[2])
    spans = SLOT_LEN // tokens
    seq, head = lax.axis_index("seq"), lax.axis_index("head")
    place = seq % spans
    f32 = jnp.float32
    side, along = seq % 2, seq // 2
    spot = along + side * (n - 1 - 2 * along)

    def member(pos):
        turn = pos // (n // 2)
        return 2 * (pos + turn * (n - 1 - 2 * pos)) + turn

    ways = ({"seq": member((spot + 1) % n)}, {"seq": member((spot + n - 1) % n)})
    signs = (-1, 1)
    by_x, by_z = {"seq": flip(seq, 0)}, {"seq": flip(seq, 1)}
    core, far = flip(head, 0), flip(head, 1)
    both = flip(core, 1)
    seq_bits = n.bit_length() - 1
    vec_peers = [{"seq": flip(seq, bit)} for bit in range(seq_bits)] + [{"head": core}, {"head": far}]
    greet((by_x, by_z, *ways, *vec_peers))

    def rows_of(owner, part):
        return pl.ds(pl.multiple_of(owner * tokens + part * half, half), half)

    x_at, z_at = flip(place, 0), flip(place, 1)
    d_at = flip(x_at, 1)
    copies = [
        remote(dkv.at[rows_of(d_at, 0)], pair_in.at[0], send, recv, 0, by_z),
        remote(dkv.at[rows_of(d_at, 1)], pair_in.at[1], send, recv, 1, by_x),
        remote(dkv.at[rows_of(x_at, 1)], pair_in.at[2], send, recv, 2, by_x),
        remote(dkv.at[rows_of(z_at, 0)], pair_in.at[3], send, recv, 3, by_z),
        remote(pair_out.at[0], pair_in.at[4], send, recv, 4, by_x),
        remote(pair_out.at[1], pair_in.at[5], send, recv, 5, by_z),
    ]
    for at in range(4):
        copies[at].start()

    local = qw.shape[0]
    gap = jnp.zeros((256 - local, width), LOW)
    partial[...] = dot_nn(dq[...], jnp.concatenate([qw[...], gap], axis=0))
    copies[0].wait_recv()
    pair_out[0] = (dkv[rows_of(x_at, 0), :].astype(f32) + pair_in[0].astype(f32)).astype(LOW)
    copies[4].start()
    copies[1].wait_recv()
    pair_out[1] = (dkv[rows_of(z_at, 1), :].astype(f32) + pair_in[1].astype(f32)).astype(LOW)
    copies[5].start()

    rings = ((big_ring, big_out, (up_grad, down_grad)), (small_ring, small_out, (small.at[0], small.at[1])))

    def chunk(kind, pos):
        return pl.ds(pl.multiple_of(((pos + 2 * n) % n) * depths[kind], 16), depths[kind])

    def reduce_copy(kind, way, step):
        ring = rings[kind][0]
        return pltpu.make_async_remote_copy(
            src_ref=ring.at[way, step], dst_ref=ring.at[way, step + 1],
            send_sem=ring_send.at[0, kind, way, step], recv_sem=ring_recv.at[0, kind, way, step],
            device_id=ways[way], device_id_type=MESH,
        )

    def spread_copy(kind, way, step):
        rows = rings[kind][1].at[way, chunk(kind, spot + signs[way] * (step - 1))]
        return pltpu.make_async_remote_copy(
            src_ref=rows, dst_ref=rows,
            send_sem=ring_send.at[1, kind, way, step], recv_sem=ring_recv.at[1, kind, way, step],
            device_id=ways[way], device_id_type=MESH,
        )

    def open_ring(kind):
        ring, _, source = rings[kind]
        for way in range(2):
            ring[way, 0] = source[way][chunk(kind, spot), :]
            reduce_copy(kind, way, 0).start()

    def add_ring(kind, way, step):
        ring, _, source = rings[kind]
        reduce_copy(kind, way, step).wait_recv()
        mine = source[way][chunk(kind, spot + signs[way] * (step + 1)), :]
        ring[way, step + 1] = (ring[way, step + 1].astype(f32) + mine.astype(f32)).astype(LOW)

    open_ring(0)
    small[1, 0:local] = dot_tn(dq[...], hid[...])[0:local].astype(LOW)
    small[1, local : 2 * local] = o_grad[...]
    spare = small.shape[1] - 2 * local
    if spare:
        small[:, 2 * local :] = jnp.zeros((2, spare, width), LOW)
    for at in range(2, 6):
        copies[at].wait_recv()
    own = []
    for part in range(2):
        mine = dkv[rows_of(place, part), :].astype(f32)
        first_in, second_in = (3, 4) if part == 0 else (2, 5)
        own.append((mine + pair_in[first_in].astype(f32) + pair_in[second_in].astype(f32)).astype(LOW))
    own = jnp.concatenate(own, axis=0)
    small[0, 0 : 2 * local] = dot_tn(own, hid[...]).astype(LOW)
    open_ring(1)
    partial[...] += dot_nn(own[:, 0:256], jnp.concatenate([kw[...], gap], axis=0)) + dot_nn(
        own[:, 128:384], jnp.concatenate([gap, vw[...]], axis=0)
    )

    def share_rows(owner):
        return partial[pl.ds(pl.multiple_of(owner * share, share), share), :]

    near_out[0] = share_rows(both).astype(LOW)
    near_out[1] = share_rows(core).astype(LOW)
    near = [remote(near_out.at[at], near_in.at[at], send, recv, 6 + at, {"head": core}) for at in range(2)]
    near[0].start()
    near[1].start()
    sums = jnp.concatenate(
        [
            jnp.concatenate(
                [column_sum(dq[...].astype(f32)), jnp.zeros((1, width - dq.shape[1]), f32)], axis=1
            ),
            jnp.concatenate(
                [column_sum(own.astype(f32)), jnp.zeros((1, width - own.shape[1]), f32)], axis=1
            ),
            jnp.zeros((6, width), f32),
        ],
        axis=0,
    )
    vec_now[0:8] = vec[...]
    vec_now[8:16] = sums
    far_copy = remote(far_out, far_in, send, recv, 8, {"head": far})

    def vec_copy(at):
        return remote(vec_send.at[at], vec_recv.at[at], send, recv, 9 + at, vec_peers[at])

    def ring_step(step):
        for kind in range(2):
            for way in range(2):
                add_ring(kind, way, step)
                reduce_copy(kind, way, step + 1).start()

    steps = seq_bits + 2
    for at in range(steps):
        vec_send[at] = vec_now[...]
        vec_copy(at).start()
        if at < n - 2:
            ring_step(at)
        if at == 0:
            near[0].wait_recv()
            far_out[...] = (share_rows(far) + near_in[0].astype(f32)).astype(LOW)
            far_copy.start()
        vec_copy(at).wait_recv()
        if at == seq_bits - 1:
            total = vec_now[...] + vec_recv[at]
            vec_now[...] = total
            vec_out[8:16] = total[8:16]
            vec_out[16:24] = total[0:8]
        else:
            vec_now[...] += vec_recv[at]
    vec_out[0:8] = vec_now[0:8]

    def ring_body(step, carry):
        ring_step(step)
        return carry

    lax.fori_loop(min(steps, n - 2), n - 2, ring_body, 0)
    for kind in range(2):
        ring, out, _ = rings[kind]
        for way in range(2):
            add_ring(kind, way, n - 2)
            out[way, chunk(kind, spot - signs[way])] = ring[way, n - 1]
            spread_copy(kind, way, 0).start()
    near[1].wait_recv()
    far_copy.wait_recv()
    in_grad[...] = first[...] + share_rows(head) + near_in[1].astype(f32) + far_in[...].astype(f32)

    def spread_body(step, carry):
        for kind in range(2):
            for way in range(2):
                spread_copy(kind, way, step).wait_recv()
                spread_copy(kind, way, step + 1).start()
        return carry

    lax.fori_loop(0, n - 2, spread_body, 0)
    for kind in range(2):
        for way in range(2):
            spread_copy(kind, way, n - 2).wait_recv()

    def close_body(step, carry):
        for kind in range(2):
            for way in range(2):
                reduce_copy(kind, way, step).wait_send()
                spread_copy(kind, way, step).wait_send()
        return carry

    lax.fori_loop(0, n - 1, close_body, 0)
    for copy in copies + near + [far_copy] + [vec_copy(at) for at in range(steps)]:
        copy.wait_send()


def tail(hid, dq, dkv, qw, kw, vw, first, up_grad, down_grad, o_grad, vec):
    n = lax.axis_size("seq")
    tokens, width = hid.shape
    share = first.shape[0]
    pair = dkv.shape[1]
    depth, less = 16 * (-(-width // (16 * n))), 16 * (-(-pair // (16 * n)))
    rows = n * depth
    f32 = jnp.float32
    if rows > width:
        up_grad = jnp.pad(up_grad, ((0, rows - width), (0, 0)))
        down_grad = jnp.pad(down_grad, ((0, rows - width), (0, 0)))
    steps = n.bit_length() + 1
    return pl.pallas_call(
        tail_kernel,
        name="tail",
        out_shape=(
            jax.ShapeDtypeStruct((share, width), f32),
            jax.ShapeDtypeStruct((2, rows, up_grad.shape[1]), LOW),
            jax.ShapeDtypeStruct((2, n * less, width), LOW),
            jax.ShapeDtypeStruct((24, width), f32),
        ),
        in_specs=[VM] * 11,
        out_specs=(VM,) * 4,
        scratch_shapes=[
            pltpu.VMEM((6, tokens // 2, pair), LOW),
            pltpu.VMEM((2, tokens // 2, pair), LOW),
            pltpu.VMEM((tokens, width), f32),
            pltpu.VMEM((2, n * less, width), LOW),
            pltpu.VMEM((2, n, depth, up_grad.shape[1]), LOW),
            pltpu.VMEM((2, n, less, width), LOW),
            pltpu.VMEM((2, share, width), LOW),
            pltpu.VMEM((2, share, width), LOW),
            pltpu.VMEM((share, width), LOW),
            pltpu.VMEM((share, width), LOW),
            pltpu.VMEM((16, width), f32),
            pltpu.VMEM((steps, 16, width), f32),
            pltpu.VMEM((steps, 16, width), f32),
            pltpu.SemaphoreType.DMA((9 + steps,)),
            pltpu.SemaphoreType.DMA((9 + steps,)),
            pltpu.SemaphoreType.DMA((2, 2, 2, n - 1)),
            pltpu.SemaphoreType.DMA((2, 2, 2, n - 1)),
        ],
        compiler_params=pltpu.CompilerParams(
            collective_id=2, has_side_effects=True, vmem_limit_bytes=28 << 20
        ),
    )(hid, dq, dkv, qw, kw, vw, first, up_grad, down_grad, o_grad, vec)


def per_device(
    hidden_in, q_weight, q_bias, k_weight, v_weight, v_bias, o_weight, o_bias, norm1_gain, norm1_shift,
    up_weight, up_bias, down_weight, down_bias, norm2_gain, norm2_shift, doc_mask, doc_blocks, rand_blocks,
    out_grad,
):
    f32 = jnp.float32
    tokens, width = hidden_in.shape
    local = q_weight.shape[1]
    rand = rand_blocks.T
    qw, kw, vw = q_weight.T, k_weight.T, v_weight.T
    query, slot_pair, o_full = project(hidden_in, qw, kw, vw, q_bias, v_bias, o_weight)
    context, probs, wide_probs = attend_forward(
        doc_blocks, rand, doc_mask.reshape(-1, 128), query, slot_pair
    )
    layer_out, first, d_ctx, up_part, down_part, o_part, vec = middle(
        context, o_full, hidden_in, o_bias, norm1_gain, norm1_shift, up_weight, up_bias, down_weight,
        down_bias, norm2_gain, norm2_shift, out_grad,
    )
    dq, dkv = attend_backward(rand, query, slot_pair, probs, wide_probs, d_ctx)
    in_grad, big, small, vecs = tail(
        hidden_in, dq, dkv, qw, kw, vw, first, up_part, down_part, o_part, vec
    )
    small = small.astype(f32)
    return (
        layer_out, in_grad, small[1, :local].T, vecs[8, :local], small[0, :local].T,
        small[0, local : 2 * local].T, vecs[9, local : 2 * local], small[1, local : 2 * local],
        vecs[0], vecs[1], vecs[2], big[0, :width].astype(f32), vecs[22], big[1, :width].astype(f32),
        vecs[3], vecs[4], vecs[5],
    )


def solution(mesh):
    columns, vector, rows, whole = P(None, "head"), P("head"), P("head", None), P()
    tokens, shares = P("seq", None), P(("seq", "head"), None)
    in_specs = (
        tokens, columns, vector, columns, columns, vector, rows, whole, whole, whole, columns, vector, rows,
        whole, whole, whole, whole, whole, tokens, shares,
    )
    out_specs = (
        shares, shares, columns, vector, columns, columns, vector, rows, whole, whole, whole, columns, vector,
        rows, whole, whole, whole,
    )
    return jax.shard_map(per_device, mesh=mesh, in_specs=in_specs, out_specs=out_specs, check_vma=False)
```

```python
import jax
import jax.numpy as jnp
from jax import lax
from jax.experimental import pallas as pl
from jax.experimental.pallas import tpu as pltpu
from jax.sharding import PartitionSpec as P

HD = 64
BLOCK = 64
SLOT_LEN = 4096
NEG = -1e30
EPS = 1e-12
WIN = 8


def dot_nt(left, right):
    return lax.dot_general(left, right, (((1,), (1,)), ((), ())), preferred_element_type=jnp.float32)


def dot_tn(left, right):
    return lax.dot_general(left, right, (((0,), (0,)), ((), ())), preferred_element_type=jnp.float32)


def dot_nn(left, right):
    return jnp.dot(left, right, preferred_element_type=jnp.float32)


def head_pick(rows, first):
    lane = lax.broadcasted_iota(jnp.int32, (1, rows.shape[1]), 1) // HD
    return [jnp.where(lane == first + head, rows, jnp.zeros_like(rows)) for head in range(3)]


def spread_heads(rows, first):
    return jnp.concatenate(head_pick(rows, first), axis=0)


def fold_heads(stacked, first):
    size = stacked.shape[0] // 3
    lane = lax.broadcasted_iota(jnp.int32, (1, stacked.shape[1]), 1) // HD
    total = None
    for head in range(3):
        part = jnp.where(lane == first + head, stacked[head * size : (head + 1) * size], 0.0)
        total = part if total is None else total + part
    return total


def slot_spot(tokens):
    spans = SLOT_LEN // tokens
    seq = lax.axis_index("seq")
    return seq % spans, seq // spans


def window_ids(place, count, rand_ref, step, local_blocks):
    mine = place * local_blocks + step
    last = SLOT_LEN // BLOCK - 1
    ids, limits = [], []
    for shift in (-1, 0, 1):
        near = mine + shift
        good = (near >= 2) & (near <= last)
        at = jnp.clip(near, 0, last)
        ids.append(at)
        limits.append(jnp.where(good, jnp.clip(count - at * BLOCK, 0, BLOCK), 0))
    for slot in range(3):
        at = rand_ref[slot, step]
        ids.append(at)
        limits.append(jnp.clip(count - at * BLOCK, 0, BLOCK))
    for at in (0, 1):
        ids.append(jnp.int32(at))
        limits.append(jnp.clip(count - at * BLOCK, 0, BLOCK))
    return ids, limits


def take_blocks(ref, ids, low):
    parts = [ref[pl.ds(pl.multiple_of(at * BLOCK, BLOCK), BLOCK), low : low + 256] for at in ids]
    return jnp.concatenate(parts, axis=0)


def attend_fwd_kernel(blocks_ref, rand_ref, mask_ref, q_ref, kv_ref, ctx_ref, p_ref, pg_ref, wide_ctx_ref, link_ref, wide_ref):
    local_blocks = q_ref.shape[0] // BLOCK
    place, slot = slot_spot(q_ref.shape[0])
    lines = SLOT_LEN // mask_ref.shape[1]
    marked = jnp.sum(mask_ref[pl.ds(pl.multiple_of(slot * lines, lines), lines), :])
    count = jnp.minimum(marked, blocks_ref[slot] * BLOCK)
    half = lax.broadcasted_iota(jnp.int32, (1, 128), 1)
    slot_blocks = SLOT_LEN // BLOCK
    for at in range(slot_blocks + 3 * local_blocks):
        link_ref[at] = 3 * local_blocks

    def one_block(step):
        for slot in range(3):
            owner = rand_ref[slot, step]
            link_ref[slot_blocks + step * 3 + slot] = link_ref[owner]
            link_ref[owner] = step * 3 + slot
        ids, limits = window_ids(place, count, rand_ref, step, local_blocks)
        rows = pl.ds(pl.multiple_of(step * BLOCK, BLOCK), BLOCK)
        q_all = spread_heads(q_ref[rows, :], 0)
        raw = dot_nt(q_all, take_blocks(kv_ref, ids, 0))
        cut = jnp.concatenate(
            [jnp.where(half < BLOCK, limits[2 * t], limits[2 * t + 1]) for t in range(WIN // 2)], axis=1
        )
        inside = lax.broadcasted_iota(jnp.int32, (1, WIN * BLOCK), 1) % BLOCK
        raw = jnp.where(inside < cut, raw, NEG)
        expo = jnp.exp(raw - jnp.max(raw, axis=1, keepdims=True))
        probs = (expo * (1.0 / jnp.sum(expo, axis=1, keepdims=True))).astype(jnp.bfloat16)
        p_ref[step] = probs
        out = dot_nn(probs, take_blocks(kv_ref, ids, 128))
        ctx_ref[rows, :] = fold_heads(out, 1).astype(jnp.bfloat16)

    @pl.when(place == 0)
    def _():
        q_all = spread_heads(q_ref[0 : 2 * BLOCK, :], 0)
        chunk = WIN * BLOCK
        rows_all = q_all.shape[0]

        def scan_scores(part, top):
            at = pl.multiple_of(part * chunk, chunk)
            raw = dot_nt(q_all, kv_ref[pl.ds(at, chunk), 0:256])
            where_at = at + lax.broadcasted_iota(jnp.int32, (1, chunk), 1)
            raw = jnp.where(where_at < count, raw, NEG)
            wide_ref[part] = raw
            return jnp.maximum(top, jnp.max(raw, axis=1, keepdims=True))

        parts = SLOT_LEN // chunk
        top = lax.fori_loop(0, parts, scan_scores, jnp.full((rows_all, 1), NEG, jnp.float32))

        def scan_sum(part, total):
            expo = jnp.exp(wide_ref[part] - top)
            wide_ref[part] = expo
            return total + jnp.sum(expo, axis=1, keepdims=True)

        total = lax.fori_loop(0, parts, scan_sum, jnp.zeros((rows_all, 1), jnp.float32))
        inv = 1.0 / total

        def scan_out(part, out):
            probs = (wide_ref[part] * inv).astype(jnp.bfloat16)
            pg_ref[part] = probs
            at = pl.multiple_of(part * chunk, chunk)
            return out + dot_nn(probs, kv_ref[pl.ds(at, chunk), 128:384])

        out = lax.fori_loop(0, parts, scan_out, jnp.zeros((rows_all, 256), jnp.float32))
        folded = fold_heads(out, 1)
        wide_ctx_ref[...] = folded
        ctx_ref[0 : 2 * BLOCK, :] = folded.astype(jnp.bfloat16)

    @pl.when(place != 0)
    def _():
        wide_ctx_ref[...] = jnp.zeros_like(wide_ctx_ref)

    def pair(at, carry):
        one_block(2 * at)
        one_block(2 * at + 1)
        return carry

    lax.fori_loop(jnp.where(place == 0, 1, 0), local_blocks // 2, pair, 0)


def attend_forward(doc_blocks, rand, doc_mask, q_rows, kv_slot):
    tokens = q_rows.shape[0]
    blocks = tokens // BLOCK
    vmem = pl.BlockSpec(memory_space=pltpu.VMEM)
    smem = pl.BlockSpec(memory_space=pltpu.SMEM)
    return pl.pallas_call(
        attend_fwd_kernel,
        name="attend_forward",
        out_shape=(
            jax.ShapeDtypeStruct((tokens, 256), jnp.bfloat16),
            jax.ShapeDtypeStruct((blocks, 3 * BLOCK, WIN * BLOCK), jnp.bfloat16),
            jax.ShapeDtypeStruct((SLOT_LEN // (WIN * BLOCK), 6 * BLOCK, WIN * BLOCK), jnp.bfloat16),
            jax.ShapeDtypeStruct((2 * BLOCK, 256), jnp.float32),
            jax.ShapeDtypeStruct((SLOT_LEN // BLOCK + 3 * blocks,), jnp.int32),
        ),
        in_specs=[smem, smem, vmem, vmem, vmem],
        out_specs=(vmem,) * 4 + (smem,),
        scratch_shapes=[pltpu.VMEM((SLOT_LEN // (WIN * BLOCK), 6 * BLOCK, WIN * BLOCK), jnp.float32)],
        compiler_params=pltpu.CompilerParams(vmem_limit_bytes=16 << 20),
    )(doc_blocks, rand, doc_mask, q_rows, kv_slot)


MESH = pl.DeviceIdType.MESH
VM = pl.BlockSpec(memory_space=pltpu.VMEM)
LOW = jnp.bfloat16


def flip(index, bit):
    step = 1 << bit
    return index + step - 2 * step * ((index // step) % 2)


def remote(src, dst, send, recv, slot, where):
    return pltpu.make_async_remote_copy(
        src_ref=src, dst_ref=dst, send_sem=send.at[slot], recv_sem=recv.at[slot],
        device_id=where, device_id_type=MESH,
    )


def greet(partners):
    barrier = pltpu.get_barrier_semaphore()
    for where in partners:
        pl.semaphore_signal(barrier, inc=1, device_id=where, device_id_type=MESH)
    pl.semaphore_wait(barrier, len(partners))


def project_kernel(hid, weights, biases, q_out, kv_out, o_out, send, recv):
    tokens = hid.shape[0]
    half = tokens // 2
    local = weights.shape[0] // 4
    qw, kw, vw, ow = (weights.at[pl.ds(at * local, local)] for at in range(4))
    seq, head = lax.axis_index("seq"), lax.axis_index("head")
    spans = SLOT_LEN // tokens
    place = seq % spans
    by_x, by_z = {"seq": flip(seq, 0)}, {"seq": flip(seq, 1)}
    core, far = {"head": flip(head, 0)}, {"head": flip(head, 1)}
    greet((by_x, by_z, core, far))

    mine, theirs = o_out.at[head], o_out.at[flip(head, 1)]
    o_core = remote(ow, mine, send, recv, 6, core)
    o_far = remote(ow, mine, send, recv, 7, far)
    o_relay = remote(theirs, theirs, send, recv, 8, core)
    o_far.start()
    o_core.start()
    o_out[head] = ow[...]

    def rows_of(owner, part):
        at = pl.multiple_of(owner * tokens + part * half, half)
        return kv_out.at[pl.ds(at, half)]

    def fill(part):
        rows = hid[part * half : (part + 1) * half, :]
        keys = dot_nt(rows, kw[...])
        values = dot_nt(rows, vw[...]) + biases[1:2, :]
        at = pl.multiple_of(place * tokens + part * half, half)
        kv_out[pl.ds(at, half), :] = jnp.concatenate([keys.astype(LOW), values.astype(LOW)], axis=1)

    own_a, own_b = rows_of(place, 0), rows_of(place, 1)
    fwd_a, fwd_b = rows_of(flip(place, 0), 0), rows_of(flip(place, 1), 1)
    copies = [
        remote(own_a, own_a, send, recv, 0, by_x),
        remote(own_b, own_b, send, recv, 1, by_z),
        remote(own_b, own_b, send, recv, 2, by_x),
        remote(own_a, own_a, send, recv, 3, by_z),
        remote(fwd_a, fwd_a, send, recv, 4, by_z),
        remote(fwd_b, fwd_b, send, recv, 5, by_x),
    ]
    fill(0)
    copies[0].start()
    fill(1)
    for at in (1, 2, 3):
        copies[at].start()
    for part in range(2):
        rows = hid[part * half : (part + 1) * half, :]
        query = (dot_nt(rows, qw[...]) + biases[0:1, :]).astype(LOW) * jnp.asarray(HD ** (-0.5), LOW)
        query = jnp.concatenate([query, jnp.zeros((half, 256 - query.shape[1]), LOW)], axis=1)
        q_out[part * half : (part + 1) * half, :] = query
    copies[0].wait_recv()
    copies[4].start()
    copies[1].wait_recv()
    copies[5].start()
    o_far.wait_recv()
    o_relay.start()
    for at in (2, 3, 4, 5):
        copies[at].wait_recv()
    o_core.wait_recv()
    o_relay.wait_recv()
    for copy in copies + [o_core, o_far, o_relay]:
        copy.wait_send()


def project(hid, weights, biases):
    tokens, width = hid.shape
    heads, local = lax.axis_size("head"), weights.shape[0] // 4
    return pl.pallas_call(
        project_kernel,
        name="project_gather",
        out_shape=(
            jax.ShapeDtypeStruct((tokens, 256), LOW),
            jax.ShapeDtypeStruct((SLOT_LEN, 2 * local), LOW),
            jax.ShapeDtypeStruct((heads, local, width), LOW),
        ),
        in_specs=[VM] * 3,
        out_specs=(VM,) * 3,
        scratch_shapes=[pltpu.SemaphoreType.DMA((9,)), pltpu.SemaphoreType.DMA((9,))],
        compiler_params=pltpu.CompilerParams(
            collective_id=0, has_side_effects=True, vmem_limit_bytes=12 << 20
        ),
    )(hid, weights, biases)


def norm_fwd(values, gain, shift):
    centred = values - jnp.mean(values, axis=1, keepdims=True)
    inv = lax.rsqrt(jnp.mean(centred * centred, axis=1, keepdims=True) + EPS)
    unit = centred * inv
    return unit * gain + shift, unit, inv


def norm_bwd(grad, unit, inv, gain):
    scaled = grad * gain
    inner = (
        scaled
        - jnp.mean(scaled, axis=1, keepdims=True)
        - unit * jnp.mean(scaled * unit, axis=1, keepdims=True)
    )
    return inner * inv


def column_sum(values):
    return jnp.sum(values, axis=0, keepdims=True)


CHUNKS = 4
ROOT = 0.7978845608028654
CUBE = 0.044715


def middle_kernel(
    ctx, o_full, hid, o_bias, gain1, shift1, up_w, up_b, down_w, down_b, gain2, shift2, out_grad,
    layer_out, first_out, d_ctx, up_grad, down_grad, o_grad, vec,
    ctx_all, normed, unit1, inv1, second, x_all, s_all, f_all, slope, act, pre_all,
    keep, to_core, from_core, to_far, from_far, send, recv,
):
    share = out_grad.shape[0]
    rows = share // CHUNKS
    width = hid.shape[1]
    head = lax.axis_index("head")
    o_bias, gain1, shift1, up_b, down_b, gain2, shift2 = (
        ref[...][None, :] for ref in (o_bias, gain1, shift1, up_b, down_b, gain2, shift2)
    )
    core, far, both = flip(head, 0), flip(head, 1), flip(flip(head, 0), 1)
    order = (head, core, far, both)
    greet(tuple({"head": at} for at in order[1:]))
    counter = [0]

    def copy_to(src, dst, where):
        slot = counter[0]
        counter[0] += 1
        made.append(remote(src, dst, send, recv, slot, {"head": where}))
        return made[-1]

    made = []

    def own_rows(part):
        return slice(part * rows, (part + 1) * rows)

    def block_rows(owner, part):
        return pl.ds(pl.multiple_of(owner * share + part * rows, rows), rows)

    ctx_copies = []
    for part in range(CHUNKS):
        for at in (3, 2, 1):
            ctx_copies.append(
                copy_to(ctx.at[block_rows(order[at], part)], ctx_all.at[head, own_rows(part)], order[at])
            )
            ctx_copies[-1].start()
    for part in range(CHUNKS):
        ctx_all[head, own_rows(part)] = ctx[block_rows(head, part), :]

    class Gather:
        def __init__(self, buffer):
            self.buffer = buffer
            self.to_core, self.to_far, self.relay = [None] * CHUNKS, [None] * CHUNKS, [None] * CHUNKS

        def start(self, part):
            own = self.buffer.at[part, 0]
            self.to_far[part] = copy_to(own, self.buffer.at[part, 2], far)
            self.to_far[part].start()
            self.to_core[part] = copy_to(own, self.buffer.at[part, 1], core)
            self.to_core[part].start()

        def pass_on(self, part):
            self.to_far[part].wait_recv()
            self.relay[part] = copy_to(self.buffer.at[part, 2], self.buffer.at[part, 3], core)
            self.relay[part].start()

        def pair(self, part, at):
            return self.buffer[part, 2 * at : 2 * at + 2].reshape(2 * rows, width)

    class Scatter:
        def __init__(self, at):
            self.at = at
            self.near, self.through, self.away = [None] * CHUNKS, [None] * CHUNKS, [None] * CHUNKS

        def put_near(self, part, partial):
            keep[part, 0] = partial[:rows]
            to_core[self.at, part, 0] = partial[rows:].astype(LOW)
            self.near[part] = copy_to(to_core.at[self.at, part, 0], from_core.at[self.at, part, 0], core)
            self.near[part].start()

        def put_far(self, part, partial):
            to_core[self.at, part, 1] = partial[rows:].astype(LOW)
            self.through[part] = copy_to(to_core.at[self.at, part, 1], from_core.at[self.at, part, 1], core)
            self.through[part].start()
            keep[part, 1] = partial[:rows]

        def pass_on(self, part):
            self.through[part].wait_recv()
            total = keep[part, 1] + from_core[self.at, part, 1].astype(jnp.float32)
            to_far[self.at, part] = total.astype(LOW)
            self.away[part] = copy_to(to_far.at[self.at, part], from_far.at[self.at, part], far)
            self.away[part].start()

        def result(self, part):
            self.near[part].wait_recv()
            self.away[part].wait_recv()
            return (
                keep[part, 0]
                + from_core[self.at, part, 0].astype(jnp.float32)
                + from_far[self.at, part].astype(jnp.float32)
            )

    def exchange(gather, scatter, make):
        for part in range(CHUNKS):
            gather.to_core[part].wait_recv()
            scatter.put_near(part, make(part, 0))
        gather.pass_on(0)
        for part in range(CHUNKS):
            gather.relay[part].wait_recv()
            scatter.put_far(part, make(part, 1))
            if part + 1 < CHUNKS:
                gather.pass_on(part + 1)
            scatter.pass_on(part)

    x_gather, s_gather, f_gather = Gather(x_all), Gather(s_all), Gather(f_all)
    ffn_scatter, branch_scatter = Scatter(0), Scatter(1)

    for part in range(CHUNKS):
        for at in range(3):
            ctx_copies[part * 3 + at].wait_recv()
        attn = None
        for at in range(4):
            rows_at = ctx_all[at, own_rows(part)]
            weight = o_full[at]
            weight = jnp.concatenate([jnp.zeros((256 - weight.shape[0], width), LOW), weight], axis=0)
            term = dot_nn(rows_at, weight)
            attn = term if attn is None else attn + term
        token = hid[block_rows(head, part), :].astype(jnp.float32)
        normed_f, unit_f, inv_f = norm_fwd(token + attn + o_bias, gain1, shift1)
        normed[own_rows(part)] = normed_f
        unit1[own_rows(part)] = unit_f
        inv1[own_rows(part)] = inv_f
        x_all[part, 0] = normed_f.astype(LOW)
        x_gather.start(part)

    def ffn_forward(part, at):
        pre = dot_nn(x_gather.pair(part, at), up_w[...]) + up_b
        square = pre * pre
        tanh = jnp.tanh(ROOT * (pre + CUBE * square * pre))
        slope[part, at] = 0.5 * (1.0 + tanh) + (0.5 * ROOT) * pre * (1.0 - tanh * tanh) * (
            1.0 + (3.0 * CUBE) * square
        )
        acted = (0.5 * pre * (1.0 + tanh)).astype(LOW)
        act[part, at] = acted
        return dot_nn(acted, down_w[...])

    exchange(x_gather, ffn_scatter, ffn_forward)

    gain2_sum, shift2_sum, down_sum = 0.0, 0.0, 0.0
    for part in range(CHUNKS):
        total = normed[own_rows(part)] + ffn_scatter.result(part) + down_b
        out, unit_f, inv_f = norm_fwd(total, gain2, shift2)
        layer_out[own_rows(part)] = out
        grad = out_grad[own_rows(part)]
        second_f = norm_bwd(grad, unit_f, inv_f, gain2)
        second[own_rows(part)] = second_f
        s_all[part, 0] = second_f.astype(LOW)
        s_gather.start(part)
        gain2_sum += column_sum(grad * unit_f)
        shift2_sum += column_sum(grad)
        down_sum += column_sum(second_f)

    bias_sum = [0.0]

    def ffn_backward(part, at):
        pulled = dot_nt(s_gather.pair(part, at), down_w[...])
        pre_grad = (pulled * slope[part, at]).astype(LOW)
        pre_all[part, at] = pre_grad
        bias_sum[0] += column_sum(pre_grad.astype(jnp.float32))
        return dot_nt(pre_grad, up_w[...])

    exchange(s_gather, branch_scatter, ffn_backward)

    tokens = 4 * share
    step = 256

    def weight_rows(at, carry):
        cut = pl.ds(pl.multiple_of(at * step, step), step)
        down_grad[cut, :] = dot_tn(
            act[:, :, :, cut].reshape(tokens, step), s_all[...].reshape(tokens, width)
        ).astype(LOW)
        up_grad[cut, :] = dot_tn(
            x_all[:, :, :, cut].reshape(tokens, step), pre_all[...].reshape(tokens, up_w.shape[1])
        ).astype(LOW)
        return carry

    gain1_sum, shift1_sum, o_sum = 0.0, 0.0, 0.0
    for part in range(CHUNKS):
        grad = second[own_rows(part)] + branch_scatter.result(part)
        unit_f = unit1[own_rows(part)]
        first_f = norm_bwd(grad, unit_f, inv1[own_rows(part)], gain1)
        first_out[own_rows(part)] = first_f
        f_all[part, 0] = first_f.astype(LOW)
        f_gather.start(part)
        gain1_sum += column_sum(grad * unit_f)
        shift1_sum += column_sum(grad)
        o_sum += column_sum(first_f)
    lax.fori_loop(0, width // step, weight_rows, 0)

    weight = o_full[head]
    weight = jnp.concatenate([jnp.zeros((256 - weight.shape[0], width), LOW), weight], axis=0)
    o_total = None

    def back(part, at):
        rows_f = f_gather.pair(part, at)
        grad = dot_nt(rows_f, weight).astype(LOW)
        term = None
        first_ctx = ctx[block_rows(order[2 * at], part), :]
        second_ctx = ctx[block_rows(order[2 * at + 1], part), :]
        d_ctx[block_rows(order[2 * at], part), :] = grad[:rows]
        d_ctx[block_rows(order[2 * at + 1], part), :] = grad[rows:]
        return dot_tn(jnp.concatenate([first_ctx, second_ctx], axis=0), rows_f)

    o_total = 0.0
    for part in range(CHUNKS):
        f_gather.to_core[part].wait_recv()
        o_total += back(part, 0)
    for part in range(CHUNKS):
        f_gather.pass_on(part)
    for part in range(CHUNKS):
        f_gather.relay[part].wait_recv()
        o_total += back(part, 1)
    o_grad[...] = o_total[256 - o_grad.shape[0] :].astype(LOW)
    zero = jnp.zeros((1, width), jnp.float32)
    vec[...] = jnp.concatenate(
        [o_sum, gain1_sum, shift1_sum, down_sum, gain2_sum, shift2_sum, bias_sum[0], zero], axis=0
    )
    for copy in made:
        copy.wait_send()


def middle(ctx, o_full, hid, o_bias, gain1, shift1, up_w, up_b, down_w, down_b, gain2, shift2, out_grad):
    tokens, width = hid.shape
    share = out_grad.shape[0]
    rows = share // CHUNKS
    hidden, local = up_w.shape[1], o_full.shape[1]
    f32 = jnp.float32
    gathered = pltpu.VMEM((CHUNKS, 4, rows, width), LOW)
    copies = CHUNKS * (3 + 3 * 3 + 2 * 3)
    return pl.pallas_call(
        middle_kernel,
        name="middle",
        out_shape=(
            jax.ShapeDtypeStruct((share, width), f32),
            jax.ShapeDtypeStruct((share, width), f32),
            jax.ShapeDtypeStruct((tokens, 256), LOW),
            jax.ShapeDtypeStruct((width, hidden), LOW),
            jax.ShapeDtypeStruct((hidden, width), LOW),
            jax.ShapeDtypeStruct((local, width), LOW),
            jax.ShapeDtypeStruct((8, width), f32),
        ),
        in_specs=[VM] * 13,
        out_specs=(VM,) * 7,
        scratch_shapes=[
            pltpu.VMEM((4, share, 256), LOW),
            pltpu.VMEM((share, width), f32),
            pltpu.VMEM((share, width), f32),
            pltpu.VMEM((share, 1), f32),
            pltpu.VMEM((share, width), f32),
            gathered,
            gathered,
            gathered,
            pltpu.VMEM((CHUNKS, 2, 2 * rows, hidden), f32),
            pltpu.VMEM((CHUNKS, 2, 2 * rows, hidden), LOW),
            pltpu.VMEM((CHUNKS, 2, 2 * rows, hidden), LOW),
            pltpu.VMEM((CHUNKS, 2, rows, width), f32),
            pltpu.VMEM((2, CHUNKS, 2, rows, width), LOW),
            pltpu.VMEM((2, CHUNKS, 2, rows, width), LOW),
            pltpu.VMEM((2, CHUNKS, rows, width), LOW),
            pltpu.VMEM((2, CHUNKS, rows, width), LOW),
            pltpu.SemaphoreType.DMA((copies,)),
            pltpu.SemaphoreType.DMA((copies,)),
        ],
        compiler_params=pltpu.CompilerParams(
            collective_id=1, has_side_effects=True, vmem_limit_bytes=30 << 20
        ),
    )(
        ctx, o_full, hid, o_bias, gain1, shift1, up_w, up_b, down_w, down_b, gain2, shift2, out_grad
    )


def tail_kernel(
    rand, links, q_rows, kv, probs, wide_probs, wide_ctx, d_ctx, hid, weights, first, up_grad, down_grad, o_grad,
    vec, in_grad, big_out, small_out, vec_out,
    dq, acc, loose, wide_dq, wide_mean, pair_send, pair_in, pair_out, partial, small, big_ring, small_ring, near_out, near_in, far_out, far_in,
    vec_now, vec_send, vec_recv, send, recv, ring_send, ring_recv,
):
    n = lax.axis_size("seq")
    tokens, width = hid.shape
    half, share = tokens // 2, first.shape[0]
    depths = (big_ring.shape[3], big_ring.shape[3], small_ring.shape[2])
    spans = SLOT_LEN // tokens
    seq, head = lax.axis_index("seq"), lax.axis_index("head")
    place = seq % spans
    f32 = jnp.float32
    side, along = seq % 2, seq // 2
    spot = along + side * (n - 1 - 2 * along)

    def member(pos):
        turn = pos // (n // 2)
        return 2 * (pos + turn * (n - 1 - 2 * pos)) + turn

    ways = ({"seq": member((spot + 1) % n)}, {"seq": member((spot + n - 1) % n)})
    signs = (-1, 1)
    by_x, by_z = {"seq": flip(seq, 0)}, {"seq": flip(seq, 1)}
    core, far = flip(head, 0), flip(head, 1)
    both = flip(core, 1)
    seq_bits = n.bit_length() - 1
    vec_peers = [{"seq": flip(seq, bit)} for bit in range(seq_bits)] + [{"head": core}, {"head": far}]
    greet((by_x, by_z, *ways, *vec_peers))

    def rows_of(owner, part):
        return pl.ds(pl.multiple_of(owner * tokens + part * half, half), half)

    x_at, z_at = flip(place, 0), flip(place, 1)
    d_at = flip(x_at, 1)

    side_cols = up_grad.shape[1] // 2
    left, right, full = pl.ds(0, side_cols), pl.ds(side_cols, side_cols), pl.ds(0, width)
    pair_of = (up_grad, down_grad)
    rings = (
        (big_ring.at[0], big_out, pair_of, left),
        (big_ring.at[1], big_out, pair_of, right),
        (small_ring, small_out, (small.at[0], small.at[1]), full),
    )
    kinds = len(rings)

    def chunk(kind, pos):
        return pl.ds(pl.multiple_of(((pos + 2 * n) % n) * depths[kind], 16), depths[kind])

    def reduce_copy(kind, way, step):
        ring = rings[kind][0]
        return pltpu.make_async_remote_copy(
            src_ref=ring.at[way, step], dst_ref=ring.at[way, step + 1],
            send_sem=ring_send.at[0, kind, way, step], recv_sem=ring_recv.at[0, kind, way, step],
            device_id=ways[way], device_id_type=MESH,
        )

    def spread_copy(kind, way, step):
        rows = rings[kind][1].at[way, chunk(kind, spot + signs[way] * (step - 1)), rings[kind][3]]
        return pltpu.make_async_remote_copy(
            src_ref=rows, dst_ref=rows,
            send_sem=ring_send.at[1, kind, way, step], recv_sem=ring_recv.at[1, kind, way, step],
            device_id=ways[way], device_id_type=MESH,
        )

    def open_ring(kind):
        ring, _, source, cols = rings[kind]
        for way in range(2):
            ring[way, 0] = source[way][chunk(kind, spot), cols]
            reduce_copy(kind, way, 0).start()

    def add_ring(kind, way, step):
        ring, _, source, cols = rings[kind]
        reduce_copy(kind, way, step).wait_recv()
        mine = source[way][chunk(kind, spot + signs[way] * (step + 1)), cols]
        ring[way, step + 1] = (ring[way, step + 1].astype(f32) + mine.astype(f32)).astype(LOW)

    open_ring(0)
    open_ring(1)
    local_blocks = tokens // BLOCK
    chunk_rows = WIN * BLOCK
    turns = local_blocks // 2
    assert turns == SLOT_LEN // chunk_rows
    scale = HD ** (-0.5)
    acc[...] = jnp.zeros_like(acc)
    loose[:, 3 * local_blocks] = jnp.zeros((3, BLOCK, 128), f32)

    def add_rows(at, size, d_key, d_value):
        where_at = pl.ds(pl.multiple_of(at, BLOCK), size)
        acc[0, where_at] += d_key[:, 0:128]
        acc[1, where_at] += d_key[:, 128:256] + d_value[:, 0:128]
        acc[2, where_at] += d_value[:, 128:256]

    def acc_rows(owner, part):
        first_block = owner * local_blocks + part * (local_blocks // 2)
        blocks = []
        for more in range(local_blocks // 2):
            block = first_block + more
            here = pl.ds(pl.multiple_of(block * BLOCK, BLOCK), BLOCK)
            there = links[block]
            blocks.append(jnp.concatenate([acc[at, here] + loose[at, there] for at in range(3)], axis=1))
        return jnp.concatenate(blocks, axis=0)

    def pick_blocks(ids, low):
        return jnp.concatenate([kv[at, :, low : low + 256] for at in ids], axis=0)

    def wide_rows(at, low):
        return kv[pl.ds(at * WIN, WIN), :, low : low + 256].reshape(chunk_rows, 256)

    def one_block(step):
        near = [(place * local_blocks + step + shift + SLOT_LEN // BLOCK) % (SLOT_LEN // BLOCK) for shift in (-1, 0, 1)]
        ids = near + [rand[slot, step] for slot in range(3)] + [0, 1]
        rows = pl.ds(pl.multiple_of(step * BLOCK, BLOCK), BLOCK)
        q_all = spread_heads(q_rows[rows, :], 0)
        do_all = spread_heads(d_ctx[rows, :], 1)
        low_probs = probs[step]
        d_prob = dot_nt(do_all, pick_blocks(ids, 128))
        wide = low_probs.astype(f32)
        mean = jnp.sum(d_prob * wide, axis=1, keepdims=True)
        d_score = (wide * (d_prob - mean)).astype(LOW)
        dq[rows, :] = (fold_heads(dot_nn(d_score, pick_blocks(ids, 0)), 0) * scale).astype(LOW)
        d_key = dot_tn(d_score, q_all)
        d_value = dot_tn(low_probs, do_all)
        for slot in (0, 1, 2, 6, 7):
            cut = slice(slot * BLOCK, (slot + 1) * BLOCK)
            add_rows(ids[slot] * BLOCK, BLOCK, d_key[cut], d_value[cut])
        for slot in range(3):
            cut = slice((3 + slot) * BLOCK, (4 + slot) * BLOCK)
            to = step * 3 + slot
            old = links[SLOT_LEN // BLOCK + to]
            loose[0, to] = d_key[cut, 0:128] + loose[0, old]
            loose[1, to] = d_key[cut, 128:256] + d_value[cut, 0:128] + loose[1, old]
            loose[2, to] = d_value[cut, 128:256] + loose[2, old]

    @pl.when(place == 0)
    def _():
        wide_dq[...] = jnp.zeros_like(wide_dq)
        product = d_ctx[0 : 2 * BLOCK, :].astype(f32) * wide_ctx[...]
        lane = lax.broadcasted_iota(jnp.int32, (1, 256), 1) // HD
        wide_mean[...] = jnp.concatenate(
            [jnp.sum(jnp.where(lane == 1 + at, product, 0.0), axis=1, keepdims=True) for at in range(3)], axis=0
        )

    def reduce_step(kind, step):
        for way in range(2):
            add_ring(kind, way, step)
            reduce_copy(kind, way, step + 1).start()

    def turn(at, carry):
        @pl.when(place == 0)
        def _():
            q_all = spread_heads(q_rows[0 : 2 * BLOCK, :], 0)
            do_all = spread_heads(d_ctx[0 : 2 * BLOCK, :], 1)
            from_row = pl.multiple_of(at * chunk_rows, chunk_rows)
            low_probs = wide_probs[at]
            d_prob = dot_nt(do_all, wide_rows(at, 128))
            d_score = (low_probs.astype(f32) * (d_prob - wide_mean[...])).astype(LOW)
            add_rows(from_row, chunk_rows, dot_tn(d_score, q_all), dot_tn(low_probs, do_all))
            wide_dq[...] += dot_nn(d_score, wide_rows(at, 0))

        @pl.when(at < n - 2)
        def _():
            reduce_step(0, at)

        @pl.when(jnp.logical_or(place != 0, at != 0))
        def _():
            one_block(2 * at)
            one_block(2 * at + 1)

        @pl.when(at < n - 2)
        def _():
            reduce_step(1, at)

        return carry

    lax.fori_loop(0, turns, turn, 0)

    @pl.when(place == 0)
    def _():
        dq[0 : 2 * BLOCK, :] = (fold_heads(wide_dq[...], 0) * scale).astype(LOW)

    sends = ((d_at, 0, by_z), (d_at, 1, by_x), (x_at, 1, by_x), (z_at, 0, by_z))
    copies = []
    for at, (owner, part, where_to) in enumerate(sends):
        pair_send[at] = acc_rows(owner, part).astype(LOW)
        copies.append(remote(pair_send.at[at], pair_in.at[at], send, recv, at, where_to))
        copies[-1].start()
    copies.append(remote(pair_out.at[0], pair_in.at[4], send, recv, 4, by_x))
    copies.append(remote(pair_out.at[1], pair_in.at[5], send, recv, 5, by_z))

    def late_ring(step, carry):
        reduce_step(0, step)
        reduce_step(1, step)
        return carry

    lax.fori_loop(min(turns, n - 2), n - 2, late_ring, 0)

    def open_spread(kind):
        ring, out, _, cols = rings[kind]
        for way in range(2):
            add_ring(kind, way, n - 2)
            out[way, chunk(kind, spot - signs[way]), cols] = ring[way, n - 1]
            spread_copy(kind, way, 0).start()

    def spread_step(kind, step):
        for way in range(2):
            spread_copy(kind, way, step).wait_recv()
            spread_copy(kind, way, step + 1).start()

    open_spread(0)
    open_spread(1)
    local = weights.shape[0] // 4
    qw, kw, vw = (weights.at[pl.ds(at * local, local)] for at in range(3))
    gap = jnp.zeros((256 - local, width), LOW)
    partial[...] = dot_nn(dq[...], jnp.concatenate([qw[...], gap], axis=0))
    copies[0].wait_recv()
    pair_out[0] = (acc_rows(x_at, 0) + pair_in[0].astype(f32)).astype(LOW)
    copies[4].start()
    copies[1].wait_recv()
    pair_out[1] = (acc_rows(z_at, 1) + pair_in[1].astype(f32)).astype(LOW)
    copies[5].start()
    small[1, 0:local] = dot_tn(dq[...], hid[...])[0:local].astype(LOW)
    small[1, local : 2 * local] = o_grad[...]
    spare = small.shape[1] - 2 * local
    if spare:
        small[:, 2 * local :] = jnp.zeros((2, spare, width), LOW)
    for at in range(2, 6):
        copies[at].wait_recv()
    own = []
    for part in range(2):
        mine = acc_rows(place, part)
        first_in, second_in = (3, 4) if part == 0 else (2, 5)
        own.append((mine + pair_in[first_in].astype(f32) + pair_in[second_in].astype(f32)).astype(LOW))
    own = jnp.concatenate(own, axis=0)
    small[0, 0 : 2 * local] = dot_tn(own, hid[...]).astype(LOW)
    open_ring(2)

    def share_rows(owner):
        return partial[pl.ds(pl.multiple_of(owner * share, share), share), :]

    near = [remote(near_out.at[at], near_in.at[at], send, recv, 6 + at, {"head": core}) for at in range(2)]

    def key_term():
        partial[...] += dot_nn(own[:, 0:256], jnp.concatenate([kw[...], gap], axis=0))

    def value_term():
        partial[...] += dot_nn(own[:, 128:384], jnp.concatenate([gap, vw[...]], axis=0))

    def send_near():
        for at, owner in enumerate((both, core)):
            near_out[at] = share_rows(owner).astype(LOW)
            near[at].start()

    def send_far():
        near[0].wait_recv()
        far_out[...] = (share_rows(far) + near_in[0].astype(f32)).astype(LOW)
        far_copy.start()

    tasks = [key_term, value_term, send_near, send_far]
    fill_row = lambda rows: jnp.concatenate([rows, jnp.zeros((1, width - rows.shape[1]), f32)], axis=1)
    sums = jnp.concatenate(
        [
            fill_row(column_sum(dq[...].astype(f32))), fill_row(column_sum(own.astype(f32))),
            jnp.zeros((6, width), f32),
        ],
        axis=0,
    )
    vec_now[0:8] = vec[...]
    vec_now[8:16] = sums
    far_copy = remote(far_out, far_in, send, recv, 8, {"head": far})

    def vec_copy(at):
        return remote(vec_send.at[at], vec_recv.at[at], send, recv, 9 + at, vec_peers[at])

    steps = seq_bits + 2

    def vec_start(at):
        vec_send[at] = vec_now[...]
        vec_copy(at).start()

    def vec_finish(at):
        vec_copy(at).wait_recv()
        total = vec_now[...] + vec_recv[at]
        vec_now[...] = total
        if at == seq_bits - 1:
            vec_out[8:16] = total[8:16]
            vec_out[16:24] = total[0:8]
        if at == steps - 1:
            vec_out[0:8] = total[0:8]

    spread_done = 0
    vec_start(0)
    for at in range(min(steps, n - 2)):
        reduce_step(2, at)
        spread_step(at % 2, at // 2)
        if at < len(tasks):
            tasks[at]()
        vec_finish(at)
        if at + 1 < steps:
            vec_start(at + 1)

    def ring_body(step, carry):
        reduce_step(2, step)
        return carry

    lax.fori_loop(steps, n - 2, ring_body, 0)
    open_spread(2)
    near[1].wait_recv()
    far_copy.wait_recv()
    in_grad[...] = first[...] + share_rows(head) + near_in[1].astype(f32) + far_in[...].astype(f32)
    done_left, done_right = (steps + 1) // 2, steps // 2

    def spread_all(step, carry):
        spread_step(0, step + done_left)
        spread_step(2, step)
        spread_step(1, step + done_left)
        return carry

    def spread_last(step, carry):
        spread_step(2, step)
        return carry

    for step in range(done_right, done_left):
        spread_step(1, step)
    rest = n - 2 - done_left
    lax.fori_loop(0, rest, spread_all, 0)
    lax.fori_loop(rest, n - 2, spread_last, 0)
    for kind in range(kinds):
        for way in range(2):
            spread_copy(kind, way, n - 2).wait_recv()

    def close_body(step, carry):
        for kind in range(kinds):
            for way in range(2):
                reduce_copy(kind, way, step).wait_send()
                spread_copy(kind, way, step).wait_send()
        return carry

    lax.fori_loop(0, n - 1, close_body, 0)
    for copy in copies + near + [far_copy] + [vec_copy(at) for at in range(steps)]:
        copy.wait_send()


def tail(rand, links, q_rows, kv, probs, wide_probs, wide_ctx, d_ctx, hid, weights, first, up_grad, down_grad, o_grad, vec):
    n = lax.axis_size("seq")
    tokens, width = hid.shape
    share = first.shape[0]
    pair = kv.shape[2]
    depth, less = 16 * (-(-width // (16 * n))), 16 * (-(-pair // (16 * n)))
    rows = n * depth
    f32 = jnp.float32
    if rows > width:
        up_grad = jnp.pad(up_grad, ((0, rows - width), (0, 0)))
        down_grad = jnp.pad(down_grad, ((0, rows - width), (0, 0)))
    steps = n.bit_length() + 1
    return pl.pallas_call(
        tail_kernel,
        name="tail",
        out_shape=(
            jax.ShapeDtypeStruct((share, width), f32),
            jax.ShapeDtypeStruct((2, rows, up_grad.shape[1]), LOW),
            jax.ShapeDtypeStruct((2, n * less, width), LOW),
            jax.ShapeDtypeStruct((24, width), f32),
        ),
        in_specs=[pl.BlockSpec(memory_space=pltpu.SMEM)] * 2 + [VM] * 13,
        out_specs=(VM,) * 4,
        scratch_shapes=[
            pltpu.VMEM((tokens, 256), LOW),
            pltpu.VMEM((3, SLOT_LEN, 128), f32),
            pltpu.VMEM((3, 3 * tokens // BLOCK + 1, BLOCK, 128), f32),
            pltpu.VMEM((6 * BLOCK, 256), f32),
            pltpu.VMEM((6 * BLOCK, 1), f32),
            pltpu.VMEM((4, tokens // 2, pair), LOW),
            pltpu.VMEM((6, tokens // 2, pair), LOW),
            pltpu.VMEM((2, tokens // 2, pair), LOW),
            pltpu.VMEM((tokens, width), f32),
            pltpu.VMEM((2, n * less, width), LOW),
            pltpu.VMEM((2, 2, n, depth, up_grad.shape[1] // 2), LOW),
            pltpu.VMEM((2, n, less, width), LOW),
            pltpu.VMEM((2, share, width), LOW),
            pltpu.VMEM((2, share, width), LOW),
            pltpu.VMEM((share, width), LOW),
            pltpu.VMEM((share, width), LOW),
            pltpu.VMEM((16, width), f32),
            pltpu.VMEM((steps, 16, width), f32),
            pltpu.VMEM((steps, 16, width), f32),
            pltpu.SemaphoreType.DMA((9 + steps,)),
            pltpu.SemaphoreType.DMA((9 + steps,)),
            pltpu.SemaphoreType.DMA((2, 3, 2, n - 1)),
            pltpu.SemaphoreType.DMA((2, 3, 2, n - 1)),
        ],
        compiler_params=pltpu.CompilerParams(
            collective_id=2, has_side_effects=True, vmem_limit_bytes=(33 if n <= 16 else 60) << 20
        ),
    )(rand, links, q_rows, kv, probs, wide_probs, wide_ctx, d_ctx, hid, weights, first, up_grad, down_grad, o_grad, vec)


def per_device(
    hidden_in, q_weight, q_bias, k_weight, v_weight, v_bias, o_weight, o_bias, norm1_gain, norm1_shift,
    up_weight, up_bias, down_weight, down_bias, norm2_gain, norm2_shift, doc_mask, doc_blocks, rand_blocks,
    out_grad,
):
    f32 = jnp.float32
    tokens, width = hidden_in.shape
    local = q_weight.shape[1]
    rand = rand_blocks.T
    weights = jnp.concatenate([q_weight.T, k_weight.T, v_weight.T, o_weight], axis=0)
    query, slot_pair, o_full = project(hidden_in, weights, jnp.stack([q_bias, v_bias]))
    context, probs, wide_probs, wide_ctx, links = attend_forward(
        doc_blocks, rand, doc_mask.reshape(-1, 128), query, slot_pair
    )
    layer_out, first, d_ctx, up_part, down_part, o_part, vec = middle(
        context, o_full, hidden_in, o_bias, norm1_gain, norm1_shift, up_weight, up_bias, down_weight,
        down_bias, norm2_gain, norm2_shift, out_grad,
    )
    in_grad, big, small, vecs = tail(
        rand, links, query, slot_pair.reshape(-1, BLOCK, 2 * local), probs, wide_probs, wide_ctx, d_ctx, hidden_in, weights, first, up_part,
        down_part, o_part, vec,
    )
    small = small.astype(f32)
    return (
        layer_out, in_grad, small[1, :local].T, vecs[8, :local], small[0, :local].T,
        small[0, local : 2 * local].T, vecs[9, local : 2 * local], small[1, local : 2 * local],
        vecs[0], vecs[1], vecs[2], big[0, :width].astype(f32), vecs[22], big[1, :width].astype(f32),
        vecs[3], vecs[4], vecs[5],
    )


def solution(mesh):
    columns, vector, rows, whole = P(None, "head"), P("head"), P("head", None), P()
    tokens, shares = P("seq", None), P(("seq", "head"), None)
    in_specs = (
        tokens, columns, vector, columns, columns, vector, rows, whole, whole, whole, columns, vector, rows,
        whole, whole, whole, whole, whole, tokens, shares,
    )
    out_specs = (
        shares, shares, columns, vector, columns, columns, vector, rows, whole, whole, whole, columns, vector,
        rows, whole, whole, whole,
    )
    return jax.shard_map(per_device, mesh=mesh, in_specs=in_specs, out_specs=out_specs, check_vma=False)
```

```python
import functools

import jax
import jax.numpy as jnp
from jax import lax
from jax.experimental import pallas as pl
from jax.experimental.pallas import tpu as pltpu
from jax.sharding import PartitionSpec as P

HD = 64
BLOCK = 64
SLOT_LEN = 4096
NEG = -1e30
EPS = 1e-12
WIN = 8


def dot_nt(left, right):
    return lax.dot_general(left, right, (((1,), (1,)), ((), ())), preferred_element_type=jnp.float32)


def dot_tn(left, right):
    return lax.dot_general(left, right, (((0,), (0,)), ((), ())), preferred_element_type=jnp.float32)


def dot_nn(left, right):
    return jnp.dot(left, right, preferred_element_type=jnp.float32)


def head_pick(rows, first):
    lane = lax.broadcasted_iota(jnp.int32, (1, rows.shape[1]), 1) // HD
    return [jnp.where(lane == first + head, rows, jnp.zeros_like(rows)) for head in range(3)]


def spread_heads(rows, first):
    return jnp.concatenate(head_pick(rows, first), axis=0)


def fold_heads(stacked, first):
    size = stacked.shape[0] // 3
    lane = lax.broadcasted_iota(jnp.int32, (1, stacked.shape[1]), 1) // HD
    total = None
    for head in range(3):
        part = jnp.where(lane == first + head, stacked[head * size : (head + 1) * size], 0.0)
        total = part if total is None else total + part
    return total


def slot_spot(tokens):
    spans = SLOT_LEN // tokens
    seq = lax.axis_index("seq")
    return seq % spans, seq // spans


def window_ids(place, count, rand_ref, step, local_blocks):
    mine = place * local_blocks + step
    last = SLOT_LEN // BLOCK - 1
    ids, limits = [], []
    for shift in (-1, 0, 1):
        near = mine + shift
        good = (near >= 2) & (near <= last)
        at = jnp.clip(near, 0, last)
        ids.append(at)
        limits.append(jnp.where(good, jnp.clip(count - at * BLOCK, 0, BLOCK), 0))
    for slot in range(3):
        at = rand_ref[slot, step]
        ids.append(at)
        limits.append(jnp.clip(count - at * BLOCK, 0, BLOCK))
    for at in (0, 1):
        ids.append(jnp.int32(at))
        limits.append(jnp.clip(count - at * BLOCK, 0, BLOCK))
    return ids, limits


def take_blocks(ref, ids, low):
    parts = [ref[pl.ds(pl.multiple_of(at * BLOCK, BLOCK), BLOCK), low : low + 256] for at in ids]
    return jnp.concatenate(parts, axis=0)


def attend_fwd_kernel(blocks_ref, rand_ref, mask_ref, q_ref, kv_ref, ctx_ref, p_ref, pg_ref, wide_ctx_ref, link_ref, wide_ref):
    local_blocks = q_ref.shape[0] // BLOCK
    place, slot = slot_spot(q_ref.shape[0])
    lines = SLOT_LEN // mask_ref.shape[1]
    marked = jnp.sum(mask_ref[pl.ds(pl.multiple_of(slot * lines, lines), lines), :])
    count = jnp.minimum(marked, blocks_ref[slot] * BLOCK)
    half = lax.broadcasted_iota(jnp.int32, (1, 128), 1)
    slot_blocks = SLOT_LEN // BLOCK
    for at in range(slot_blocks + 3 * local_blocks):
        link_ref[at] = 3 * local_blocks

    def one_block(step):
        for slot in range(3):
            owner = rand_ref[slot, step]
            link_ref[slot_blocks + step * 3 + slot] = link_ref[owner]
            link_ref[owner] = step * 3 + slot
        ids, limits = window_ids(place, count, rand_ref, step, local_blocks)
        rows = pl.ds(pl.multiple_of(step * BLOCK, BLOCK), BLOCK)
        q_all = spread_heads(q_ref[rows, :], 0)
        raw = dot_nt(q_all, take_blocks(kv_ref, ids, 0))
        cut = jnp.concatenate(
            [jnp.where(half < BLOCK, limits[2 * t], limits[2 * t + 1]) for t in range(WIN // 2)], axis=1
        )
        inside = lax.broadcasted_iota(jnp.int32, (1, WIN * BLOCK), 1) % BLOCK
        raw = jnp.where(inside < cut, raw, NEG)
        expo = jnp.exp(raw - jnp.max(raw, axis=1, keepdims=True))
        probs = (expo * (1.0 / jnp.sum(expo, axis=1, keepdims=True))).astype(jnp.bfloat16)
        p_ref[step] = probs
        out = dot_nn(probs, take_blocks(kv_ref, ids, 128))
        ctx_ref[rows, :] = fold_heads(out, 1).astype(jnp.bfloat16)

    @pl.when(place == 0)
    def _():
        q_all = spread_heads(q_ref[0 : 2 * BLOCK, :], 0)
        chunk = WIN * BLOCK
        rows_all = q_all.shape[0]

        def scan_scores(part, top):
            at = pl.multiple_of(part * chunk, chunk)
            raw = dot_nt(q_all, kv_ref[pl.ds(at, chunk), 0:256])
            where_at = at + lax.broadcasted_iota(jnp.int32, (1, chunk), 1)
            raw = jnp.where(where_at < count, raw, NEG)
            wide_ref[part] = raw
            return jnp.maximum(top, jnp.max(raw, axis=1, keepdims=True))

        parts = SLOT_LEN // chunk
        top = lax.fori_loop(0, parts, scan_scores, jnp.full((rows_all, 1), NEG, jnp.float32))

        def scan_sum(part, total):
            expo = jnp.exp(wide_ref[part] - top)
            wide_ref[part] = expo
            return total + jnp.sum(expo, axis=1, keepdims=True)

        total = lax.fori_loop(0, parts, scan_sum, jnp.zeros((rows_all, 1), jnp.float32))
        inv = 1.0 / total

        def scan_out(part, out):
            probs = (wide_ref[part] * inv).astype(jnp.bfloat16)
            pg_ref[part] = probs
            at = pl.multiple_of(part * chunk, chunk)
            return out + dot_nn(probs, kv_ref[pl.ds(at, chunk), 128:384])

        out = lax.fori_loop(0, parts, scan_out, jnp.zeros((rows_all, 256), jnp.float32))
        folded = fold_heads(out, 1)
        wide_ctx_ref[...] = folded
        ctx_ref[0 : 2 * BLOCK, :] = folded.astype(jnp.bfloat16)

    @pl.when(place != 0)
    def _():
        wide_ctx_ref[...] = jnp.zeros_like(wide_ctx_ref)

    def pair(at, carry):
        one_block(2 * at)
        one_block(2 * at + 1)
        return carry

    lax.fori_loop(jnp.where(place == 0, 1, 0), local_blocks // 2, pair, 0)


def attend_forward(doc_blocks, rand, doc_mask, q_rows, kv_slot):
    tokens = q_rows.shape[0]
    blocks = tokens // BLOCK
    vmem = pl.BlockSpec(memory_space=pltpu.VMEM)
    smem = pl.BlockSpec(memory_space=pltpu.SMEM)
    return pl.pallas_call(
        attend_fwd_kernel,
        name="attend_forward",
        out_shape=(
            jax.ShapeDtypeStruct((tokens, 256), jnp.bfloat16),
            jax.ShapeDtypeStruct((blocks, 3 * BLOCK, WIN * BLOCK), jnp.bfloat16),
            jax.ShapeDtypeStruct((SLOT_LEN // (WIN * BLOCK), 6 * BLOCK, WIN * BLOCK), jnp.bfloat16),
            jax.ShapeDtypeStruct((2 * BLOCK, 256), jnp.float32),
            jax.ShapeDtypeStruct((SLOT_LEN // BLOCK + 3 * blocks,), jnp.int32),
        ),
        in_specs=[smem, smem, vmem, vmem, vmem],
        out_specs=(vmem,) * 4 + (smem,),
        scratch_shapes=[pltpu.VMEM((SLOT_LEN // (WIN * BLOCK), 6 * BLOCK, WIN * BLOCK), jnp.float32)],
        compiler_params=pltpu.CompilerParams(vmem_limit_bytes=16 << 20),
    )(doc_blocks, rand, doc_mask, q_rows, kv_slot)


MESH = pl.DeviceIdType.MESH
VM = pl.BlockSpec(memory_space=pltpu.VMEM)
LOW = jnp.bfloat16


def flip(index, bit):
    step = 1 << bit
    return index + step - 2 * step * ((index // step) % 2)


def remote(src, dst, send, recv, slot, where):
    return pltpu.make_async_remote_copy(
        src_ref=src, dst_ref=dst, send_sem=send.at[slot], recv_sem=recv.at[slot],
        device_id=where, device_id_type=MESH,
    )


def greet(partners):
    barrier = pltpu.get_barrier_semaphore()
    for where in partners:
        pl.semaphore_signal(barrier, inc=1, device_id=where, device_id_type=MESH)
    pl.semaphore_wait(barrier, len(partners))


def project_kernel(hid, weights, biases, q_out, kv_out, o_out, send, recv):
    tokens = hid.shape[0]
    half = tokens // 2
    local = weights.shape[0] // 4
    qw, kw, vw, ow = (weights.at[pl.ds(at * local, local)] for at in range(4))
    seq, head = lax.axis_index("seq"), lax.axis_index("head")
    spans = SLOT_LEN // tokens
    place = seq % spans
    by_x, by_z = {"seq": flip(seq, 0)}, {"seq": flip(seq, 1)}
    core, far = {"head": flip(head, 0)}, {"head": flip(head, 1)}
    greet((by_x, by_z, core, far))

    mine, theirs = o_out.at[head], o_out.at[flip(head, 1)]
    o_core = remote(ow, mine, send, recv, 6, core)
    o_far = remote(ow, mine, send, recv, 7, far)
    o_relay = remote(theirs, theirs, send, recv, 8, core)
    o_far.start()
    o_core.start()
    o_out[head] = ow[...]

    def rows_of(owner, part):
        at = pl.multiple_of(owner * tokens + part * half, half)
        return kv_out.at[pl.ds(at, half)]

    def fill(part):
        rows = hid[part * half : (part + 1) * half, :]
        keys = dot_nt(rows, kw[...])
        values = dot_nt(rows, vw[...]) + biases[1:2, :]
        at = pl.multiple_of(place * tokens + part * half, half)
        kv_out[pl.ds(at, half), :] = jnp.concatenate([keys.astype(LOW), values.astype(LOW)], axis=1)

    own_a, own_b = rows_of(place, 0), rows_of(place, 1)
    fwd_a, fwd_b = rows_of(flip(place, 0), 0), rows_of(flip(place, 1), 1)
    copies = [
        remote(own_a, own_a, send, recv, 0, by_x),
        remote(own_b, own_b, send, recv, 1, by_z),
        remote(own_b, own_b, send, recv, 2, by_x),
        remote(own_a, own_a, send, recv, 3, by_z),
        remote(fwd_a, fwd_a, send, recv, 4, by_z),
        remote(fwd_b, fwd_b, send, recv, 5, by_x),
    ]
    fill(0)
    copies[0].start()
    fill(1)
    for at in (1, 2, 3):
        copies[at].start()
    for part in range(2):
        rows = hid[part * half : (part + 1) * half, :]
        query = (dot_nt(rows, qw[...]) + biases[0:1, :]).astype(LOW) * jnp.asarray(HD ** (-0.5), LOW)
        query = jnp.concatenate([query, jnp.zeros((half, 256 - query.shape[1]), LOW)], axis=1)
        q_out[part * half : (part + 1) * half, :] = query
    copies[0].wait_recv()
    copies[4].start()
    copies[1].wait_recv()
    copies[5].start()
    o_far.wait_recv()
    o_relay.start()
    for at in (2, 3, 4, 5):
        copies[at].wait_recv()
    o_core.wait_recv()
    o_relay.wait_recv()
    for copy in copies + [o_core, o_far, o_relay]:
        copy.wait_send()


def project(hid, weights, biases):
    tokens, width = hid.shape
    heads, local = lax.axis_size("head"), weights.shape[0] // 4
    return pl.pallas_call(
        project_kernel,
        name="project_gather",
        out_shape=(
            jax.ShapeDtypeStruct((tokens, 256), LOW),
            jax.ShapeDtypeStruct((SLOT_LEN, 2 * local), LOW),
            jax.ShapeDtypeStruct((heads, local, width), LOW),
        ),
        in_specs=[VM] * 3,
        out_specs=(VM,) * 3,
        scratch_shapes=[pltpu.SemaphoreType.DMA((9,)), pltpu.SemaphoreType.DMA((9,))],
        compiler_params=pltpu.CompilerParams(
            collective_id=0, has_side_effects=True, vmem_limit_bytes=12 << 20
        ),
    )(hid, weights, biases)


def norm_fwd(values, gain, shift):
    centred = values - jnp.mean(values, axis=1, keepdims=True)
    inv = lax.rsqrt(jnp.mean(centred * centred, axis=1, keepdims=True) + EPS)
    unit = centred * inv
    return unit * gain + shift, unit, inv


def norm_bwd(grad, unit, inv, gain):
    scaled = grad * gain
    inner = (
        scaled
        - jnp.mean(scaled, axis=1, keepdims=True)
        - unit * jnp.mean(scaled * unit, axis=1, keepdims=True)
    )
    return inner * inv


def column_sum(values):
    return jnp.sum(values, axis=0, keepdims=True)


CHUNKS = 4
EARLY = (1, 1)


def ring_place(n):
    seq = lax.axis_index("seq")
    side, along = seq % 2, seq // 2
    spot = along + side * (n - 1 - 2 * along)

    def member(pos):
        turn = pos // (n // 2)
        return 2 * (pos + turn * (n - 1 - 2 * pos)) + turn

    return spot, ({"seq": member((spot + 1) % n)}, {"seq": member((spot + n - 1) % n)})


def ring_rows(n, spot, depth):
    return pl.ds(pl.multiple_of(((spot + 2 * n) % n) * depth, 16), depth)


def ring_depth(n, rows):
    return 16 * (-(-rows // (16 * n)))


ROOT = 0.7978845608028654
CUBE = 0.044715


def middle_kernel(
    ctx, o_full, hid, o_bias, gain1, shift1, up_w, up_b, down_w, down_b, gain2, shift2, out_grad,
    layer_out, first_out, d_ctx, up_grad, down_grad, o_grad, vec, state,
    ctx_all, normed, unit1, inv1, second, x_all, s_all, f_all, slope, act, pre_all,
    keep, to_core, from_core, to_far, from_far, ring, send, recv, ring_send, ring_recv,
):
    share = out_grad.shape[0]
    rows = share // CHUNKS
    width = hid.shape[1]
    head = lax.axis_index("head")
    o_bias, gain1, shift1, up_b, down_b, gain2, shift2 = (
        ref[...][None, :] for ref in (o_bias, gain1, shift1, up_b, down_b, gain2, shift2)
    )
    core, far, both = flip(head, 0), flip(head, 1), flip(flip(head, 0), 1)
    order = (head, core, far, both)
    n = lax.axis_size("seq")
    spot, ways = ring_place(n)
    greet(tuple({"head": at} for at in order[1:]) + ways)
    counter = [0]
    ring_from = (down_grad, up_grad)
    depth, side_cols = ring.shape[3], ring.shape[4]

    def ring_chunk(kind, way, back):
        rows_at = ring_rows(n, spot + (-back, back)[way], depth)
        return ring_from[kind][rows_at, way * side_cols : (way + 1) * side_cols]

    def ring_copy(kind, way, at):
        return pltpu.make_async_remote_copy(
            src_ref=ring.at[kind, way, at], dst_ref=ring.at[kind, way, at + 1],
            send_sem=ring_send.at[kind, way, at], recv_sem=ring_recv.at[kind, way, at],
            device_id=ways[way], device_id_type=MESH,
        )

    def ring_open(kind):
        for way in range(2):
            ring[kind, way, 0] = ring_chunk(kind, way, 0)
            ring_copy(kind, way, 0).start()

    def ring_step(kind, at):
        for way in range(2):
            ring_copy(kind, way, at).wait_recv()
            total = ring[kind, way, at + 1].astype(jnp.float32) + ring_chunk(kind, way, at + 1).astype(jnp.float32)
            if at + 1 < EARLY[kind]:
                ring[kind, way, at + 1] = total.astype(LOW)
                ring_copy(kind, way, at + 1).start()
            else:
                state[kind, way] = total.astype(LOW)

    spare = up_grad.shape[0] - width
    if spare:
        up_grad[width:] = jnp.zeros((spare, up_grad.shape[1]), LOW)
        down_grad[width:] = jnp.zeros((spare, width), LOW)

    def copy_to(src, dst, where):
        slot = counter[0]
        counter[0] += 1
        made.append(remote(src, dst, send, recv, slot, {"head": where}))
        return made[-1]

    made = []

    def own_rows(part):
        return slice(part * rows, (part + 1) * rows)

    def block_rows(owner, part):
        return pl.ds(pl.multiple_of(owner * share + part * rows, rows), rows)

    ctx_copies = []
    for part in range(CHUNKS):
        for at in (3, 2, 1):
            ctx_copies.append(
                copy_to(ctx.at[block_rows(order[at], part)], ctx_all.at[head, own_rows(part)], order[at])
            )
            ctx_copies[-1].start()
    for part in range(CHUNKS):
        ctx_all[head, own_rows(part)] = ctx[block_rows(head, part), :]

    class Gather:
        def __init__(self, buffer):
            self.buffer = buffer
            self.to_core, self.to_far, self.relay = [None] * CHUNKS, [None] * CHUNKS, [None] * CHUNKS

        def start(self, part):
            own = self.buffer.at[part, 0]
            self.to_far[part] = copy_to(own, self.buffer.at[part, 2], far)
            self.to_far[part].start()
            self.to_core[part] = copy_to(own, self.buffer.at[part, 1], core)
            self.to_core[part].start()

        def pass_on(self, part):
            self.to_far[part].wait_recv()
            self.relay[part] = copy_to(self.buffer.at[part, 2], self.buffer.at[part, 3], core)
            self.relay[part].start()

        def pair(self, part, at):
            return self.buffer[part, 2 * at : 2 * at + 2].reshape(2 * rows, width)

    class Scatter:
        def __init__(self, at):
            self.at = at
            self.near, self.through, self.away = [None] * CHUNKS, [None] * CHUNKS, [None] * CHUNKS

        def put_near(self, part, partial):
            keep[part, 0] = partial[:rows]
            to_core[self.at, part, 0] = partial[rows:].astype(LOW)
            self.near[part] = copy_to(to_core.at[self.at, part, 0], from_core.at[self.at, part, 0], core)
            self.near[part].start()

        def put_far(self, part, partial):
            to_core[self.at, part, 1] = partial[rows:].astype(LOW)
            self.through[part] = copy_to(to_core.at[self.at, part, 1], from_core.at[self.at, part, 1], core)
            self.through[part].start()
            keep[part, 1] = partial[:rows]

        def pass_on(self, part):
            self.through[part].wait_recv()
            total = keep[part, 1] + from_core[self.at, part, 1].astype(jnp.float32)
            to_far[self.at, part] = total.astype(LOW)
            self.away[part] = copy_to(to_far.at[self.at, part], from_far.at[self.at, part], far)
            self.away[part].start()

        def result(self, part):
            self.near[part].wait_recv()
            self.away[part].wait_recv()
            return (
                keep[part, 0]
                + from_core[self.at, part, 0].astype(jnp.float32)
                + from_far[self.at, part].astype(jnp.float32)
            )

    def exchange(gather, scatter, make):
        for part in range(CHUNKS):
            gather.to_core[part].wait_recv()
            scatter.put_near(part, make(part, 0))
        gather.pass_on(0)
        for part in range(CHUNKS):
            gather.relay[part].wait_recv()
            scatter.put_far(part, make(part, 1))
            if part + 1 < CHUNKS:
                gather.pass_on(part + 1)
            scatter.pass_on(part)

    x_gather, s_gather, f_gather = Gather(x_all), Gather(s_all), Gather(f_all)
    ffn_scatter, branch_scatter = Scatter(0), Scatter(1)

    for part in range(CHUNKS):
        for at in range(3):
            ctx_copies[part * 3 + at].wait_recv()
        attn = None
        for at in range(4):
            rows_at = ctx_all[at, own_rows(part)]
            weight = o_full[at]
            weight = jnp.concatenate([jnp.zeros((256 - weight.shape[0], width), LOW), weight], axis=0)
            term = dot_nn(rows_at, weight)
            attn = term if attn is None else attn + term
        token = hid[block_rows(head, part), :].astype(jnp.float32)
        normed_f, unit_f, inv_f = norm_fwd(token + attn + o_bias, gain1, shift1)
        normed[own_rows(part)] = normed_f
        unit1[own_rows(part)] = unit_f
        inv1[own_rows(part)] = inv_f
        x_all[part, 0] = normed_f.astype(LOW)
        x_gather.start(part)

    def ffn_forward(part, at):
        pre = dot_nn(x_gather.pair(part, at), up_w[...]) + up_b
        square = pre * pre
        tanh = jnp.tanh(ROOT * (pre + CUBE * square * pre))
        slope[part, at] = 0.5 * (1.0 + tanh) + (0.5 * ROOT) * pre * (1.0 - tanh * tanh) * (
            1.0 + (3.0 * CUBE) * square
        )
        acted = (0.5 * pre * (1.0 + tanh)).astype(LOW)
        act[part, at] = acted
        return dot_nn(acted, down_w[...])

    exchange(x_gather, ffn_scatter, ffn_forward)

    gain2_sum, shift2_sum, down_sum = 0.0, 0.0, 0.0
    for part in range(CHUNKS):
        total = normed[own_rows(part)] + ffn_scatter.result(part) + down_b
        out, unit_f, inv_f = norm_fwd(total, gain2, shift2)
        layer_out[own_rows(part)] = out
        grad = out_grad[own_rows(part)]
        second_f = norm_bwd(grad, unit_f, inv_f, gain2)
        second[own_rows(part)] = second_f
        s_all[part, 0] = second_f.astype(LOW)
        s_gather.start(part)
        gain2_sum += column_sum(grad * unit_f)
        shift2_sum += column_sum(grad)
        down_sum += column_sum(second_f)

    bias_sum = [0.0]

    def ffn_backward(part, at):
        pulled = dot_nt(s_gather.pair(part, at), down_w[...])
        pre_grad = (pulled * slope[part, at]).astype(LOW)
        pre_all[part, at] = pre_grad
        bias_sum[0] += column_sum(pre_grad.astype(jnp.float32))
        return dot_nt(pre_grad, up_w[...])

    exchange(s_gather, branch_scatter, ffn_backward)

    tokens = 4 * share
    step = 256

    def down_rows(at):
        cut = slice(at * step, (at + 1) * step)
        down_grad[cut, :] = dot_tn(
            act[:, :, :, cut].reshape(tokens, step), s_all[...].reshape(tokens, width)
        ).astype(LOW)

    def up_rows(at):
        cut = slice(at * step, (at + 1) * step)
        up_grad[cut, :] = dot_tn(
            x_all[:, :, :, cut].reshape(tokens, step), pre_all[...].reshape(tokens, up_w.shape[1])
        ).astype(LOW)

    blocks = width // step
    work = [functools.partial(down_rows, at) for at in range(blocks)] + [functools.partial(ring_open, 0)]
    later = [functools.partial(up_rows, at) for at in range(blocks)] + [functools.partial(ring_open, 1)]
    later.insert(2, functools.partial(ring_step, 0, 0))
    moves = []
    for at in range(max(EARLY)):
        moves += [functools.partial(ring_step, 0, at)] if 0 < at < EARLY[0] else []
        moves += [functools.partial(ring_step, 1, at)] if at < EARLY[1] else []

    gain1_sum, shift1_sum, o_sum = 0.0, 0.0, 0.0
    for part in range(CHUNKS):
        grad = second[own_rows(part)] + branch_scatter.result(part)
        unit_f = unit1[own_rows(part)]
        first_f = norm_bwd(grad, unit_f, inv1[own_rows(part)], gain1)
        first_out[own_rows(part)] = first_f
        f_all[part, 0] = first_f.astype(LOW)
        f_gather.start(part)
        gain1_sum += column_sum(grad * unit_f)
        shift1_sum += column_sum(grad)
        o_sum += column_sum(first_f)
        if work:
            work.pop(0)()
    for task in work + later:
        task()

    weight = o_full[head]
    weight = jnp.concatenate([jnp.zeros((256 - weight.shape[0], width), LOW), weight], axis=0)
    o_total = None

    def back(part, at):
        rows_f = f_gather.pair(part, at)
        grad = dot_nt(rows_f, weight).astype(LOW)
        term = None
        first_ctx = ctx[block_rows(order[2 * at], part), :]
        second_ctx = ctx[block_rows(order[2 * at + 1], part), :]
        d_ctx[block_rows(order[2 * at], part), :] = grad[:rows]
        d_ctx[block_rows(order[2 * at + 1], part), :] = grad[rows:]
        return dot_tn(jnp.concatenate([first_ctx, second_ctx], axis=0), rows_f)

    o_total = 0.0
    for part in range(CHUNKS):
        f_gather.to_core[part].wait_recv()
        o_total += back(part, 0)
    f_gather.pass_on(0)
    for part in range(CHUNKS):
        if part + 1 < CHUNKS:
            f_gather.pass_on(part + 1)
        if moves:
            moves.pop(0)()
        f_gather.relay[part].wait_recv()
        o_total += back(part, 1)
    for task in moves:
        task()
    o_grad[...] = o_total[256 - o_grad.shape[0] :].astype(LOW)
    zero = jnp.zeros((1, width), jnp.float32)
    vec[...] = jnp.concatenate(
        [o_sum, gain1_sum, shift1_sum, down_sum, gain2_sum, shift2_sum, bias_sum[0], zero], axis=0
    )
    for copy in made:
        copy.wait_send()
    for kind in range(2):
        for way in range(2):
            for at in range(EARLY[kind]):
                ring_copy(kind, way, at).wait_send()


def middle(ctx, o_full, hid, o_bias, gain1, shift1, up_w, up_b, down_w, down_b, gain2, shift2, out_grad):
    tokens, width = hid.shape
    share = out_grad.shape[0]
    rows = share // CHUNKS
    hidden, local = up_w.shape[1], o_full.shape[1]
    n = lax.axis_size("seq")
    depth = ring_depth(n, width)
    assert hidden == width
    f32 = jnp.float32
    gathered = pltpu.VMEM((CHUNKS, 4, rows, width), LOW)
    copies = CHUNKS * (3 + 3 * 3 + 2 * 3)
    return pl.pallas_call(
        middle_kernel,
        name="middle",
        out_shape=(
            jax.ShapeDtypeStruct((share, width), f32),
            jax.ShapeDtypeStruct((share, width), f32),
            jax.ShapeDtypeStruct((tokens, 256), LOW),
            jax.ShapeDtypeStruct((n * depth, hidden), LOW),
            jax.ShapeDtypeStruct((n * depth, width), LOW),
            jax.ShapeDtypeStruct((local, width), LOW),
            jax.ShapeDtypeStruct((8, width), f32),
            jax.ShapeDtypeStruct((2, 2, depth, width // 2), LOW),
        ),
        in_specs=[VM] * 13,
        out_specs=(VM,) * 8,
        scratch_shapes=[
            pltpu.VMEM((4, share, 256), LOW),
            pltpu.VMEM((share, width), f32),
            pltpu.VMEM((share, width), f32),
            pltpu.VMEM((share, 1), f32),
            pltpu.VMEM((share, width), f32),
            gathered,
            gathered,
            gathered,
            pltpu.VMEM((CHUNKS, 2, 2 * rows, hidden), f32),
            pltpu.VMEM((CHUNKS, 2, 2 * rows, hidden), LOW),
            pltpu.VMEM((CHUNKS, 2, 2 * rows, hidden), LOW),
            pltpu.VMEM((CHUNKS, 2, rows, width), f32),
            pltpu.VMEM((2, CHUNKS, 2, rows, width), LOW),
            pltpu.VMEM((2, CHUNKS, 2, rows, width), LOW),
            pltpu.VMEM((2, CHUNKS, rows, width), LOW),
            pltpu.VMEM((2, CHUNKS, rows, width), LOW),
            pltpu.VMEM((2, 2, max(EARLY) + 1, depth, width // 2), LOW),
            pltpu.SemaphoreType.DMA((copies,)),
            pltpu.SemaphoreType.DMA((copies,)),
            pltpu.SemaphoreType.DMA((2, 2, max(EARLY))),
            pltpu.SemaphoreType.DMA((2, 2, max(EARLY))),
        ],
        compiler_params=pltpu.CompilerParams(
            collective_id=1, has_side_effects=True, vmem_limit_bytes=30 << 20
        ),
    )(
        ctx, o_full, hid, o_bias, gain1, shift1, up_w, up_b, down_w, down_b, gain2, shift2, out_grad
    )


FILL = ((), (1, 0), (0, 1))


def tail_kernel(
    rand, links, q_rows, kv, probs, wide_probs, wide_ctx, d_ctx, hid, weights, first, up_grad, down_grad, o_grad,
    vec, state, in_grad, big_out, small_out, vec_out,
    dq, acc, loose, wide_dq, wide_mean, pair_send, pair_in, pair_out, partial, small, big_ring, small_ring, near_out, near_in, far_out, far_in,
    vec_now, vec_send, vec_recv, send, recv, ring_send, ring_recv, fold_send, fold_recv,
):
    n = lax.axis_size("seq")
    tokens, width = hid.shape
    half, share = tokens // 2, first.shape[0]
    depths = (big_ring.shape[3],) * 2 + (small_ring.shape[3],) * 2
    spans = SLOT_LEN // tokens
    seq, head = lax.axis_index("seq"), lax.axis_index("head")
    place = seq % spans
    f32 = jnp.float32
    spot, ways = ring_place(n)
    signs = (-1, 1)
    by_x, by_z = {"seq": flip(seq, 0)}, {"seq": flip(seq, 1)}
    core, far = flip(head, 0), flip(head, 1)
    both = flip(core, 1)
    seq_bits = n.bit_length() - 1
    vec_peers = [{"seq": flip(seq, bit)} for bit in range(seq_bits)] + [{"head": core}, {"head": far}]
    greet((by_x, by_z, *ways, *vec_peers))

    def rows_of(owner, part):
        return pl.ds(pl.multiple_of(owner * tokens + part * half, half), half)

    x_at, z_at = flip(place, 0), flip(place, 1)
    d_at = flip(x_at, 1)

    side_cols = width // 2
    sides = (pl.ds(0, side_cols), pl.ds(side_cols, side_cols))
    rings = (
        (big_ring.at[0], (big_out.at[0],) * 2, (down_grad,) * 2, sides),
        (big_ring.at[1], (big_out.at[1],) * 2, (up_grad,) * 2, sides),
    )
    kinds = len(rings)

    def chunk(kind, pos):
        return ring_rows(n, pos, depths[kind])

    reaches = ((n // 2, n // 2 - 1), (n // 2 - 1, n // 2))

    def guard(holds, body):
        if isinstance(holds, bool):
            if holds:
                body()
        else:
            pl.when(holds)(body)

    def fold_copy(kind, way, step):
        return pltpu.make_async_remote_copy(
            src_ref=small_ring.at[kind, way, step], dst_ref=small_ring.at[kind, way, step + 1],
            send_sem=fold_send.at[0, kind, way, step], recv_sem=fold_recv.at[0, kind, way, step],
            device_id=ways[way], device_id_type=MESH,
        )

    def fan_copy(kind, way, step):
        rows = small_out.at[kind, chunk(2, spot + signs[way] * step)]
        return pltpu.make_async_remote_copy(
            src_ref=rows, dst_ref=rows,
            send_sem=fold_send.at[1, kind, way, step], recv_sem=fold_recv.at[1, kind, way, step],
            device_id=ways[way], device_id_type=MESH,
        )

    def fold_mine(kind, way, step):
        return small[kind, chunk(2, spot - signs[way] * (reaches[kind][way] - step)), :]

    def fold_open(kind):
        for way in range(2):
            small_ring[kind, way, 0] = fold_mine(kind, way, 0)
            fold_copy(kind, way, 0).start()

    def fold_step(kind, step):
        for way in range(2):

            def body(way=way):
                fold_copy(kind, way, step).wait_recv()
                total = small_ring[kind, way, step + 1].astype(f32) + fold_mine(kind, way, step + 1).astype(f32)
                small_ring[kind, way, step + 1] = total.astype(LOW)
                fold_copy(kind, way, step + 1).start()

            guard(step < reaches[kind][way] - 1, body)

    def fold_close(kind):
        total = small[kind, chunk(2, spot), :].astype(f32)
        for way in range(2):
            reach = reaches[kind][way]
            fold_copy(kind, way, reach - 1).wait_recv()
            total += small_ring[kind, way, reach].astype(f32)
        small_out[kind, chunk(2, spot)] = total.astype(LOW)
        for way in range(2):
            fan_copy(kind, way, 0).start()

    def fan_step(kind, step):
        for way in range(2):

            def body(way=way):
                fan_copy(kind, way, step).wait_recv()
                fan_copy(kind, way, step + 1).start()

            guard(step < reaches[kind][way] - 1, body)

    def fan_close(kind):
        for way in range(2):
            fan_copy(kind, way, reaches[kind][way] - 1).wait_recv()

    def reduce_copy(kind, way, step):
        ring = rings[kind][0]
        return pltpu.make_async_remote_copy(
            src_ref=ring.at[way, step], dst_ref=ring.at[way, step + 1],
            send_sem=ring_send.at[0, kind, way, step], recv_sem=ring_recv.at[0, kind, way, step],
            device_id=ways[way], device_id_type=MESH,
        )

    def spread_copy(kind, way, step):
        rows = rings[kind][1][way].at[chunk(kind, spot + signs[way] * (step - 1)), rings[kind][3][way]]
        return pltpu.make_async_remote_copy(
            src_ref=rows, dst_ref=rows,
            send_sem=ring_send.at[1, kind, way, step], recv_sem=ring_recv.at[1, kind, way, step],
            device_id=ways[way], device_id_type=MESH,
        )

    def open_ring(kind):
        ring, _, source, cols = rings[kind]
        for way in range(2):
            ring[way, 0] = source[way][chunk(kind, spot), cols[way]]
            reduce_copy(kind, way, 0).start()

    def add_ring(kind, way, step):
        ring, _, source, cols = rings[kind]
        reduce_copy(kind, way, step).wait_recv()
        mine = source[way][chunk(kind, spot + signs[way] * (step + 1)), cols[way]]
        ring[way, step + 1] = (ring[way, step + 1].astype(f32) + mine.astype(f32)).astype(LOW)

    for kind in range(2):
        for way in range(2):
            rings[kind][0][way, EARLY[kind]] = state[kind, way]
            reduce_copy(kind, way, EARLY[kind]).start()
    local_blocks = tokens // BLOCK
    chunk_rows = WIN * BLOCK
    turns = local_blocks // 2
    assert turns == SLOT_LEN // chunk_rows
    scale = HD ** (-0.5)
    acc[...] = jnp.zeros_like(acc)
    loose[:, 3 * local_blocks] = jnp.zeros((3, BLOCK, 128), f32)

    def add_rows(at, size, d_key, d_value):
        where_at = pl.ds(pl.multiple_of(at, BLOCK), size)
        acc[0, where_at] += d_key[:, 0:128]
        acc[1, where_at] += d_key[:, 128:256] + d_value[:, 0:128]
        acc[2, where_at] += d_value[:, 128:256]

    def acc_rows(owner, part):
        first_block = owner * local_blocks + part * (local_blocks // 2)
        blocks = []
        for more in range(local_blocks // 2):
            block = first_block + more
            here = pl.ds(pl.multiple_of(block * BLOCK, BLOCK), BLOCK)
            there = links[block]
            blocks.append(jnp.concatenate([acc[at, here] + loose[at, there] for at in range(3)], axis=1))
        return jnp.concatenate(blocks, axis=0)

    def pick_blocks(ids, low):
        return jnp.concatenate([kv[at, :, low : low + 256] for at in ids], axis=0)

    def wide_rows(at, low):
        return kv[pl.ds(at * WIN, WIN), :, low : low + 256].reshape(chunk_rows, 256)

    def one_block(step):
        near = [(place * local_blocks + step + shift + SLOT_LEN // BLOCK) % (SLOT_LEN // BLOCK) for shift in (-1, 0, 1)]
        ids = near + [rand[slot, step] for slot in range(3)] + [0, 1]
        rows = pl.ds(pl.multiple_of(step * BLOCK, BLOCK), BLOCK)
        q_all = spread_heads(q_rows[rows, :], 0)
        do_all = spread_heads(d_ctx[rows, :], 1)
        low_probs = probs[step]
        d_prob = dot_nt(do_all, pick_blocks(ids, 128))
        wide = low_probs.astype(f32)
        mean = jnp.sum(d_prob * wide, axis=1, keepdims=True)
        d_score = (wide * (d_prob - mean)).astype(LOW)
        dq[rows, :] = (fold_heads(dot_nn(d_score, pick_blocks(ids, 0)), 0) * scale).astype(LOW)
        d_key = dot_tn(d_score, q_all)
        d_value = dot_tn(low_probs, do_all)
        for slot in (0, 1, 2, 6, 7):
            cut = slice(slot * BLOCK, (slot + 1) * BLOCK)
            add_rows(ids[slot] * BLOCK, BLOCK, d_key[cut], d_value[cut])
        for slot in range(3):
            cut = slice((3 + slot) * BLOCK, (4 + slot) * BLOCK)
            to = step * 3 + slot
            old = links[SLOT_LEN // BLOCK + to]
            loose[0, to] = d_key[cut, 0:128] + loose[0, old]
            loose[1, to] = d_key[cut, 128:256] + d_value[cut, 0:128] + loose[1, old]
            loose[2, to] = d_value[cut, 128:256] + loose[2, old]

    @pl.when(place == 0)
    def _():
        wide_dq[...] = jnp.zeros_like(wide_dq)
        product = d_ctx[0 : 2 * BLOCK, :].astype(f32) * wide_ctx[...]
        lane = lax.broadcasted_iota(jnp.int32, (1, 256), 1) // HD
        wide_mean[...] = jnp.concatenate(
            [jnp.sum(jnp.where(lane == 1 + at, product, 0.0), axis=1, keepdims=True) for at in range(3)], axis=0
        )

    def reduce_step(kind, step):
        for way in range(2):
            add_ring(kind, way, step)
            reduce_copy(kind, way, step + 1).start()

    def open_spread(kind):
        ring, out, _, cols = rings[kind]
        for way in range(2):
            add_ring(kind, way, n - 2)
            out[way][chunk(kind, spot - signs[way]), cols[way]] = ring[way, n - 1]
            spread_copy(kind, way, 0).start()

    def spread_step(kind, step):
        for way in range(2):
            spread_copy(kind, way, step).wait_recv()
            spread_copy(kind, way, step + 1).start()

    def advance(kind, at):
        step = at + EARLY[kind]

        @pl.when(step < n - 2)
        def _():
            reduce_step(kind, step)

        if turns + EARLY[kind] > n - 2:

            @pl.when(step == n - 2)
            def _():
                open_spread(kind)

    def turn(at, carry):
        @pl.when(place == 0)
        def _():
            q_all = spread_heads(q_rows[0 : 2 * BLOCK, :], 0)
            do_all = spread_heads(d_ctx[0 : 2 * BLOCK, :], 1)
            from_row = pl.multiple_of(at * chunk_rows, chunk_rows)
            low_probs = wide_probs[at]
            d_prob = dot_nt(do_all, wide_rows(at, 128))
            d_score = (low_probs.astype(f32) * (d_prob - wide_mean[...])).astype(LOW)
            add_rows(from_row, chunk_rows, dot_tn(d_score, q_all), dot_tn(low_probs, do_all))
            wide_dq[...] += dot_nn(d_score, wide_rows(at, 0))

        advance(0, at)

        @pl.when(jnp.logical_or(place != 0, at != 0))
        def _():
            one_block(2 * at)
            one_block(2 * at + 1)

        advance(1, at)
        return carry

    lax.fori_loop(0, turns, turn, 0)

    @pl.when(place == 0)
    def _():
        dq[0 : 2 * BLOCK, :] = (fold_heads(wide_dq[...], 0) * scale).astype(LOW)

    sends = ((d_at, 0, by_z), (d_at, 1, by_x), (x_at, 1, by_x), (z_at, 0, by_z))
    copies = []
    for at, (owner, part, where_to) in enumerate(sends):
        pair_send[at] = acc_rows(owner, part).astype(LOW)
        copies.append(remote(pair_send.at[at], pair_in.at[at], send, recv, at, where_to))
        copies[-1].start()
    copies.append(remote(pair_out.at[0], pair_in.at[4], send, recv, 4, by_x))
    copies.append(remote(pair_out.at[1], pair_in.at[5], send, recv, 5, by_z))

    state_of = [
        [min(turns + EARLY[kind], n - 1), 0] for kind in range(2)
    ]

    def one_move(kind):
        reduced, spread = state_of[kind]
        if reduced < n - 2:
            reduce_step(kind, reduced)
            state_of[kind][0] += 1
        elif reduced == n - 2:
            open_spread(kind)
            state_of[kind][0] += 1
        elif spread < n - 2:
            spread_step(kind, spread)
            state_of[kind][1] += 1
        else:
            return False
        return True

    def fill(order):
        for kind in order:
            one_move(kind)

    def finish(kind):
        reduced, spread = state_of[kind]

        def more_reduce(step, carry):
            reduce_step(kind, step)
            return carry

        def more_spread(step, carry):
            spread_step(kind, step)
            return carry

        if reduced < n - 2:
            lax.fori_loop(reduced, n - 2, more_reduce, 0)
        if reduced <= n - 2:
            open_spread(kind)
        if spread < n - 2:
            lax.fori_loop(spread, n - 2, more_spread, 0)

    local = weights.shape[0] // 4
    qw, kw, vw = (weights.at[pl.ds(at * local, local)] for at in range(3))
    small[1, 0:local] = dot_tn(dq[...], hid[...])[0:local].astype(LOW)
    small[1, local : 2 * local] = o_grad[...]
    spare = small.shape[1] - 2 * local
    if spare:
        small[:, 2 * local :] = jnp.zeros((2, spare, width), LOW)
    fold_open(1)
    gap = jnp.zeros((256 - local, width), LOW)
    partial[...] = dot_nn(dq[...], jnp.concatenate([qw[...], gap], axis=0))
    copies[0].wait_recv()
    pair_out[0] = (acc_rows(x_at, 0) + pair_in[0].astype(f32)).astype(LOW)
    copies[4].start()
    copies[1].wait_recv()
    pair_out[1] = (acc_rows(z_at, 1) + pair_in[1].astype(f32)).astype(LOW)
    copies[5].start()
    fill(FILL[0])
    for at in range(2, 6):
        copies[at].wait_recv()
    own = []
    for part in range(2):
        mine = acc_rows(place, part)
        first_in, second_in = (3, 4) if part == 0 else (2, 5)
        own.append((mine + pair_in[first_in].astype(f32) + pair_in[second_in].astype(f32)).astype(LOW))
    own = jnp.concatenate(own, axis=0)
    small[0, 0 : 2 * local] = dot_tn(own, hid[...]).astype(LOW)
    fold_open(0)
    fill(FILL[1])

    def share_rows(owner):
        return partial[pl.ds(pl.multiple_of(owner * share, share), share), :]

    near = [remote(near_out.at[at], near_in.at[at], send, recv, 6 + at, {"head": core}) for at in range(2)]

    def key_term():
        partial[...] += dot_nn(own[:, 0:256], jnp.concatenate([kw[...], gap], axis=0))

    def value_term():
        partial[...] += dot_nn(own[:, 128:384], jnp.concatenate([gap, vw[...]], axis=0))

    def send_near():
        for at, owner in enumerate((both, core)):
            near_out[at] = share_rows(owner).astype(LOW)
            near[at].start()

    def send_far():
        near[0].wait_recv()
        far_out[...] = (share_rows(far) + near_in[0].astype(f32)).astype(LOW)
        far_copy.start()

    def finish_rows():
        near[1].wait_recv()
        far_copy.wait_recv()
        in_grad[...] = first[...] + share_rows(head) + near_in[1].astype(f32) + far_in[...].astype(f32)

    tasks = [key_term, value_term, send_near, send_far, None, finish_rows]
    fill_row = lambda rows: jnp.concatenate([rows, jnp.zeros((1, width - rows.shape[1]), f32)], axis=1)
    sums = jnp.concatenate(
        [
            fill_row(column_sum(dq[...].astype(f32))), fill_row(column_sum(own.astype(f32))),
            jnp.zeros((6, width), f32),
        ],
        axis=0,
    )
    vec_now[0:8] = vec[...]
    vec_now[8:16] = sums
    far_copy = remote(far_out, far_in, send, recv, 8, {"head": far})

    def vec_copy(at):
        return remote(vec_send.at[at], vec_recv.at[at], send, recv, 9 + at, vec_peers[at])

    steps = seq_bits + 2

    def vec_start(at):
        vec_send[at] = vec_now[...]
        vec_copy(at).start()

    def vec_finish(at):
        vec_copy(at).wait_recv()
        total = vec_now[...] + vec_recv[at]
        vec_now[...] = total
        if at == seq_bits - 1:
            vec_out[8:16] = total[8:16]
            vec_out[16:24] = total[0:8]
        if at == steps - 1:
            vec_out[0:8] = total[0:8]

    unrolled = min(n // 2 - 1, 4)

    def twice(move):
        def body(step, carry=0):
            move(0, step)
            move(1, step)
            return carry

        return body

    def close_fold():
        if unrolled < n // 2 - 1:
            lax.fori_loop(unrolled, n // 2 - 1, twice(fold_step), 0)
        fold_close(0)
        fold_close(1)

    def close_fan():
        if unrolled < n // 2 - 1:
            lax.fori_loop(unrolled, n // 2 - 1, twice(fan_step), 0)
        fan_close(0)
        fan_close(1)

    slots = [functools.partial(twice(fold_step), at) for at in range(unrolled)] + [close_fold]
    slots += [functools.partial(twice(fan_step), at) for at in range(unrolled)] + [close_fan]
    vec_start(0)
    for at, slot in enumerate(slots):
        slot()
        fill(FILL[2])
        if at < len(tasks) and tasks[at]:
            tasks[at]()
        if at < steps:
            vec_finish(at)
            if at + 1 < steps:
                vec_start(at + 1)
    for kind in range(2):
        finish(kind)
    for kind in range(kinds):
        for way in range(2):
            spread_copy(kind, way, n - 2).wait_recv()

    def close_body(step, carry):
        for kind in range(kinds):
            for way in range(2):
                guard(step >= EARLY[kind], lambda kind=kind, way=way: reduce_copy(kind, way, step).wait_send())
                spread_copy(kind, way, step).wait_send()
        return carry

    def close_small(step, carry):
        for kind in range(2):
            for way in range(2):

                def body(kind=kind, way=way):
                    fold_copy(kind, way, step).wait_send()
                    fan_copy(kind, way, step).wait_send()

                guard(step < reaches[kind][way], body)
        return carry

    lax.fori_loop(0, n // 2, close_small, 0)
    lax.fori_loop(0, n - 1, close_body, 0)
    for copy in copies + near + [far_copy] + [vec_copy(at) for at in range(steps)]:
        copy.wait_send()


def tail(rand, links, q_rows, kv, probs, wide_probs, wide_ctx, d_ctx, hid, weights, first, up_grad, down_grad, o_grad, vec, state):
    n = lax.axis_size("seq")
    tokens, width = hid.shape
    share = first.shape[0]
    pair = kv.shape[2]
    depth, less = ring_depth(n, width), ring_depth(n, pair)
    rows = n * depth
    f32 = jnp.float32
    steps = n.bit_length() + 1
    return pl.pallas_call(
        tail_kernel,
        name="tail",
        out_shape=(
            jax.ShapeDtypeStruct((share, width), f32),
            jax.ShapeDtypeStruct((2, rows, up_grad.shape[1]), LOW),
            jax.ShapeDtypeStruct((2, n * less, width), LOW),
            jax.ShapeDtypeStruct((24, width), f32),
        ),
        in_specs=[pl.BlockSpec(memory_space=pltpu.SMEM)] * 2 + [VM] * 14,
        out_specs=(VM,) * 4,
        scratch_shapes=[
            pltpu.VMEM((tokens, 256), LOW),
            pltpu.VMEM((3, SLOT_LEN, 128), f32),
            pltpu.VMEM((3, 3 * tokens // BLOCK + 1, BLOCK, 128), f32),
            pltpu.VMEM((6 * BLOCK, 256), f32),
            pltpu.VMEM((6 * BLOCK, 1), f32),
            pltpu.VMEM((4, tokens // 2, pair), LOW),
            pltpu.VMEM((6, tokens // 2, pair), LOW),
            pltpu.VMEM((2, tokens // 2, pair), LOW),
            pltpu.VMEM((tokens, width), f32),
            pltpu.VMEM((2, n * less, width), LOW),
            pltpu.VMEM((2, 2, n, depth, up_grad.shape[1] // 2), LOW),
            pltpu.VMEM((2, 2, n // 2 + 1, less, width), LOW),
            pltpu.VMEM((2, share, width), LOW),
            pltpu.VMEM((2, share, width), LOW),
            pltpu.VMEM((share, width), LOW),
            pltpu.VMEM((share, width), LOW),
            pltpu.VMEM((16, width), f32),
            pltpu.VMEM((steps, 16, width), f32),
            pltpu.VMEM((steps, 16, width), f32),
            pltpu.SemaphoreType.DMA((9 + steps,)),
            pltpu.SemaphoreType.DMA((9 + steps,)),
            pltpu.SemaphoreType.DMA((2, 2, 2, n - 1)),
            pltpu.SemaphoreType.DMA((2, 2, 2, n - 1)),
            pltpu.SemaphoreType.DMA((2, 2, 2, n // 2)),
            pltpu.SemaphoreType.DMA((2, 2, 2, n // 2)),
        ],
        compiler_params=pltpu.CompilerParams(
            collective_id=2, has_side_effects=True, vmem_limit_bytes=(33 if n <= 16 else 61) << 20
        ),
    )(rand, links, q_rows, kv, probs, wide_probs, wide_ctx, d_ctx, hid, weights, first, up_grad, down_grad, o_grad, vec, state)


def per_device(
    hidden_in, q_weight, q_bias, k_weight, v_weight, v_bias, o_weight, o_bias, norm1_gain, norm1_shift,
    up_weight, up_bias, down_weight, down_bias, norm2_gain, norm2_shift, doc_mask, doc_blocks, rand_blocks,
    out_grad,
):
    f32 = jnp.float32
    tokens, width = hidden_in.shape
    local = q_weight.shape[1]
    rand = rand_blocks.T
    weights = jnp.concatenate([q_weight.T, k_weight.T, v_weight.T, o_weight], axis=0)
    query, slot_pair, o_full = project(hidden_in, weights, jnp.stack([q_bias, v_bias]))
    context, probs, wide_probs, wide_ctx, links = attend_forward(
        doc_blocks, rand, doc_mask.reshape(-1, 128), query, slot_pair
    )
    layer_out, first, d_ctx, up_part, down_part, o_part, vec, state = middle(
        context, o_full, hidden_in, o_bias, norm1_gain, norm1_shift, up_weight, up_bias, down_weight,
        down_bias, norm2_gain, norm2_shift, out_grad,
    )
    in_grad, big, small, vecs = tail(
        rand, links, query, slot_pair.reshape(-1, BLOCK, 2 * local), probs, wide_probs, wide_ctx, d_ctx, hidden_in, weights, first, up_part,
        down_part, o_part, vec, state,
    )
    small = small.astype(f32)
    return (
        layer_out, in_grad, small[1, :local].T, vecs[8, :local], small[0, :local].T,
        small[0, local : 2 * local].T, vecs[9, local : 2 * local], small[1, local : 2 * local],
        vecs[0], vecs[1], vecs[2], big[1, :width].astype(f32), vecs[22], big[0, :width].astype(f32),
        vecs[3], vecs[4], vecs[5],
    )


def solution(mesh):
    columns, vector, rows, whole = P(None, "head"), P("head"), P("head", None), P()
    tokens, shares = P("seq", None), P(("seq", "head"), None)
    in_specs = (
        tokens, columns, vector, columns, columns, vector, rows, whole, whole, whole, columns, vector, rows,
        whole, whole, whole, whole, whole, tokens, shares,
    )
    out_specs = (
        shares, shares, columns, vector, columns, columns, vector, rows, whole, whole, whole, columns, vector,
        rows, whole, whole, whole,
    )
    return jax.shard_map(per_device, mesh=mesh, in_specs=in_specs, out_specs=out_specs, check_vma=False)
```
